32 devices in a mesh: gx: 8 (over y, x, core), gy: 4 (over z).
Axes of the slice: x: 2, y: 2, z: 4, core: 2. Of those that a mesh axis runs over, the one named last changes fastest.
Arguments:
- distribution: float32 [8, 32, 32768], P('gx', 'gy'), may hold values from 0.2 to 2
- relax_rate: float32 [8, 32], P('gx', 'gy'), may hold values from 0.05 to 0.8
- block_level: int32 [8], replicated, may hold values from 0 to 1, as said below
- block_link: int32 [2, 64], replicated, may hold values from 0 to 7, as said below
- remap_values: bfloat16 [2, 64, 512, 512], P(None, 'gy'), may hold values from -0.25 to 0.25
Outputs:
- updated: float32 [8, 32, 32768], P('gx', 'gy')
The draws below stay inside these ranges and needn't reach their ends.
Inputs may be any that keep to these rules, and one draw needn't show every extreme that they name: `block_level`: every maximal run of streamwise blocks with one level holds at least two blocks; the first run holds exactly two, so the level changes between blocks 1 and 2. `block_link`: in each direction every coarse block is named by exactly 8 fine blocks.
All inputs are finite; a program needn't handle non-finite values.
Results may differ from the reference program's by a relative error of at most 0.00095.
Values may be sent and summed in bfloat16 or wider, within the bound.
No kernel may reach another device: no remote copies, remote signals or barrier semaphores. Data moves between devices by JAX's collectives and lax.ppermute only.
A program may use at most 64 MiB of HBM per device.

```python
import math
import jax
import jax.numpy as jnp
from jax import lax

SC = 16
SF = 32
BLK = 512
CX = 1
NVF = 32768
VBC = 8
VBF = 64
NXC = 8
NYC = 32
BLOCKS_X = 8
N_GX = 8


def draw_block_level(key, part):
    length_key, start_key = jax.random.split(key)
    run_lengths = 2 + jax.random.randint(length_key, (BLOCKS_X,), 0, 2).astype(jnp.int32)
    run_lengths = run_lengths.at[0].set(2)
    run_starts = jnp.cumsum(run_lengths).astype(jnp.int32) - run_lengths
    position = jnp.arange(BLOCKS_X, dtype=jnp.int32)
    run_number = jnp.sum((run_starts[None, :] <= position[:, None]).astype(jnp.int32), 1) - 1
    first_level = jax.random.randint(start_key, (), 0, 2).astype(jnp.int32)
    levels = (first_level + run_number) % 2
    levels = levels.at[BLOCKS_X - 1].set(levels[BLOCKS_X - 2])
    return levels.astype(jnp.int32)


def draw_block_link(key, part):
    first_key, second_key = jax.random.split(key)
    first_row = jax.random.permutation(first_key, VBF) % VBC
    second_row = jax.random.permutation(second_key, VBF) % VBC
    return jnp.stack([first_row, second_row]).astype(jnp.int32)


def steps_of(rng, shape, cuts, smallest, high):
    factor_of = 1.0
    for dim, shards_of in cuts:
        draws = jax.random.uniform(jax.random.fold_in(jax.random.fold_in(rng, 6), dim), (shards_of,), jnp.float32, smallest / len(cuts), high / len(cuts))
        factor_of = factor_of * jnp.repeat(jnp.exp(draws), shape[dim] // shards_of).reshape((-1,) + (1,) * (len(shape) - 1 - dim))
    return factor_of


def centred(stream_key, dims, spread, limit, cuts=(), held_as=jnp.bfloat16):
    drawn = spread * jax.random.normal(stream_key, dims, jnp.float32)
    if cuts:
        drawn = drawn * steps_of(stream_key, dims, cuts, -0.22, 0.18)
    return jnp.clip(drawn, -limit, limit).astype(held_as)


def setup_inputs(seed: int = 0) -> dict:
    streams_of = jax.random.split(jax.random.key(seed), 6)
    distribution = jnp.clip(jnp.exp(math.log(2.0) - 2.3025851 * jax.random.uniform(streams_of[0], (NXC, NYC, NVF), jnp.float32) ** steps_of(streams_of[0], (NXC, NYC, NVF), ((0, 8), (1, 4)), -0.2, 0.2)), 0.2, 2.0)
    relax_rate = jnp.clip(jnp.exp(math.log(0.8) - 2.7725887 * jax.random.uniform(streams_of[1], (NXC, NYC), jnp.float32) ** steps_of(streams_of[1], (NXC, NYC), ((0, 8), (1, 4)), -0.2, 0.2)), 0.05, 0.8)
    block_level = draw_block_level(jax.random.fold_in(streams_of[5], 71), 0)
    block_link = draw_block_link(jax.random.fold_in(streams_of[5], 71), 0)
    remap_values = centred(streams_of[4], (2, VBF, BLK, BLK), BLK ** -0.5, 0.25, ((1, 4),))
    return {"distribution": distribution, "relax_rate": relax_rate, "block_level": block_level, "block_link": block_link, "remap_values": remap_values}


cfl_ratio = 0.03
spacing_coarse = 0.5
spacing_fine = 0.4

def velocity_tables(level, points):
    position = jnp.arange(points, dtype=jnp.int32)
    side = jnp.where(level == 1, SF, SC).astype(jnp.int32)
    spacing = jnp.where(level == 1, spacing_fine, spacing_coarse).astype(jnp.float32)
    centre = (side - 1).astype(jnp.float32) * 0.5
    along_x = spacing * ((position // (side * side)).astype(jnp.float32) - centre)
    along_y = spacing * ((position // side % side).astype(jnp.float32) - centre)
    along_z = spacing * ((position % side).astype(jnp.float32) - centre)
    valid = position < side * side * side
    return (along_x, along_y, along_z, valid, spacing)

def relax_update(distribution, relax_rate, level, from_lower, from_upper, from_left, from_right):
    points = distribution.shape[-1]
    along_x, along_y, along_z, valid, spacing = velocity_tables(level, points)
    weight = spacing * spacing * spacing
    masked = jnp.where(valid, distribution, 0.0)
    particle_count_field = weight * lax.optimization_barrier(jnp.sum(masked, -1))
    mean_flow_first_axis = weight * lax.optimization_barrier(jnp.sum(masked * along_x, -1)) / particle_count_field
    mean_flow_second_axis = weight * lax.optimization_barrier(jnp.sum(masked * along_y, -1)) / particle_count_field
    mean_flow_third_axis = weight * lax.optimization_barrier(jnp.sum(masked * along_z, -1)) / particle_count_field
    motion_squared_half = weight * lax.optimization_barrier(jnp.sum(masked * (along_x * along_x + along_y * along_y + along_z * along_z), -1)) / particle_count_field
    thermal_level = (motion_squared_half - mean_flow_first_axis * mean_flow_first_axis - mean_flow_second_axis * mean_flow_second_axis - mean_flow_third_axis * mean_flow_third_axis) / 3.0
    relative_speed_first = along_x - mean_flow_first_axis[..., None]
    relative_speed_second = along_y - mean_flow_second_axis[..., None]
    relative_speed_third = along_z - mean_flow_third_axis[..., None]
    maxwell_prefactor = 2.0 * math.pi * thermal_level
    maxwell_target_state = (particle_count_field / (maxwell_prefactor * jnp.sqrt(maxwell_prefactor)))[..., None] * jnp.exp(-(relative_speed_first * relative_speed_first + relative_speed_second * relative_speed_second + relative_speed_third * relative_speed_third) / (2.0 * thermal_level[..., None]))
    forward_x = jnp.maximum(along_x, 0.0)
    backward_x = jnp.minimum(along_x, 0.0)
    forward_y = jnp.maximum(along_y, 0.0)
    backward_y = jnp.minimum(along_y, 0.0)
    transport = forward_x * (distribution - from_lower) + backward_x * (from_upper - distribution)
    transport = transport + forward_y * (distribution - from_left) + backward_y * (from_right - distribution)
    result = distribution - cfl_ratio * transport + relax_rate[..., None] * (maxwell_target_state - distribution)
    return jnp.where(valid, result, 0.0)

def remap_face(face_tile, source_level, block_link, remap_values):
    rows_count = face_tile.shape[0]
    pieces = face_tile.reshape(rows_count, VBF, BLK)
    fine_index = jnp.arange(VBF, dtype=jnp.int32)
    coarse_source = source_level == 0
    in_block = jnp.where(coarse_source, block_link[0], fine_index).astype(jnp.int32)
    out_block = jnp.where(coarse_source, fine_index, block_link[1]).astype(jnp.int32)
    values = lax.dynamic_index_in_dim(remap_values, source_level, 0, keepdims=False).astype(jnp.float32)
    inputs = jnp.take(pieces, in_block, axis=1).astype(jnp.float32)
    products = jnp.einsum('rjx,jxy->rjy', inputs, values, precision=lax.Precision.HIGHEST)
    selector = (out_block[:, None] == fine_index[None, :]).astype(jnp.float32)
    placed = jnp.einsum('rjy,jo->roy', products, selector, precision=lax.Precision.HIGHEST)
    return placed.reshape(rows_count, NVF)

def reference(distribution, relax_rate, block_level, block_link, remap_values):

    def neighbour_layer(raw, source_level, differs):

        def active(layer):
            return remap_face(layer.astype(jnp.bfloat16), source_level, block_link, remap_values)

        def passive(layer):
            return layer
        return lax.cond(differs, active, passive, raw)

    def block_step(block):
        start = block * CX
        own = lax.dynamic_slice_in_dim(distribution, start, CX, 0)
        rates = lax.dynamic_slice_in_dim(relax_rate, start, CX, 0)
        level = block_level[block]
        lower_level = block_level[jnp.maximum(block - 1, 0)]
        upper_level = block_level[jnp.minimum(block + 1, N_GX - 1)]
        below = lax.dynamic_index_in_dim(distribution, jnp.maximum(start - 1, 0), 0, keepdims=False)
        above = lax.dynamic_index_in_dim(distribution, jnp.minimum(start + CX, NXC - 1), 0, keepdims=False)
        lower_ghost = neighbour_layer(below, lower_level, (block > 0) & (lower_level != level))
        upper_ghost = neighbour_layer(above, upper_level, (block < N_GX - 1) & (upper_level != level))
        lower_ghost = jnp.where(block > 0, lower_ghost, 0.0)
        upper_ghost = jnp.where(block < N_GX - 1, upper_ghost, 0.0)
        from_lower = jnp.concatenate([lower_ghost[None], own[:-1]], 0)
        from_upper = jnp.concatenate([own[1:], upper_ghost[None]], 0)
        zero_column = jnp.zeros((CX, 1, NVF), jnp.float32)
        from_left = jnp.concatenate([zero_column, own[:, :-1]], 1)
        from_right = jnp.concatenate([own[:, 1:], zero_column], 1)
        return relax_update(own, rates, level, from_lower, from_upper, from_left, from_right)
    blocks = lax.map(block_step, jnp.arange(N_GX, dtype=jnp.int32))
    return blocks.reshape(NXC, NYC, NVF)
```

```python
import functools
import math

import jax
import jax.numpy as jnp
from jax import lax
from jax.experimental import pallas as pl
from jax.experimental.pallas import tpu as pltpu
from jax.sharding import PartitionSpec as P

SC = 16
SF = 32
BLK = 512
NVC = 4096
NVF = 32768
VBC = NVC // BLK
VBF = NVF // BLK
HALF_F = VBF // 2
HALF_C = VBC // 2

cfl_ratio = 0.03
spacing_coarse = 0.5
spacing_fine = 0.4

BOTH = ("gx", "gy")
SMEM = pl.BlockSpec(memory_space=pltpu.SMEM)
VMEM = pl.BlockSpec(memory_space=pltpu.VMEM)
ANY = pl.BlockSpec(memory_space=pl.ANY)
F32 = jnp.float32
BF16 = jnp.bfloat16


def place(level_ref):
    block = lax.axis_index("gx")
    own = level_ref[block]
    lower = level_ref[jnp.maximum(block - 1, 0)]
    upper = level_ref[jnp.minimum(block + 1, level_ref.shape[0] - 1)]
    return block, own, lower != own, upper != own


def block_at(ref, index):
    return ref[:, pl.ds(pl.multiple_of(index * BLK, BLK), BLK)]


def prepare_kernel(
    level_ref, link_ref, cells_ref, even_ref, odd_ref, ahead_ref, back_ref, index_ref, row_ref
):
    block, own, lower_differs, upper_differs = place(level_ref)
    fine = own == 1
    cells_y = cells_ref.shape[0]

    def fill(target_ref, going_up):
        differs = jnp.where(going_up, upper_differs, lower_differs)
        gathers = differs & fine

        @pl.when(gathers)
        def _():
            def look(f, count):
                index_ref[count] = f
                hit = (link_ref[1, f] >= HALF_C) == going_up
                return count + hit.astype(jnp.int32)

            lax.fori_loop(0, VBF, look, jnp.int32(0), unroll=4)

        @pl.when(jnp.logical_not(gathers))
        def _():
            plain = going_up & jnp.logical_not(differs)
            start = jnp.where(plain, jnp.where(fine, HALF_F, HALF_C), 0)

            def number(j, carry):
                index_ref[j] = start + j
                return carry

            lax.fori_loop(0, HALF_F, number, 0, unroll=4)

        def copy(j, carry):
            target_ref[j] = block_at(cells_ref, index_ref[j]).astype(BF16)
            return carry

        @pl.when(fine)
        def _():
            lax.fori_loop(0, HALF_F, copy, 0, unroll=4)

        @pl.when(jnp.logical_not(fine))
        def _():
            lax.fori_loop(0, VBC, copy, 0, unroll=4)

    on_even = block % 2 == 0
    fill(odd_ref, jnp.logical_not(on_even))
    fill(even_ref, on_even)

    def rows(target_ref, row, parity):
        @pl.when(fine)
        def _():
            for i in range(HALF_F):
                row_ref[i : i + 1, :] = cells_ref[
                    row : row + 1, (2 * i + parity) * BLK : (2 * i + parity + 1) * BLK
                ]

        @pl.when(jnp.logical_not(fine))
        def _():
            for i in range(VBC):
                row_ref[i : i + 1, :] = cells_ref[row : row + 1, i * BLK : (i + 1) * BLK]

        target_ref[...] = row_ref[...].astype(BF16)

    rows(ahead_ref, cells_y - 1, 1)
    rows(back_ref, 0, 0)


def prepare(levels, links, cells):
    half = jax.ShapeDtypeStruct((HALF_F, cells.shape[0], BLK), BF16)
    row = jax.ShapeDtypeStruct((HALF_F, BLK), BF16)
    return pl.pallas_call(
        prepare_kernel,
        name="prepare",
        out_shape=(half, half, row, row),
        in_specs=[SMEM, SMEM, VMEM],
        out_specs=(VMEM,) * 4,
        scratch_shapes=[pltpu.SMEM((VBF + 1,), jnp.int32), pltpu.VMEM((HALF_F, BLK), F32)],
        cost_estimate=pl.CostEstimate(flops=10**6, bytes_accessed=2 * 10**6, transcendentals=0),
        compiler_params=pltpu.CompilerParams(vmem_limit_bytes=8 << 20),
    )(levels, links, cells)


def relax_kernel(level_ref, rate_ref, cells_ref, left_ref, right_ref, out_ref, side_ref):
    _, own, _, _ = place(level_ref)
    rows_n = cells_ref.shape[0]

    def run(side, spacing):
        width = side * side
        mid = width // 2
        centre = (side - 1) * 0.5
        lane = lax.broadcasted_iota(jnp.int32, (rows_n, width), 1)
        along_y = spacing * ((lane // side).astype(F32) - centre)
        along_z = spacing * ((lane % side).astype(F32) - centre)

        def plane_at(i):
            return cells_ref[:, pl.ds(pl.multiple_of(i * width, width), width)]

        def speed_at(i):
            return spacing * (lax.convert_element_type(i, F32) - centre)

        def gather(i, sums):
            total, first, second = sums
            plane = plane_at(i)
            speed = speed_at(i)
            return total + plane, first + plane * speed, second + plane * (speed * speed)

        zero = jnp.zeros((rows_n, width), F32)
        total, first, second = lax.fori_loop(0, side, gather, (zero, zero, zero), unroll=4)

        def over(value):
            return jnp.broadcast_to(jnp.sum(value, axis=1, keepdims=True), (rows_n, 128))

        weight = spacing * spacing * spacing
        density = weight * over(total)
        scale = weight / density
        mean_x = scale * over(first)
        mean_y = scale * over(total * along_y)
        mean_z = scale * over(total * along_z)
        square = scale * over(second + total * (along_y * along_y + along_z * along_z))
        heat = (square - mean_x * mean_x - mean_y * mean_y - mean_z * mean_z) / 3.0
        row = lax.broadcasted_iota(jnp.int32, (rows_n, 128), 0)
        rate = jnp.zeros((rows_n, 128), F32)
        for r in range(rows_n):
            rate = jnp.where(row == r, rate_ref[0, r], rate)
        spread = 2.0 * math.pi * heat
        peak = rate * density / (spread * jnp.sqrt(spread))
        inverse = -0.5 / heat

        def wide(value):
            return jnp.concatenate([value] * (width // 128), axis=1)

        off_y = along_y - wide(mean_y)
        off_z = along_z - wide(mean_z)
        across = wide(peak) * jnp.exp((off_y * off_y + off_z * off_z) * wide(inverse))
        drift = cfl_ratio * jnp.abs(along_y)
        keep = (1.0 - wide(rate)) - drift
        wide_row = lax.broadcasted_iota(jnp.int32, (rows_n, mid), 0)

        def update(i, carry):
            plane = plane_at(i)
            speed = speed_at(i)
            off_x = speed - mean_x
            along = wide(jnp.exp(off_x * off_x * inverse))
            if side == SF:
                right = side_ref[1, pl.ds(i, 1), :]
                left = side_ref[0, pl.ds(i, 1), :]
            else:
                slot, offset = i // 2, (i % 2) * width
                right = side_ref[1, slot : slot + 1, offset : offset + mid]
                left = side_ref[0, slot : slot + 1, offset + mid : offset + width]
            low, high = plane[:, :mid], plane[:, mid:]
            beyond = jnp.where(wide_row == rows_n - 1, right, pltpu.roll(low, rows_n - 1, 0))
            before = jnp.where(wide_row == 0, left, pltpu.roll(high, 1, 0))
            beside = jnp.concatenate([beyond, before], axis=1)
            factor = keep - cfl_ratio * jnp.abs(speed)
            out_ref[:, pl.ds(pl.multiple_of(i * width, width), width)] = (
                plane * factor + drift * beside + along * across
            )
            return carry

        if side == SF:
            lax.fori_loop(0, side, update, 0, unroll=4)
        else:
            for i in range(side):
                update(i, 0)

    side_ref[0] = left_ref[...].astype(F32)
    side_ref[1] = right_ref[...].astype(F32)

    @pl.when(own == 1)
    def _():
        run(SF, spacing_fine)

    @pl.when(own != 1)
    def _():
        run(SC, spacing_coarse)


def relax(levels, rate, cells, left, right):
    return pl.pallas_call(
        relax_kernel,
        name="relax",
        out_shape=jax.ShapeDtypeStruct(cells.shape, F32),
        in_specs=[SMEM, SMEM, VMEM, VMEM, VMEM],
        out_specs=VMEM,
        scratch_shapes=[pltpu.VMEM((2, HALF_F, BLK), F32)],
        cost_estimate=pl.CostEstimate(flops=10**7, bytes_accessed=4 * 10**6, transcendentals=10**5),
        compiler_params=pltpu.CompilerParams(vmem_limit_bytes=16 << 20),
    )(levels, rate, cells, left, right)


def pieces_kernel(group, level_ref, link_ref, even_ref, odd_ref, *out_refs):
    block, own, lower_differs, _ = place(level_ref)
    me = lax.axis_index("gy")
    local = VBF // group
    use_even = (block % 2 == 0) != lower_differs

    def count(f, starts):
        hit = ((link_ref[1, f] >= HALF_C) == lower_differs).astype(jnp.int32)
        return starts + hit

    def fill(source_ref):
        for s, out_ref in enumerate(out_refs):
            holder = lax.rem(me + s, group)
            start = lax.fori_loop(0, holder * local, count, jnp.int32(0))
            for j in range(local):
                out_ref[j] = source_ref[jnp.minimum(start + j, HALF_F - 1)]

    @pl.when(use_even)
    def _():
        fill(even_ref)

    @pl.when(jnp.logical_not(use_even))
    def _():
        fill(odd_ref)


def pieces(levels, links, even, odd, group):
    piece = jax.ShapeDtypeStruct((VBF // group,) + even.shape[1:], BF16)
    return pl.pallas_call(
        functools.partial(pieces_kernel, group),
        name="pieces",
        out_shape=(piece,) * group,
        in_specs=[SMEM, SMEM, VMEM, VMEM],
        out_specs=(VMEM,) * group,
        cost_estimate=pl.CostEstimate(flops=10**5, bytes_accessed=10**6, transcendentals=0),
        compiler_params=pltpu.CompilerParams(vmem_limit_bytes=8 << 20),
    )(levels, links, even, odd)


def coarse_kernel(group, level_ref, even_ref, odd_ref, out_ref):
    block, own, lower_differs, _ = place(level_ref)
    use_even = (block % 2 == 0) != lower_differs

    @pl.when(use_even)
    def _():
        out_ref[...] = even_ref[0:VBC]

    @pl.when(jnp.logical_not(use_even))
    def _():
        out_ref[...] = odd_ref[0:VBC]


def coarse_piece(levels, even, odd, group):
    return pl.pallas_call(
        functools.partial(coarse_kernel, group),
        name="coarse_piece",
        out_shape=jax.ShapeDtypeStruct((VBC,) + even.shape[1:], BF16),
        in_specs=[SMEM, VMEM, VMEM],
        out_specs=VMEM,
        cost_estimate=pl.CostEstimate(flops=10**5, bytes_accessed=10**6, transcendentals=0),
        compiler_params=pltpu.CompilerParams(vmem_limit_bytes=8 << 20),
    )(levels, even, odd)


def stacked(refs, index):
    return jnp.concatenate([ref[index].astype(F32) for ref in refs], axis=0).astype(BF16)


def to_coarse_kernel(group, level_ref, link_ref, values_ref, *refs):
    in_refs, out_refs = refs[:group], refs[group : 2 * group]
    held_ref, sum_ref, sems = refs[2 * group :]
    _, _, lower_differs, _ = place(level_ref)
    local = values_ref.shape[1]
    cells_y = in_refs[0].shape[1]
    first = lax.axis_index("gy") * local
    offset = jnp.where(lower_differs, HALF_C, 0)

    def copy(j):
        return pltpu.make_async_copy(values_ref.at[1, j], held_ref.at[j], sems.at[j])

    targets = [link_ref[1, first + j] - offset for j in range(local)]
    needed = [(t >= 0) & (t < HALF_C) for t in targets]
    for j in range(local):

        @pl.when(needed[j])
        def _(j=j):
            copy(j).start()

    sum_ref[...] = jnp.zeros_like(sum_ref)
    slot = jnp.int32(0)
    for j in range(local):

        @pl.when(needed[j])
        def _(j=j, slot=slot):
            copy(j).wait()
            sum_ref[targets[j]] += jnp.dot(
                stacked(in_refs, slot), held_ref[j], preferred_element_type=F32
            )

        slot = slot + needed[j].astype(jnp.int32)
    for s, out_ref in enumerate(out_refs):
        out_ref[...] = sum_ref[:, s * cells_y : (s + 1) * cells_y, :].astype(BF16)


def to_fine_kernel(group, level_ref, link_ref, values_ref, *refs):
    in_refs, out_refs = refs[:group], refs[group : 2 * group]
    held_ref, sems = refs[2 * group :]
    _, _, lower_differs, _ = place(level_ref)
    local = values_ref.shape[1]
    cells_y = in_refs[0].shape[1]
    first = lax.axis_index("gy") * local
    active = (first >= HALF_F) == lower_differs

    @pl.when(active)
    def _():
        def copy(j):
            return pltpu.make_async_copy(values_ref.at[0, j], held_ref.at[j], sems.at[j])

        for j in range(local):
            copy(j).start()
        for j in range(local):
            copy(j).wait()
            product = jnp.dot(
                stacked(in_refs, link_ref[0, first + j]),
                held_ref[j],
                preferred_element_type=F32,
            ).astype(BF16)
            for s, out_ref in enumerate(out_refs):
                out_ref[j] = product[s * cells_y : (s + 1) * cells_y, :]


def multiply(kernel, levels, links, values, arrived, slots, scratch):
    group = len(arrived)
    local = values.shape[1]
    out = jax.ShapeDtypeStruct((slots,) + arrived[0].shape[1:], BF16)
    return pl.pallas_call(
        functools.partial(kernel, group),
        name=kernel.__name__,
        out_shape=(out,) * group,
        in_specs=[SMEM, SMEM, ANY] + [VMEM] * group,
        out_specs=(VMEM,) * group,
        scratch_shapes=[pltpu.VMEM((local, BLK, BLK), BF16)]
        + scratch
        + [pltpu.SemaphoreType.DMA((local,))],
        cost_estimate=pl.CostEstimate(
            flops=2 * local * 32 * BLK * BLK, bytes_accessed=2 * local * BLK * BLK, transcendentals=0
        ),
        compiler_params=pltpu.CompilerParams(vmem_limit_bytes=24 << 20),
    )(levels, links, values, *arrived)


def finish_kernel(role, group, level_ref, base_ref, even_ref, odd_ref, *refs):
    in_refs, out_ref = refs[:-1], refs[-1]
    block, own, lower_differs, upper_differs = place(level_ref)
    on_even = block % 2 == 0
    me = lax.axis_index("gy")

    def add(index, ghost, side, spacing):
        per = (side * side) // 128
        centre = (side - 1) * 0.5
        for c in range(BLK // 128):
            plane = (index * (BLK // 128) + c) // per
            speed = cfl_ratio * spacing * jnp.abs(lax.convert_element_type(plane, F32) - centre)
            at = pl.ds(pl.multiple_of(index * BLK + c * 128, 128), 128)
            out_ref[:, at] = base_ref[:, at] + speed * ghost[:, c * 128 : (c + 1) * 128]

    def plain(upward, count, side, spacing):
        def step(j, carry):
            a, b = even_ref[j], odd_ref[j]
            take_even = on_even == upward
            ghost = jnp.where(take_even, a.astype(F32), b.astype(F32))
            add(j if upward else count + j, ghost, side, spacing)
            return carry

        lax.fori_loop(0, count, step, 0, unroll=4)

    def halves(count, side, spacing, remapped):
        for upward, differs in ((True, upper_differs), (False, lower_differs)):
            if remapped is None:
                plain(upward, count, side, spacing)
            else:
                pl.when(jnp.logical_not(differs))(
                    functools.partial(plain, upward, count, side, spacing)
                )
                pl.when(differs)(functools.partial(remapped, upward))

    def from_fine(upward):
        for o in range(HALF_C):
            ghost = in_refs[0][o].astype(F32)
            for ref in in_refs[1:]:
                ghost = ghost + ref[o].astype(F32)
            add(o if upward else HALF_C + o, ghost, SC, spacing_coarse)

    def from_coarse(upward):
        for s, ref in enumerate(in_refs):
            local = ref.shape[0]
            first = lax.rem(me + s, group) * local

            @pl.when((first < HALF_F) == upward)
            def _(ref=ref, first=first, local=local):
                def step(j, carry):
                    add(first + j, ref[j].astype(F32), SF, spacing_fine)
                    return carry

                lax.fori_loop(0, local, step, 0, unroll=4)

    def fine():
        halves(HALF_F, SF, spacing_fine, None if role == 0 else from_coarse)

    def coarse():
        out_ref[:, NVC:] = jnp.zeros((out_ref.shape[0], NVF - NVC), F32)
        halves(HALF_C, SC, spacing_coarse, None if role == 0 else from_fine)

    if role != 1:
        pl.when(own == 1)(fine) if role == 0 else fine()
    if role != 2:
        pl.when(own != 1)(coarse) if role == 0 else coarse()


def finish(role, group, levels, base, even, odd, arrived):
    return pl.pallas_call(
        functools.partial(finish_kernel, role, group),
        name="finish",
        out_shape=jax.ShapeDtypeStruct(base.shape, F32),
        in_specs=[SMEM, VMEM, VMEM, VMEM] + [VMEM] * len(arrived),
        out_specs=VMEM,
        cost_estimate=pl.CostEstimate(flops=10**6, bytes_accessed=3 * 10**6, transcendentals=0),
        compiler_params=pltpu.CompilerParams(vmem_limit_bytes=16 << 20),
    )(levels, base, even, odd, *arrived)


def on_device(distribution, relax_rate, block_level, block_link, remap_values):
    blocks, group = lax.axis_size("gx"), lax.axis_size("gy")
    cells_y = distribution.shape[1]
    cells = distribution[0]

    def partners(parity):
        pairs = []
        for low in range(parity, blocks - 1, 2):
            for y in range(group):
                here, there = low * group + y, (low + 1) * group + y
                pairs += [(here, there), (there, here)]
        return pairs

    def shift(value, by):
        return lax.ppermute(value, "gy", [(i, (i + by) % group) for i in range(group)])

    block = lax.axis_index("gx")
    own = block_level[block]
    lower = block_level[jnp.maximum(block - 1, 0)]
    upper = block_level[jnp.minimum(block + 1, blocks - 1)]
    role = jnp.where((lower != own) | (upper != own), 1 + own, 0)

    even, odd, ahead, back = prepare(block_level, block_link, cells)
    odd = lax.ppermute(odd, BOTH, partners(1))
    even = lax.ppermute(even, BOTH, partners(0))

    def beside(ahead, back):
        left = lax.ppermute(ahead, "gy", [(i, i + 1) for i in range(group - 1)])
        right = lax.ppermute(back, "gy", [(i + 1, i) for i in range(group - 1)])
        return relax(block_level, relax_rate, cells, left, right)

    def around(outgoing, by):
        return [outgoing[0]] + [shift(outgoing[s], by * s) for s in range(1, group)]

    def alone(even, odd, ahead, back):
        base = beside(ahead, back)
        return finish(0, group, block_level, base, even, odd, ())

    def to_coarse(even, odd, ahead, back):
        arrived = around(pieces(block_level, block_link, even, odd, group), 1)
        sums = pltpu.VMEM((HALF_C, group * cells_y, BLK), F32)
        made = multiply(
            to_coarse_kernel, block_level, block_link, remap_values, arrived, HALF_C, [sums]
        )
        arrived = around(made, -1)
        base = beside(ahead, back)
        return finish(1, group, block_level, base, even, odd, arrived)

    def to_fine(even, odd, ahead, back):
        piece = coarse_piece(block_level, even, odd, group)
        arrived = around([piece] * group, 1)
        local = remap_values.shape[1]
        made = multiply(to_fine_kernel, block_level, block_link, remap_values, arrived, local, [])
        arrived = around(made, -1)
        base = beside(ahead, back)
        return finish(2, group, block_level, base, even, odd, arrived)

    updated = lax.switch(role, [alone, to_coarse, to_fine], even, odd, ahead, back)
    return updated[None]


def solution(mesh):
    in_specs = (P("gx", "gy", None), P("gx", "gy"), P(), P(), P(None, "gy", None, None))
    out_specs = P("gx", "gy", None)
    return jax.shard_map(
        on_device, mesh=mesh, in_specs=in_specs, out_specs=out_specs, check_vma=False
    )
```

```python
import functools
import math

import jax
import jax.numpy as jnp
from jax import lax
from jax.experimental import pallas as pl
from jax.experimental.pallas import tpu as pltpu
from jax.sharding import PartitionSpec as P

SC = 16
SF = 32
BLK = 512
NVC = 4096
NVF = 32768
VBC = NVC // BLK
VBF = NVF // BLK
HALF_F = VBF // 2
HALF_C = VBC // 2

cfl_ratio = 0.03
spacing_coarse = 0.5
spacing_fine = 0.4

BOTH = ("gx", "gy")
SMEM = pl.BlockSpec(memory_space=pltpu.SMEM)
VMEM = pl.BlockSpec(memory_space=pltpu.VMEM)
HBM = pl.BlockSpec(memory_space=pltpu.HBM)
F32 = jnp.float32
BF16 = jnp.bfloat16


def place(level_ref):
    block = lax.axis_index("gx")
    own = level_ref[block]
    lower = level_ref[jnp.maximum(block - 1, 0)]
    upper = level_ref[jnp.minimum(block + 1, level_ref.shape[0] - 1)]
    return block, own, lower != own, upper != own


def peer(me, step, group):
    if group & (group - 1):
        raise ValueError(group)
    return me ^ step


def block_at(ref, index):
    return ref[:, pl.ds(pl.multiple_of(index * BLK, BLK), BLK)]


def prepare_kernel(
    level_ref,
    link_ref,
    cells_ref,
    role_ref,
    small_ref,
    even_ref,
    odd_ref,
    ahead_ref,
    back_ref,
    index_ref,
    row_ref,
):
    block, own, lower_differs, upper_differs = place(level_ref)
    fine = own == 1
    cells_y = cells_ref.shape[0]
    use_odd = (block % 2 == 0) == lower_differs
    role = jnp.where(fine, jnp.where(use_odd, 3, 2), 1)
    role_ref[0] = jnp.where(lower_differs | upper_differs, role, 0)
    for j in range(VBC):
        small_ref[j] = cells_ref[:, j * BLK : (j + 1) * BLK].astype(BF16)

    def fill(target_ref, going_up):
        differs = jnp.where(going_up, upper_differs, lower_differs)
        gathers = differs & fine

        @pl.when(gathers)
        def _():
            def look(f, count):
                index_ref[count] = f
                hit = (link_ref[1, f] >= HALF_C) == going_up
                return count + hit.astype(jnp.int32)

            lax.fori_loop(0, VBF, look, jnp.int32(0), unroll=4)

        @pl.when(jnp.logical_not(gathers))
        def _():
            plain = going_up & jnp.logical_not(differs)
            start = jnp.where(plain, jnp.where(fine, HALF_F, HALF_C), 0)

            def number(j, carry):
                index_ref[j] = start + j
                return carry

            lax.fori_loop(0, HALF_F, number, 0, unroll=4)

        def copy(j, carry):
            target_ref[j] = block_at(cells_ref, index_ref[j]).astype(BF16)
            return carry

        @pl.when(fine)
        def _():
            lax.fori_loop(0, HALF_F, copy, 0, unroll=4)

        @pl.when(jnp.logical_not(fine))
        def _():
            lax.fori_loop(0, VBC, copy, 0, unroll=4)

    on_even = block % 2 == 0
    fill(odd_ref, jnp.logical_not(on_even))
    fill(even_ref, on_even)

    def rows(target_ref, row, parity):
        @pl.when(fine)
        def _():
            for i in range(HALF_F):
                row_ref[i : i + 1, :] = cells_ref[
                    row : row + 1, (2 * i + parity) * BLK : (2 * i + parity + 1) * BLK
                ]

        @pl.when(jnp.logical_not(fine))
        def _():
            for i in range(VBC):
                row_ref[i : i + 1, :] = cells_ref[row : row + 1, i * BLK : (i + 1) * BLK]

        target_ref[...] = row_ref[...].astype(BF16)

    rows(ahead_ref, cells_y - 1, 1)
    rows(back_ref, 0, 0)


def prepare(levels, links, cells):
    half = jax.ShapeDtypeStruct((HALF_F, cells.shape[0], BLK), BF16)
    small = jax.ShapeDtypeStruct((VBC, cells.shape[0], BLK), BF16)
    row = jax.ShapeDtypeStruct((HALF_F, BLK), BF16)
    return pl.pallas_call(
        prepare_kernel,
        name="prepare",
        out_shape=(jax.ShapeDtypeStruct((1,), jnp.int32), small, half, half, row, row),
        in_specs=[SMEM, SMEM, VMEM],
        out_specs=(SMEM,) + (VMEM,) * 5,
        scratch_shapes=[pltpu.SMEM((VBF + 1,), jnp.int32), pltpu.VMEM((HALF_F, BLK), F32)],
        cost_estimate=pl.CostEstimate(flops=10**6, bytes_accessed=2 * 10**6, transcendentals=0),
        compiler_params=pltpu.CompilerParams(vmem_limit_bytes=8 << 20),
    )(levels, links, cells)


CHUNKS = 8
PART = NVF // CHUNKS


def ghost_at(ref, index):
    return ref[index].astype(F32)


def relax_kernel(
    alone,
    level_ref,
    rate_ref,
    cells_ref,
    even_ref,
    odd_ref,
    left_ref,
    right_ref,
    out_ref,
    *refs,
):
    side_ref, done_ref, sems = refs[-3:]
    block, own, lower_differs, upper_differs = place(level_ref)
    on_even = block % 2 == 0
    rows_n = cells_ref.shape[0]

    def flush(chunk):
        at = pl.ds(chunk * PART, PART)
        return pltpu.make_async_copy(done_ref.at[:, at], out_ref.at[:, at], sems.at[chunk])

    def run(side, spacing):
        width = side * side
        mid = width // 2
        middle = side // 2
        centre = (side - 1) * 0.5
        lane = lax.broadcasted_iota(jnp.int32, (rows_n, width), 1)
        along_y = spacing * ((lane // side).astype(F32) - centre)
        along_z = spacing * ((lane % side).astype(F32) - centre)

        def span(i):
            start = i * width
            return pl.ds(start if isinstance(i, int) else pl.multiple_of(start, width), width)

        def speed_at(i):
            return spacing * (lax.convert_element_type(i, F32) - centre)

        def gather(i, sums):
            total, first, second = sums
            plane = cells_ref[:, span(i)]
            speed = speed_at(i)
            return total + plane, first + plane * speed, second + plane * (speed * speed)

        zero = jnp.zeros((rows_n, width), F32)
        total, first, second = lax.fori_loop(0, side, gather, (zero, zero, zero), unroll=4)

        def over(value):
            return jnp.broadcast_to(jnp.sum(value, axis=1, keepdims=True), (rows_n, 128))

        weight = spacing * spacing * spacing
        density = weight * over(total)
        scale = weight / density
        mean_x = scale * over(first)
        mean_y = scale * over(total * along_y)
        mean_z = scale * over(total * along_z)
        square = scale * over(second + total * (along_y * along_y + along_z * along_z))
        heat = (square - mean_x * mean_x - mean_y * mean_y - mean_z * mean_z) / 3.0
        row = lax.broadcasted_iota(jnp.int32, (rows_n, 128), 0)
        rate = jnp.zeros((rows_n, 128), F32)
        for r in range(rows_n):
            rate = jnp.where(row == r, rate_ref[0, r], rate)
        spread = 2.0 * math.pi * heat
        peak = rate * density / (spread * jnp.sqrt(spread))
        inverse = -0.5 / heat

        def wide(value):
            return jnp.concatenate([value] * (width // 128), axis=1)

        off_y = along_y - wide(mean_y)
        off_z = along_z - wide(mean_z)
        across = wide(peak) * jnp.exp((off_y * off_y + off_z * off_z) * wide(inverse))
        drift = cfl_ratio * jnp.abs(along_y)
        keep = (1.0 - wide(rate)) - drift
        wide_row = lax.broadcasted_iota(jnp.int32, (rows_n, mid), 0)

        def update(i, upward):
            plane = cells_ref[:, span(i)]
            speed = speed_at(i)
            off_x = speed - mean_x
            along = wide(jnp.exp(off_x * off_x * inverse))
            take_even = on_even == upward
            if side == SF:
                right = side_ref[1, pl.ds(i, 1), :]
                left = side_ref[0, pl.ds(i, 1), :]
                slot = 2 * (i if upward else i - middle)
                ghosts = []
                for half in range(2):
                    a, b = ghost_at(even_ref, slot + half), ghost_at(odd_ref, slot + half)
                    ghosts.append(jnp.where(take_even, a, b))
                ghost = jnp.concatenate(ghosts, axis=1)
            else:
                slot, offset = i // 2, (i % 2) * width
                right = side_ref[1, slot : slot + 1, offset : offset + mid]
                left = side_ref[0, slot : slot + 1, offset + mid : offset + width]
                slot = slot if upward else slot - HALF_C
                a, b = ghost_at(even_ref, slot), ghost_at(odd_ref, slot)
                ghost = jnp.where(take_even, a, b)[:, offset : offset + width]
            if not alone:
                ghost = jnp.where(upper_differs if upward else lower_differs, 0.0, ghost)
            low, high = plane[:, :mid], plane[:, mid:]
            beyond = jnp.where(wide_row == rows_n - 1, right, pltpu.roll(low, rows_n - 1, 0))
            before = jnp.where(wide_row == 0, left, pltpu.roll(high, 1, 0))
            beside = jnp.concatenate([beyond, before], axis=1)
            push = cfl_ratio * jnp.abs(speed)
            done_ref[:, span(i)] = (
                plane * (keep - push) + push * ghost + drift * beside + along * across
            )

        if side == SF:
            each = side // CHUNKS
            for chunk in range(CHUNKS):
                upward = chunk < CHUNKS // 2

                def step(k, carry, chunk=chunk, upward=upward):
                    update(chunk * each + k, upward)
                    return carry

                lax.fori_loop(0, each, step, 0, unroll=4)
                flush(chunk).start()
        else:
            for i in range(side):
                update(i, i < middle)
            flush(0).start()
            done_ref[:, NVC:] = jnp.zeros((rows_n, NVF - NVC), F32)
            for chunk in range(1, CHUNKS):
                flush(chunk).start()

    side_ref[0] = left_ref[...].astype(F32)
    side_ref[1] = right_ref[...].astype(F32)

    @pl.when(own == 1)
    def _():
        run(SF, spacing_fine)

    @pl.when(own != 1)
    def _():
        run(SC, spacing_coarse)

    if not alone:
        base_ref = refs[0]
        start = jnp.where(upper_differs, 0, 1)

        @pl.when(own == 1)
        def _():
            @pl.when(upper_differs)
            def _():
                base_ref[...] = done_ref[:, : NVF // 2]

            @pl.when(jnp.logical_not(upper_differs))
            def _():
                base_ref[...] = done_ref[:, NVF // 2 :]

        @pl.when(own != 1)
        def _():
            @pl.when(upper_differs)
            def _():
                base_ref[:, : NVC // 2] = done_ref[:, : NVC // 2]

            @pl.when(jnp.logical_not(upper_differs))
            def _():
                base_ref[:, : NVC // 2] = done_ref[:, NVC // 2 : NVC]

    for chunk in range(CHUNKS):
        flush(chunk).wait()


def relax(alone, levels, rate, cells, even, odd, left, right):
    out = jax.ShapeDtypeStruct(cells.shape, F32)
    half = jax.ShapeDtypeStruct((cells.shape[0], NVF // 2), F32)
    return pl.pallas_call(
        functools.partial(relax_kernel, alone),
        name="relax",
        out_shape=(out,) if alone else (out, half),
        in_specs=[SMEM, SMEM, VMEM, VMEM, VMEM, VMEM, VMEM],
        out_specs=(HBM,) if alone else (HBM, VMEM),
        scratch_shapes=[
            pltpu.VMEM((2, HALF_F, BLK), F32),
            pltpu.VMEM(cells.shape, F32),
            pltpu.SemaphoreType.DMA((CHUNKS,)),
        ],
        cost_estimate=pl.CostEstimate(flops=10**7, bytes_accessed=4 * 10**6, transcendentals=10**5),
        compiler_params=pltpu.CompilerParams(vmem_limit_bytes=16 << 20),
    )(levels, rate, cells, even, odd, left, right)


def pieces_kernel(group, level_ref, link_ref, even_ref, odd_ref, *out_refs):
    block, own, lower_differs, _ = place(level_ref)
    me = lax.axis_index("gy")
    local = VBF // group
    use_even = (block % 2 == 0) != lower_differs

    def count(f, starts):
        hit = ((link_ref[1, f] >= HALF_C) == lower_differs).astype(jnp.int32)
        return starts + hit

    def fill(source_ref):
        for s, out_ref in enumerate(out_refs):
            holder = peer(me, s, group)
            start = lax.fori_loop(0, holder * local, count, jnp.int32(0))
            for j in range(local):
                out_ref[j] = source_ref[jnp.minimum(start + j, HALF_F - 1)]

    @pl.when(use_even)
    def _():
        fill(even_ref)

    @pl.when(jnp.logical_not(use_even))
    def _():
        fill(odd_ref)


def pieces(levels, links, even, odd, group):
    piece = jax.ShapeDtypeStruct((VBF // group,) + even.shape[1:], BF16)
    return pl.pallas_call(
        functools.partial(pieces_kernel, group),
        name="pieces",
        out_shape=(piece,) * group,
        in_specs=[SMEM, SMEM, VMEM, VMEM],
        out_specs=(VMEM,) * group,
        cost_estimate=pl.CostEstimate(flops=10**5, bytes_accessed=10**6, transcendentals=0),
        compiler_params=pltpu.CompilerParams(vmem_limit_bytes=8 << 20),
    )(levels, links, even, odd)


def stacked(refs, index):
    return jnp.concatenate([ref[index].astype(F32) for ref in refs], axis=0).astype(BF16)


def to_coarse_kernel(group, level_ref, link_ref, values_ref, *refs):
    in_refs, out_refs, sum_ref = refs[:group], refs[group : 2 * group], refs[-1]
    _, _, lower_differs, _ = place(level_ref)
    local = values_ref.shape[0]
    cells_y = in_refs[0].shape[1]
    first = lax.axis_index("gy") * local
    offset = jnp.where(lower_differs, HALF_C, 0)

    targets = [link_ref[1, first + j] - offset for j in range(local)]
    needed = [(t >= 0) & (t < HALF_C) for t in targets]
    sum_ref[...] = jnp.zeros_like(sum_ref)
    slot = jnp.int32(0)
    for j in range(local):

        @pl.when(needed[j])
        def _(j=j, slot=slot):
            sum_ref[targets[j]] += jnp.dot(
                stacked(in_refs, slot), values_ref[j], preferred_element_type=F32
            )

        slot = slot + needed[j].astype(jnp.int32)
    for s, out_ref in enumerate(out_refs):
        out_ref[...] = sum_ref[:, s * cells_y : (s + 1) * cells_y, :].astype(BF16)


def to_fine_kernel(group, level_ref, link_ref, values_ref, *refs):
    in_refs, out_refs = refs[:group], refs[group : 2 * group]
    _, _, lower_differs, _ = place(level_ref)
    local = values_ref.shape[0]
    cells_y = in_refs[0].shape[1]
    first = lax.axis_index("gy") * local
    active = (first >= HALF_F) == lower_differs

    @pl.when(active)
    def _():
        for j in range(local):
            product = jnp.dot(
                stacked(in_refs, link_ref[0, first + j]),
                values_ref[j],
                preferred_element_type=F32,
            ).astype(BF16)
            for s, out_ref in enumerate(out_refs):
                out_ref[j] = product[s * cells_y : (s + 1) * cells_y, :]


def multiply(kernel, levels, links, values, arrived, slots, scratch):
    group = len(arrived)
    local = values.shape[0]
    out = jax.ShapeDtypeStruct((slots,) + arrived[0].shape[1:], BF16)
    return pl.pallas_call(
        functools.partial(kernel, group),
        name=kernel.__name__,
        out_shape=(out,) * group,
        in_specs=[SMEM, SMEM, VMEM] + [VMEM] * group,
        out_specs=(VMEM,) * group,
        scratch_shapes=scratch,
        cost_estimate=pl.CostEstimate(
            flops=2 * local * 32 * BLK * BLK, bytes_accessed=2 * local * BLK * BLK, transcendentals=0
        ),
        compiler_params=pltpu.CompilerParams(vmem_limit_bytes=24 << 20),
    )(levels, links, values, *arrived)


def finish_kernel(role, group, level_ref, base_ref, held_ref, *refs):
    in_refs, out_ref, done_ref, sems = refs[:-3], refs[-3], refs[-2], refs[-1]
    _, _, _, upper_differs = place(level_ref)
    me = lax.axis_index("gy")
    parts = sems.shape[0]
    side, spacing, count = (
        (SC, spacing_coarse, HALF_C) if role == 1 else (SF, spacing_fine, HALF_F)
    )
    whole = count * BLK
    part = whole // parts
    centre = (side - 1) * 0.5

    def flush(index):
        start = index * part + jnp.where(upper_differs, 0, whole)
        at = pl.ds(pl.multiple_of(start, part), part)
        return pltpu.make_async_copy(
            done_ref.at[:, pl.ds(pl.multiple_of(index * part, part), part)],
            out_ref.at[:, at],
            sems.at[index],
        )

    first_plane = jnp.where(upper_differs, 0, side // 2)
    if role == 1:
        width = side * side
        for o in range(HALF_C):
            ghost = in_refs[0][o].astype(F32)
            for ref in in_refs[1:]:
                ghost = ghost + ref[o].astype(F32)
            for k in range(BLK // width):
                plane = lax.convert_element_type(first_plane + o * (BLK // width) + k, F32)
                push = cfl_ratio * spacing * jnp.abs(plane - centre)
                at = slice(o * BLK + k * width, o * BLK + (k + 1) * width)
                done_ref[:, at] = base_ref[:, at] + push * ghost[:, k * width : (k + 1) * width]
        flush(0).start()
        flush(0).wait()
        return

    offset = jnp.where(upper_differs, 0, HALF_F)
    for s, ref in enumerate(in_refs):
        local = ref.shape[0]
        first = peer(me, s, group) * local - offset

        @pl.when((first >= 0) & (first < HALF_F))
        def _(ref=ref, first=first, local=local):
            for j in range(local):
                slot = first + j
                plane = lax.convert_element_type(first_plane + slot // 2, F32)
                push = cfl_ratio * spacing * jnp.abs(plane - centre)
                at = pl.ds(pl.multiple_of(slot * BLK, BLK), BLK)
                done_ref[:, at] = base_ref[:, at] + push * ref[j].astype(F32)
            flush(lax.div(first, local)).start()

    for index in range(parts):
        flush(index).wait()


def finish(role, levels, base, held, arrived):
    group = len(arrived)
    rows_n = base.shape[0]
    parts = 1 if role == 1 else group // 2
    whole = NVC // 2 if role == 1 else NVF // 2
    return pl.pallas_call(
        functools.partial(finish_kernel, role, group),
        name="finish",
        out_shape=jax.ShapeDtypeStruct(held.shape, F32),
        in_specs=[SMEM, VMEM, HBM] + [VMEM] * group,
        out_specs=HBM,
        scratch_shapes=[pltpu.VMEM((rows_n, whole), F32), pltpu.SemaphoreType.DMA((parts,))],
        input_output_aliases={2: 0},
        cost_estimate=pl.CostEstimate(flops=10**6, bytes_accessed=10**6, transcendentals=0),
        compiler_params=pltpu.CompilerParams(vmem_limit_bytes=8 << 20),
    )(levels, base, held, *arrived)


def on_device(distribution, relax_rate, block_level, block_link, remap_values):
    blocks, group = lax.axis_size("gx"), lax.axis_size("gy")
    cells_y = distribution.shape[1]
    local = remap_values.shape[1]
    cells = distribution[0]

    def exchange(value, parity):
        pairs = []
        for low in range(parity, blocks - 1, 2):
            for y in range(group):
                here, there = low * group + y, (low + 1) * group + y
                pairs += [(here, there), (there, here)]
        return lax.ppermute(value, BOTH, pairs)

    def around(outgoing):
        return [outgoing[0]] + [
            lax.ppermute(outgoing[s], "gy", [(i, peer(i, s, group)) for i in range(group)])
            for s in range(1, group)
        ]

    role, small, even, odd, ahead, back = prepare(block_level, block_link, cells)
    odd_small = exchange(small, 1)
    even_small = exchange(small, 0)
    odd = exchange(odd, 1)
    even = exchange(even, 0)

    def beside(ahead, back):
        left = lax.ppermute(ahead, "gy", [(i, i + 1) for i in range(group - 1)])
        right = lax.ppermute(back, "gy", [(i + 1, i) for i in range(group - 1)])
        return left, right

    def alone():
        left, right = beside(ahead, back)
        return relax(True, block_level, relax_rate, cells, even, odd, left, right)[0]

    def remapped(role, kernel, slots, scratch, outgoing):
        arrived = around(outgoing)
        sides = beside(ahead, back)
        arrived, sides = lax.optimization_barrier((arrived, sides))
        values = remap_values[1 if role == 1 else 0]
        made = multiply(kernel, block_level, block_link, values, arrived, slots, scratch)
        held, base = relax(False, block_level, relax_rate, cells, even, odd, *sides)
        return finish(role, block_level, base, held, around(made))

    def to_coarse():
        sums = pltpu.VMEM((HALF_C, group * cells_y, BLK), F32)
        outgoing = pieces(block_level, block_link, even, odd, group)
        return remapped(1, to_coarse_kernel, HALF_C, [sums], outgoing)

    def to_fine_even():
        return remapped(2, to_fine_kernel, local, [], [even_small] * group)

    def to_fine_odd():
        return remapped(2, to_fine_kernel, local, [], [odd_small] * group)

    updated = lax.switch(role[0], [alone, to_coarse, to_fine_even, to_fine_odd])
    return updated[None]


def solution(mesh):
    in_specs = (P("gx", "gy", None), P("gx", "gy"), P(), P(), P(None, "gy", None, None))
    out_specs = P("gx", "gy", None)
    return jax.shard_map(
        on_device, mesh=mesh, in_specs=in_specs, out_specs=out_specs, check_vma=False
    )
```

```python
import functools
import math

import jax
import jax.numpy as jnp
from jax import lax
from jax.experimental import pallas as pl
from jax.experimental.pallas import tpu as pltpu
from jax.sharding import PartitionSpec as P

SC = 16
SF = 32
BLK = 512
NVC = 4096
NVF = 32768
VBC = NVC // BLK
VBF = NVF // BLK
HALF_F = VBF // 2
HALF_C = VBC // 2

cfl_ratio = 0.03
spacing_coarse = 0.5
spacing_fine = 0.4

BOTH = ("gx", "gy")
SMEM = pl.BlockSpec(memory_space=pltpu.SMEM)
VMEM = pl.BlockSpec(memory_space=pltpu.VMEM)
HBM = pl.BlockSpec(memory_space=pltpu.HBM)
F32 = jnp.float32
BF16 = jnp.bfloat16


def place(level_ref):
    block = lax.axis_index("gx")
    own = level_ref[block]
    lower = level_ref[jnp.maximum(block - 1, 0)]
    upper = level_ref[jnp.minimum(block + 1, level_ref.shape[0] - 1)]
    return block, own, lower != own, upper != own


def peer(me, step, group):
    if group & (group - 1):
        raise ValueError(group)
    return me ^ step


def few(local):
    return max(1, (3 * local) // 4)


def block_at(ref, index):
    return ref[:, pl.ds(pl.multiple_of(index * BLK, BLK), BLK)]


def prepare_kernel(
    level_ref,
    link_ref,
    cells_ref,
    role_ref,
    even_ref,
    odd_ref,
    ahead_ref,
    back_ref,
    index_ref,
    row_ref,
):
    block, own, lower_differs, upper_differs = place(level_ref)
    fine = own == 1
    cells_y = cells_ref.shape[0]
    group = lax.axis_size("gy")
    local = VBF // group

    def hits(f):
        return ((link_ref[1, f] >= HALF_C) == lower_differs).astype(jnp.int32)

    def most(h, worst):
        count = lax.fori_loop(
            0, local, lambda j, total: total + hits(h * local + j), jnp.int32(0), unroll=4
        )
        return jnp.maximum(worst, count)

    worst = lax.fori_loop(0, group, most, jnp.int32(0))
    coarse_role = jnp.where(worst > few(local), 2, 1)
    role = jnp.where(fine, jnp.where(lower_differs, 3, 4), coarse_role)
    role_ref[0] = jnp.where(lower_differs | upper_differs, role, 0)

    def fill(target_ref, going_up):
        differs = jnp.where(going_up, upper_differs, lower_differs)
        gathers = differs & fine

        @pl.when(gathers)
        def _():
            def look(f, count):
                index_ref[count] = f
                hit = (link_ref[1, f] >= HALF_C) == going_up
                return count + hit.astype(jnp.int32)

            lax.fori_loop(0, VBF, look, jnp.int32(0), unroll=8)

            def copy(j, carry):
                target_ref[j] = block_at(cells_ref, index_ref[j]).astype(BF16)
                return carry

            lax.fori_loop(0, HALF_F, copy, 0, unroll=8)

        @pl.when(fine & jnp.logical_not(differs))
        def _():
            start = jnp.where(going_up, HALF_F, 0)
            for j in range(HALF_F):
                target_ref[j] = block_at(cells_ref, start + j).astype(BF16)

        @pl.when(jnp.logical_not(fine))
        def _():
            start = jnp.where(going_up & jnp.logical_not(differs), HALF_C, 0)
            for j in range(VBC):
                target_ref[j] = block_at(cells_ref, start + j).astype(BF16)

    on_even = block % 2 == 0
    fill(odd_ref, jnp.logical_not(on_even))
    fill(even_ref, on_even)

    def rows(target_ref, row, parity):
        @pl.when(fine)
        def _():
            for i in range(HALF_F):
                row_ref[i : i + 1, :] = cells_ref[
                    row : row + 1, (2 * i + parity) * BLK : (2 * i + parity + 1) * BLK
                ]

        @pl.when(jnp.logical_not(fine))
        def _():
            for i in range(VBC):
                row_ref[i : i + 1, :] = cells_ref[row : row + 1, i * BLK : (i + 1) * BLK]

        target_ref[...] = row_ref[...].astype(BF16)

    rows(ahead_ref, cells_y - 1, 1)
    rows(back_ref, 0, 0)


def prepare(levels, links, cells):
    half = jax.ShapeDtypeStruct((HALF_F, cells.shape[0], BLK), BF16)
    row = jax.ShapeDtypeStruct((HALF_F, BLK), BF16)
    return pl.pallas_call(
        prepare_kernel,
        name="prepare",
        out_shape=(jax.ShapeDtypeStruct((1,), jnp.int32), half, half, row, row),
        in_specs=[SMEM, SMEM, VMEM],
        out_specs=(SMEM,) + (VMEM,) * 4,
        scratch_shapes=[pltpu.SMEM((VBF + 1,), jnp.int32), pltpu.VMEM((HALF_F, BLK), F32)],
        cost_estimate=pl.CostEstimate(flops=10**6, bytes_accessed=2 * 10**6, transcendentals=0),
        compiler_params=pltpu.CompilerParams(vmem_limit_bytes=8 << 20),
    )(levels, links, cells)


CHUNKS = 8
PART = NVF // CHUNKS


def ghost_at(ref, index):
    return ref[index].astype(F32)


def relax_kernel(
    alone,
    level_ref,
    rate_ref,
    cells_ref,
    even_ref,
    odd_ref,
    *refs,
):
    side_ref, done_ref, sems = refs[-3:]
    results = 1 if alone else 2
    row_refs, out_ref = refs[: -3 - results], refs[-3 - results]
    block, own, lower_differs, upper_differs = place(level_ref)
    on_even = block % 2 == 0
    rows_n = cells_ref.shape[0]

    def flush(chunk):
        at = pl.ds(chunk * PART, PART)
        return pltpu.make_async_copy(done_ref.at[:, at], out_ref.at[:, at], sems.at[chunk])

    def run(side, spacing):
        width = side * side
        mid = width // 2
        middle = side // 2
        centre = (side - 1) * 0.5
        lane = lax.broadcasted_iota(jnp.int32, (rows_n, width), 1)
        along_y = spacing * ((lane // side).astype(F32) - centre)
        along_z = spacing * ((lane % side).astype(F32) - centre)

        def span(i):
            start = i * width
            return pl.ds(start if isinstance(i, int) else pl.multiple_of(start, width), width)

        def speed_at(i):
            return spacing * (lax.convert_element_type(i, F32) - centre)

        def gather(i, sums):
            total, first, second = sums
            plane = cells_ref[:, span(i)]
            speed = speed_at(i)
            return total + plane, first + plane * speed, second + plane * (speed * speed)

        zero = jnp.zeros((rows_n, width), F32)
        total, first, second = lax.fori_loop(0, side, gather, (zero, zero, zero), unroll=4)

        def over(value):
            return jnp.broadcast_to(jnp.sum(value, axis=1, keepdims=True), (rows_n, 128))

        weight = spacing * spacing * spacing
        density = weight * over(total)
        scale = weight / density
        mean_x = scale * over(first)
        mean_y = scale * over(total * along_y)
        mean_z = scale * over(total * along_z)
        square = scale * over(second + total * (along_y * along_y + along_z * along_z))
        heat = (square - mean_x * mean_x - mean_y * mean_y - mean_z * mean_z) / 3.0
        row = lax.broadcasted_iota(jnp.int32, (rows_n, 128), 0)
        rate = jnp.zeros((rows_n, 128), F32)
        for r in range(rows_n):
            rate = jnp.where(row == r, rate_ref[0, r], rate)
        spread = 2.0 * math.pi * heat
        peak = rate * density / (spread * jnp.sqrt(spread))
        inverse = -0.5 / heat

        def wide(value):
            return jnp.concatenate([value] * (width // 128), axis=1)

        off_y = along_y - wide(mean_y)
        off_z = along_z - wide(mean_z)
        across = wide(peak) * jnp.exp((off_y * off_y + off_z * off_z) * wide(inverse))
        drift = cfl_ratio * jnp.abs(along_y)
        keep = (1.0 - wide(rate)) - drift
        wide_row = lax.broadcasted_iota(jnp.int32, (rows_n, mid), 0)

        def update(i, upward):
            plane = cells_ref[:, span(i)]
            speed = speed_at(i)
            off_x = speed - mean_x
            along = wide(jnp.exp(off_x * off_x * inverse))
            take_even = on_even == upward
            if side == SF:
                right = side_ref[1, pl.ds(i, 1), :]
                left = side_ref[0, pl.ds(i, 1), :]
                slot = 2 * (i if upward else i - middle)
                ghosts = []
                for half in range(2):
                    a, b = ghost_at(even_ref, slot + half), ghost_at(odd_ref, slot + half)
                    ghosts.append(jnp.where(take_even, a, b))
                ghost = jnp.concatenate(ghosts, axis=1)
            else:
                slot, offset = i // 2, (i % 2) * width
                right = side_ref[1, slot : slot + 1, offset : offset + mid]
                left = side_ref[0, slot : slot + 1, offset + mid : offset + width]
                slot = slot if upward else slot - HALF_C
                a, b = ghost_at(even_ref, slot), ghost_at(odd_ref, slot)
                ghost = jnp.where(take_even, a, b)[:, offset : offset + width]
            if not alone:
                ghost = jnp.where(upper_differs if upward else lower_differs, 0.0, ghost)
            low, high = plane[:, :mid], plane[:, mid:]
            beyond = jnp.where(wide_row == rows_n - 1, right, pltpu.roll(low, rows_n - 1, 0))
            before = jnp.where(wide_row == 0, left, pltpu.roll(high, 1, 0))
            beside = jnp.concatenate([beyond, before], axis=1)
            push = cfl_ratio * jnp.abs(speed)
            done_ref[:, span(i)] = (
                plane * (keep - push) + push * ghost + drift * beside + along * across
            )

        if side == SF:
            each = side // CHUNKS
            for chunk in range(CHUNKS):
                upward = chunk < CHUNKS // 2

                def step(k, carry, chunk=chunk, upward=upward):
                    update(chunk * each + k, upward)
                    return carry

                lax.fori_loop(0, each, step, 0, unroll=4)
                flush(chunk).start()
        else:
            for i in range(side):
                update(i, i < middle)
            flush(0).start()
            done_ref[:, NVC:] = jnp.zeros((rows_n, NVF - NVC), F32)
            for chunk in range(1, CHUNKS):
                flush(chunk).start()

    for k, row_ref in enumerate(row_refs):
        side_ref[k] = row_ref[...].astype(F32)

    @pl.when(own == 1)
    def _():
        run(SF, spacing_fine)

    @pl.when(own != 1)
    def _():
        run(SC, spacing_coarse)

    if not alone:
        base_ref = refs[-4]
        start = jnp.where(upper_differs, 0, 1)

        @pl.when(own == 1)
        def _():
            @pl.when(upper_differs)
            def _():
                base_ref[...] = done_ref[:, : NVF // 2]

            @pl.when(jnp.logical_not(upper_differs))
            def _():
                base_ref[...] = done_ref[:, NVF // 2 :]

        @pl.when(own != 1)
        def _():
            @pl.when(upper_differs)
            def _():
                base_ref[:, : NVC // 2] = done_ref[:, : NVC // 2]

            @pl.when(jnp.logical_not(upper_differs))
            def _():
                base_ref[:, : NVC // 2] = done_ref[:, NVC // 2 : NVC]

    for chunk in range(CHUNKS):
        flush(chunk).wait()


def relax(alone, levels, rate, cells, even, odd, rows):
    out = jax.ShapeDtypeStruct(cells.shape, F32)
    half = jax.ShapeDtypeStruct((cells.shape[0], NVF // 2), F32)
    return pl.pallas_call(
        functools.partial(relax_kernel, alone),
        name="relax",
        out_shape=(out,) if alone else (out, half),
        in_specs=[SMEM, SMEM, VMEM, VMEM, VMEM] + [VMEM] * len(rows),
        out_specs=(HBM,) if alone else (HBM, VMEM),
        scratch_shapes=[
            pltpu.VMEM((2, HALF_F, BLK), F32),
            pltpu.VMEM(cells.shape, F32),
            pltpu.SemaphoreType.DMA((CHUNKS,)),
        ],
        cost_estimate=pl.CostEstimate(flops=10**7, bytes_accessed=4 * 10**6, transcendentals=10**5),
        compiler_params=pltpu.CompilerParams(vmem_limit_bytes=16 << 20),
    )(levels, rate, cells, even, odd, *rows)


def coarse_kernel(level_ref, even_ref, odd_ref, out_ref):
    block, _, lower_differs, _ = place(level_ref)
    use_even = (block % 2 == 0) != lower_differs
    for j in range(VBC):
        a, b = even_ref[j].astype(F32), odd_ref[j].astype(F32)
        out_ref[j] = jnp.where(use_even, a, b).astype(BF16)


def coarse_piece(levels, even, odd):
    return pl.pallas_call(
        coarse_kernel,
        name="coarse_piece",
        out_shape=jax.ShapeDtypeStruct((VBC,) + even.shape[1:], BF16),
        in_specs=[SMEM, VMEM, VMEM],
        out_specs=VMEM,
        cost_estimate=pl.CostEstimate(flops=10**5, bytes_accessed=10**6, transcendentals=0),
        compiler_params=pltpu.CompilerParams(vmem_limit_bytes=8 << 20),
    )(levels, even, odd)


def pieces_kernel(group, level_ref, link_ref, even_ref, odd_ref, *refs):
    out_refs, start_ref = refs[:-1], refs[-1]
    block, own, lower_differs, _ = place(level_ref)
    me = lax.axis_index("gy")
    local = VBF // group
    use_even = (block % 2 == 0) != lower_differs

    def count(h, total):
        start_ref[h] = total
        for j in range(local):
            hit = (link_ref[1, h * local + j] >= HALF_C) == lower_differs
            total = total + hit.astype(jnp.int32)
        return total

    lax.fori_loop(0, group, count, jnp.int32(0))

    def fill(source_ref):
        for s, out_ref in enumerate(out_refs):
            start = start_ref[peer(me, s, group)]
            for j in range(out_ref.shape[0]):
                out_ref[j] = source_ref[jnp.minimum(start + j, HALF_F - 1)]

    @pl.when(use_even)
    def _():
        fill(even_ref)

    @pl.when(jnp.logical_not(use_even))
    def _():
        fill(odd_ref)


def pieces(levels, links, even, odd, group, slots):
    piece = jax.ShapeDtypeStruct((slots,) + even.shape[1:], BF16)
    return pl.pallas_call(
        functools.partial(pieces_kernel, group),
        name="pieces",
        out_shape=(piece,) * group,
        in_specs=[SMEM, SMEM, VMEM, VMEM],
        out_specs=(VMEM,) * group,
        scratch_shapes=[pltpu.SMEM((group,), jnp.int32)],
        cost_estimate=pl.CostEstimate(flops=10**5, bytes_accessed=10**6, transcendentals=0),
        compiler_params=pltpu.CompilerParams(vmem_limit_bytes=8 << 20),
    )(levels, links, even, odd)


def stacked(refs, index):
    return jnp.concatenate([ref[index].astype(F32) for ref in refs], axis=0).astype(BF16)


def to_coarse_kernel(group, level_ref, link_ref, values_ref, *refs):
    in_refs, out_refs, sum_ref = refs[:group], refs[group : 2 * group], refs[-1]
    _, _, lower_differs, _ = place(level_ref)
    local = values_ref.shape[0]
    cells_y = in_refs[0].shape[1]
    first = lax.axis_index("gy") * local
    offset = jnp.where(lower_differs, HALF_C, 0)

    targets = [link_ref[1, first + j] - offset for j in range(local)]
    needed = [(t >= 0) & (t < HALF_C) for t in targets]
    sum_ref[...] = jnp.zeros_like(sum_ref)
    slot = jnp.int32(0)
    for j in range(local):

        @pl.when(needed[j])
        def _(j=j, slot=slot):
            sum_ref[targets[j]] += jnp.dot(
                stacked(in_refs, slot), values_ref[j], preferred_element_type=F32
            )

        slot = slot + needed[j].astype(jnp.int32)
    for s, out_ref in enumerate(out_refs):
        out_ref[...] = sum_ref[:, s * cells_y : (s + 1) * cells_y, :].astype(BF16)


def to_fine_kernel(group, level_ref, link_ref, values_ref, *refs):
    in_refs, out_refs = refs[:group], refs[group : 2 * group]
    _, _, lower_differs, _ = place(level_ref)
    local = values_ref.shape[0]
    cells_y = in_refs[0].shape[1]
    first = lax.axis_index("gy") * local
    active = (first >= HALF_F) == lower_differs

    @pl.when(active)
    def _():
        for j in range(local):
            product = jnp.dot(
                stacked(in_refs, link_ref[0, first + j]),
                values_ref[j],
                preferred_element_type=F32,
            ).astype(BF16)
            for s, out_ref in enumerate(out_refs):
                out_ref[j] = product[s * cells_y : (s + 1) * cells_y, :]


def load_kernel(level_ref, link_ref, values_ref, held_ref, sems):
    _, own, lower_differs, upper_differs = place(level_ref)
    local = values_ref.shape[1]
    first = lax.axis_index("gy") * local
    fine = own == 1
    source = jnp.where(fine, 0, 1)

    def needed(j):
        coarse = (link_ref[1, first + j] >= HALF_C) == lower_differs
        here = jnp.where(fine, (first >= HALF_F) == lower_differs, coarse)
        return here & (lower_differs | upper_differs)

    def copy(j):
        return pltpu.make_async_copy(values_ref.at[source, j], held_ref.at[j], sems.at[j])

    for j in range(local):
        pl.when(needed(j))(lambda j=j: copy(j).start())
    for j in range(local):
        pl.when(needed(j))(lambda j=j: copy(j).wait())


def load(levels, links, values):
    local = values.shape[1]
    return pl.pallas_call(
        load_kernel,
        name="load",
        out_shape=jax.ShapeDtypeStruct(values.shape[1:], BF16),
        in_specs=[SMEM, SMEM, HBM],
        out_specs=VMEM,
        scratch_shapes=[pltpu.SemaphoreType.DMA((local,))],
        cost_estimate=pl.CostEstimate(
            flops=0, bytes_accessed=2 * values.size, transcendentals=0
        ),
        compiler_params=pltpu.CompilerParams(vmem_limit_bytes=40 << 20),
    )(levels, links, values)


def multiply(kernel, levels, links, values, arrived, slots, scratch):
    group = len(arrived)
    local = values.shape[0]
    out = jax.ShapeDtypeStruct((slots,) + arrived[0].shape[1:], BF16)
    return pl.pallas_call(
        functools.partial(kernel, group),
        name=kernel.__name__,
        out_shape=(out,) * group,
        in_specs=[SMEM, SMEM, VMEM] + [VMEM] * group,
        out_specs=(VMEM,) * group,
        scratch_shapes=scratch,
        cost_estimate=pl.CostEstimate(
            flops=2 * local * 32 * BLK * BLK, bytes_accessed=2 * local * BLK * BLK, transcendentals=0
        ),
        compiler_params=pltpu.CompilerParams(vmem_limit_bytes=24 << 20),
    )(levels, links, values, *arrived)


def finish_kernel(role, group, level_ref, base_ref, held_ref, *refs):
    in_refs, out_ref, done_ref, sems = refs[:-3], refs[-3], refs[-2], refs[-1]
    _, _, _, upper_differs = place(level_ref)
    me = lax.axis_index("gy")
    parts = sems.shape[0]
    side, spacing, count = (
        (SC, spacing_coarse, HALF_C) if role == 1 else (SF, spacing_fine, HALF_F)
    )
    whole = count * BLK
    part = whole // parts
    centre = (side - 1) * 0.5

    def flush(index):
        start = index * part + jnp.where(upper_differs, 0, whole)
        at = pl.ds(pl.multiple_of(start, part), part)
        return pltpu.make_async_copy(
            done_ref.at[:, pl.ds(pl.multiple_of(index * part, part), part)],
            out_ref.at[:, at],
            sems.at[index],
        )

    first_plane = jnp.where(upper_differs, 0, side // 2)
    if role == 1:
        width = side * side
        for o in range(HALF_C):
            ghost = in_refs[0][o].astype(F32)
            for ref in in_refs[1:]:
                ghost = ghost + ref[o].astype(F32)
            for k in range(BLK // width):
                plane = lax.convert_element_type(first_plane + o * (BLK // width) + k, F32)
                push = cfl_ratio * spacing * jnp.abs(plane - centre)
                at = slice(o * BLK + k * width, o * BLK + (k + 1) * width)
                done_ref[:, at] = base_ref[:, at] + push * ghost[:, k * width : (k + 1) * width]
        flush(0).start()
        flush(0).wait()
        return

    offset = jnp.where(upper_differs, 0, HALF_F)
    for s, ref in enumerate(in_refs):
        local = ref.shape[0]
        first = peer(me, s, group) * local - offset

        @pl.when((first >= 0) & (first < HALF_F))
        def _(ref=ref, first=first, local=local):
            for j in range(local):
                slot = first + j
                plane = lax.convert_element_type(first_plane + slot // 2, F32)
                push = cfl_ratio * spacing * jnp.abs(plane - centre)
                at = pl.ds(pl.multiple_of(slot * BLK, BLK), BLK)
                done_ref[:, at] = base_ref[:, at] + push * ref[j].astype(F32)
            flush(lax.div(first, local)).start()

    for index in range(parts):
        flush(index).wait()


def finish(role, levels, base, held, arrived):
    group = len(arrived)
    rows_n = base.shape[0]
    parts = 1 if role == 1 else group // 2
    whole = NVC // 2 if role == 1 else NVF // 2
    return pl.pallas_call(
        functools.partial(finish_kernel, role, group),
        name="finish",
        out_shape=jax.ShapeDtypeStruct(held.shape, F32),
        in_specs=[SMEM, VMEM, HBM] + [VMEM] * group,
        out_specs=HBM,
        scratch_shapes=[pltpu.VMEM((rows_n, whole), F32), pltpu.SemaphoreType.DMA((parts,))],
        input_output_aliases={2: 0},
        cost_estimate=pl.CostEstimate(flops=10**6, bytes_accessed=10**6, transcendentals=0),
        compiler_params=pltpu.CompilerParams(vmem_limit_bytes=8 << 20),
    )(levels, base, held, *arrived)


def on_device(distribution, relax_rate, block_level, block_link, remap_values):
    blocks, group = lax.axis_size("gx"), lax.axis_size("gy")
    cells_y = distribution.shape[1]
    local = remap_values.shape[1]
    cells = distribution[0]

    def exchange(value, parity):
        pairs = []
        for low in range(parity, blocks - 1, 2):
            for y in range(group):
                here, there = low * group + y, (low + 1) * group + y
                pairs += [(here, there), (there, here)]
        return lax.ppermute(value, BOTH, pairs)

    everyone = range(group)

    def around(outgoing, sources=everyone, targets=everyone):
        arrived = [outgoing[0]]
        for s in range(1, group):
            pairs = [(i, peer(i, s, group)) for i in sources if peer(i, s, group) in targets]
            arrived.append(lax.ppermute(outgoing[s], "gy", pairs) if pairs else outgoing[0])
        return arrived

    role, even, odd, ahead, back = prepare(block_level, block_link, cells)
    odd = exchange(odd, 1)
    even = exchange(even, 0)
    left = lax.ppermute(ahead, "gy", [(i, i + 1) for i in range(group - 1)])
    right = lax.ppermute(back, "gy", [(i + 1, i) for i in range(group - 1)])
    held = load(block_level, block_link, remap_values)

    def settle(alone):
        return relax(alone, block_level, relax_rate, cells, even, odd, [left, right])

    def alone():
        return settle(True)[0]

    def to_coarse(slots):
        outgoing = pieces(block_level, block_link, even, odd, group, slots)
        arrived = around(outgoing)
        sums = [pltpu.VMEM((HALF_C, group * cells_y, BLK), F32)]
        made = multiply(
            to_coarse_kernel, block_level, block_link, held, arrived, HALF_C, sums
        )
        out, base = settle(False)
        return finish(1, block_level, base, out, around(made))

    def to_fine(active):
        piece = coarse_piece(block_level, even, odd)
        arrived = around([piece] * group, targets=active)
        made = multiply(to_fine_kernel, block_level, block_link, held, arrived, local, [])
        out, base = settle(False)
        return finish(2, block_level, base, out, around(made, sources=active))

    updated = lax.switch(
        role[0],
        [
            alone,
            lambda: to_coarse(few(local)),
            lambda: to_coarse(local),
            lambda: to_fine(range(group // 2, group)),
            lambda: to_fine(range(group // 2)),
        ],
    )
    return updated[None]


def solution(mesh):
    in_specs = (P("gx", "gy", None), P("gx", "gy"), P(), P(), P(None, "gy", None, None))
    out_specs = P("gx", "gy", None)
    return jax.shard_map(
        on_device, mesh=mesh, in_specs=in_specs, out_specs=out_specs, check_vma=False
    )
```

```python
import functools
import math

import jax
import jax.numpy as jnp
from jax import lax
from jax.experimental import pallas as pl
from jax.experimental.pallas import tpu as pltpu
from jax.sharding import PartitionSpec as P

SC = 16
SF = 32
BLK = 512
NVC = 4096
NVF = 32768
VBC = NVC // BLK
VBF = NVF // BLK
HALF_F = VBF // 2
HALF_C = VBC // 2

cfl_ratio = 0.03
spacing_coarse = 0.5
spacing_fine = 0.4

BOTH = ("gx", "gy")
SMEM = pl.BlockSpec(memory_space=pltpu.SMEM)
VMEM = pl.BlockSpec(memory_space=pltpu.VMEM)
HBM = pl.BlockSpec(memory_space=pltpu.HBM)
F32 = jnp.float32
BF16 = jnp.bfloat16


def place(level_ref):
    block = lax.axis_index("gx")
    own = level_ref[block]
    lower = level_ref[jnp.maximum(block - 1, 0)]
    upper = level_ref[jnp.minimum(block + 1, level_ref.shape[0] - 1)]
    return block, own, lower != own, upper != own


def peer(me, step, group):
    if group & (group - 1):
        raise ValueError(group)
    return me ^ step


def order(group):
    return sorted(range(group), key=lambda s: (s == 1, s))


def few(local):
    return max(1, (3 * local) // 4)


def block_at(ref, index):
    return ref[:, pl.ds(pl.multiple_of(index * BLK, BLK), BLK)]


def prepare_kernel(level_ref, link_ref, cells_ref, even_ref, odd_ref, index_ref):
    block, own, lower_differs, upper_differs = place(level_ref)
    fine = own == 1

    def fill(target_ref, going_up):
        differs = jnp.where(going_up, upper_differs, lower_differs)
        gathers = differs & fine

        @pl.when(gathers)
        def _():
            def look(f, count):
                index_ref[count] = f
                hit = (link_ref[1, f] >= HALF_C) == going_up
                return count + hit.astype(jnp.int32)

            lax.fori_loop(0, VBF, look, jnp.int32(0), unroll=8)

            def copy(j, carry):
                target_ref[j] = block_at(cells_ref, index_ref[j]).astype(BF16)
                return carry

            lax.fori_loop(0, HALF_F, copy, 0, unroll=8)

        @pl.when(fine & jnp.logical_not(differs))
        def _():
            start = jnp.where(going_up, HALF_F, 0)
            for j in range(HALF_F):
                target_ref[j] = block_at(cells_ref, start + j).astype(BF16)

        @pl.when(jnp.logical_not(fine))
        def _():
            start = jnp.where(going_up & jnp.logical_not(differs), HALF_C, 0)
            for j in range(VBC):
                target_ref[j] = block_at(cells_ref, start + j).astype(BF16)

    on_even = block % 2 == 0
    fill(odd_ref, jnp.logical_not(on_even))
    fill(even_ref, on_even)


def prepare(levels, links, cells):
    half = jax.ShapeDtypeStruct((HALF_F, cells.shape[0], BLK), BF16)
    return pl.pallas_call(
        prepare_kernel,
        name="prepare",
        out_shape=(half, half),
        in_specs=[SMEM, SMEM, VMEM],
        out_specs=(VMEM,) * 2,
        scratch_shapes=[pltpu.SMEM((VBF + 1,), jnp.int32)],
        cost_estimate=pl.CostEstimate(flops=10**6, bytes_accessed=2 * 10**6, transcendentals=0),
        compiler_params=pltpu.CompilerParams(vmem_limit_bytes=8 << 20),
    )(levels, links, cells)


def rows_kernel(level_ref, cells_ref, ahead_ref, back_ref, row_ref):
    _, own, _, _ = place(level_ref)
    cells_y = cells_ref.shape[0]

    def rows(target_ref, row, parity):
        @pl.when(own == 1)
        def _():
            for i in range(HALF_F):
                row_ref[i : i + 1, :] = cells_ref[
                    row : row + 1, (2 * i + parity) * BLK : (2 * i + parity + 1) * BLK
                ]

        @pl.when(own != 1)
        def _():
            for i in range(VBC):
                row_ref[i : i + 1, :] = cells_ref[row : row + 1, i * BLK : (i + 1) * BLK]

        target_ref[...] = row_ref[...].astype(BF16)

    rows(ahead_ref, cells_y - 1, 1)
    rows(back_ref, 0, 0)


def edge_rows(levels, cells):
    row = jax.ShapeDtypeStruct((HALF_F, BLK), BF16)
    return pl.pallas_call(
        rows_kernel,
        name="edge_rows",
        out_shape=(row, row),
        in_specs=[SMEM, VMEM],
        out_specs=(VMEM, VMEM),
        scratch_shapes=[pltpu.VMEM((HALF_F, BLK), F32)],
        cost_estimate=pl.CostEstimate(flops=10**6, bytes_accessed=2 * 10**6, transcendentals=0),
        compiler_params=pltpu.CompilerParams(vmem_limit_bytes=8 << 20),
    )(levels, cells)


CHUNKS = 8
PART = NVF // CHUNKS


def ghost_at(ref, index):
    return ref[index].astype(F32)


def relax_kernel(
    alone,
    level_ref,
    rate_ref,
    cells_ref,
    even_ref,
    odd_ref,
    *refs,
):
    side_ref, done_ref, sems = refs[-3:]
    results = 1 if alone else 2
    row_refs, out_ref = refs[: -3 - results], refs[-3 - results]
    block, own, lower_differs, upper_differs = place(level_ref)
    on_even = block % 2 == 0
    rows_n = cells_ref.shape[0]

    def flush(chunk):
        at = pl.ds(chunk * PART, PART)
        return pltpu.make_async_copy(done_ref.at[:, at], out_ref.at[:, at], sems.at[chunk])

    def run(side, spacing):
        width = side * side
        mid = width // 2
        middle = side // 2
        centre = (side - 1) * 0.5
        lane = lax.broadcasted_iota(jnp.int32, (rows_n, width), 1)
        along_y = spacing * ((lane // side).astype(F32) - centre)
        along_z = spacing * ((lane % side).astype(F32) - centre)

        def span(i):
            start = i * width
            return pl.ds(start if isinstance(i, int) else pl.multiple_of(start, width), width)

        def speed_at(i):
            return spacing * (lax.convert_element_type(i, F32) - centre)

        def gather(i, sums):
            total, first, second = sums
            plane = cells_ref[:, span(i)]
            speed = speed_at(i)
            return total + plane, first + plane * speed, second + plane * (speed * speed)

        zero = jnp.zeros((rows_n, width), F32)
        total, first, second = lax.fori_loop(0, side, gather, (zero, zero, zero), unroll=4)

        def over(value):
            return jnp.broadcast_to(jnp.sum(value, axis=1, keepdims=True), (rows_n, 128))

        weight = spacing * spacing * spacing
        density = weight * over(total)
        scale = weight / density
        mean_x = scale * over(first)
        mean_y = scale * over(total * along_y)
        mean_z = scale * over(total * along_z)
        square = scale * over(second + total * (along_y * along_y + along_z * along_z))
        heat = (square - mean_x * mean_x - mean_y * mean_y - mean_z * mean_z) / 3.0
        row = lax.broadcasted_iota(jnp.int32, (rows_n, 128), 0)
        rate = jnp.zeros((rows_n, 128), F32)
        for r in range(rows_n):
            rate = jnp.where(row == r, rate_ref[0, r], rate)
        spread = 2.0 * math.pi * heat
        peak = rate * density / (spread * jnp.sqrt(spread))
        inverse = -0.5 / heat

        def wide(value):
            return jnp.concatenate([value] * (width // 128), axis=1)

        off_y = along_y - wide(mean_y)
        off_z = along_z - wide(mean_z)
        across = wide(peak) * jnp.exp((off_y * off_y + off_z * off_z) * wide(inverse))
        drift = cfl_ratio * jnp.abs(along_y)
        keep = (1.0 - wide(rate)) - drift
        wide_row = lax.broadcasted_iota(jnp.int32, (rows_n, mid), 0)

        def update(i, upward):
            plane = cells_ref[:, span(i)]
            speed = speed_at(i)
            off_x = speed - mean_x
            along = wide(jnp.exp(off_x * off_x * inverse))
            take_even = on_even == upward
            if side == SF:
                right = side_ref[1, pl.ds(i, 1), :]
                left = side_ref[0, pl.ds(i, 1), :]
                slot = 2 * (i if upward else i - middle)
                ghosts = []
                for half in range(2):
                    a, b = ghost_at(even_ref, slot + half), ghost_at(odd_ref, slot + half)
                    ghosts.append(jnp.where(take_even, a, b))
                ghost = jnp.concatenate(ghosts, axis=1)
            else:
                slot, offset = i // 2, (i % 2) * width
                right = side_ref[1, slot : slot + 1, offset : offset + mid]
                left = side_ref[0, slot : slot + 1, offset + mid : offset + width]
                slot = slot if upward else slot - HALF_C
                a, b = ghost_at(even_ref, slot), ghost_at(odd_ref, slot)
                ghost = jnp.where(take_even, a, b)[:, offset : offset + width]
            if not alone:
                ghost = jnp.where(upper_differs if upward else lower_differs, 0.0, ghost)
            low, high = plane[:, :mid], plane[:, mid:]
            beyond = jnp.where(wide_row == rows_n - 1, right, pltpu.roll(low, rows_n - 1, 0))
            before = jnp.where(wide_row == 0, left, pltpu.roll(high, 1, 0))
            beside = jnp.concatenate([beyond, before], axis=1)
            push = cfl_ratio * jnp.abs(speed)
            done_ref[:, span(i)] = (
                plane * (keep - push) + push * ghost + drift * beside + along * across
            )

        if side == SF:
            each = side // CHUNKS
            for chunk in range(CHUNKS):
                upward = chunk < CHUNKS // 2

                def step(k, carry, chunk=chunk, upward=upward):
                    update(chunk * each + k, upward)
                    return carry

                lax.fori_loop(0, each, step, 0, unroll=4)
                flush(chunk).start()
        else:
            for i in range(side):
                update(i, i < middle)
            flush(0).start()
            done_ref[:, NVC:] = jnp.zeros((rows_n, NVF - NVC), F32)
            for chunk in range(1, CHUNKS):
                flush(chunk).start()

    for k, row_ref in enumerate(row_refs):
        side_ref[k] = row_ref[...].astype(F32)

    @pl.when(own == 1)
    def _():
        run(SF, spacing_fine)

    @pl.when(own != 1)
    def _():
        run(SC, spacing_coarse)

    if not alone:
        base_ref = refs[-4]
        start = jnp.where(upper_differs, 0, 1)

        @pl.when(own == 1)
        def _():
            @pl.when(upper_differs)
            def _():
                base_ref[...] = done_ref[:, : NVF // 2]

            @pl.when(jnp.logical_not(upper_differs))
            def _():
                base_ref[...] = done_ref[:, NVF // 2 :]

        @pl.when(own != 1)
        def _():
            @pl.when(upper_differs)
            def _():
                base_ref[:, : NVC // 2] = done_ref[:, : NVC // 2]

            @pl.when(jnp.logical_not(upper_differs))
            def _():
                base_ref[:, : NVC // 2] = done_ref[:, NVC // 2 : NVC]

    for chunk in range(CHUNKS):
        flush(chunk).wait()


def relax(alone, levels, rate, cells, even, odd, rows):
    out = jax.ShapeDtypeStruct(cells.shape, F32)
    half = jax.ShapeDtypeStruct((cells.shape[0], NVF // 2), F32)
    return pl.pallas_call(
        functools.partial(relax_kernel, alone),
        name="relax",
        out_shape=(out,) if alone else (out, half),
        in_specs=[SMEM, SMEM, VMEM, VMEM, VMEM] + [VMEM] * len(rows),
        out_specs=(HBM,) if alone else (HBM, VMEM),
        scratch_shapes=[
            pltpu.VMEM((2, HALF_F, BLK), F32),
            pltpu.VMEM(cells.shape, F32),
            pltpu.SemaphoreType.DMA((CHUNKS,)),
        ],
        cost_estimate=pl.CostEstimate(flops=10**7, bytes_accessed=4 * 10**6, transcendentals=10**5),
        compiler_params=pltpu.CompilerParams(vmem_limit_bytes=16 << 20),
    )(levels, rate, cells, even, odd, *rows)


def coarse_kernel(level_ref, even_ref, odd_ref, *out_refs):
    block, _, lower_differs, _ = place(level_ref)
    use_even = (block % 2 == 0) != lower_differs
    for j in range(VBC):
        a, b = even_ref[j].astype(F32), odd_ref[j].astype(F32)
        piece = jnp.where(use_even, a, b).astype(BF16)
        for out_ref in out_refs:
            out_ref[j] = piece


def coarse_pieces(levels, even, odd, group):
    piece = jax.ShapeDtypeStruct((VBC,) + even.shape[1:], BF16)
    return pl.pallas_call(
        coarse_kernel,
        name="coarse_pieces",
        out_shape=(piece,) * group,
        in_specs=[SMEM, VMEM, VMEM],
        out_specs=(VMEM,) * group,
        cost_estimate=pl.CostEstimate(flops=10**5, bytes_accessed=10**6, transcendentals=0),
        compiler_params=pltpu.CompilerParams(vmem_limit_bytes=8 << 20),
    )(levels, even, odd)


def pieces_kernel(group, level_ref, link_ref, even_ref, odd_ref, *refs):
    out_refs, start_ref = refs[:-1], refs[-1]
    block, own, lower_differs, _ = place(level_ref)
    me = lax.axis_index("gy")
    local = VBF // group
    use_even = (block % 2 == 0) != lower_differs

    def count(h, total):
        start_ref[h] = total
        for j in range(local):
            hit = (link_ref[1, h * local + j] >= HALF_C) == lower_differs
            total = total + hit.astype(jnp.int32)
        return total

    lax.fori_loop(0, group, count, jnp.int32(0))

    def fill(source_ref):
        for s, out_ref in zip(order(group), out_refs):
            start = start_ref[peer(me, s, group)]
            for j in range(out_ref.shape[0]):
                out_ref[j] = source_ref[jnp.minimum(start + j, HALF_F - 1)]

    @pl.when(use_even)
    def _():
        fill(even_ref)

    @pl.when(jnp.logical_not(use_even))
    def _():
        fill(odd_ref)


def pieces(levels, links, even, odd, group, slots):
    piece = jax.ShapeDtypeStruct((slots,) + even.shape[1:], BF16)
    return pl.pallas_call(
        functools.partial(pieces_kernel, group),
        name="pieces",
        out_shape=(piece,) * group,
        in_specs=[SMEM, SMEM, VMEM, VMEM],
        out_specs=(VMEM,) * group,
        scratch_shapes=[pltpu.SMEM((group,), jnp.int32)],
        cost_estimate=pl.CostEstimate(flops=10**5, bytes_accessed=10**6, transcendentals=0),
        compiler_params=pltpu.CompilerParams(vmem_limit_bytes=8 << 20),
    )(levels, links, even, odd)


def stacked(refs, index):
    return jnp.concatenate([ref[index].astype(F32) for ref in refs], axis=0).astype(BF16)


def to_coarse_kernel(group, level_ref, link_ref, values_ref, *refs):
    in_refs, out_refs, sum_ref = refs[:group], refs[group : 2 * group], refs[-1]
    _, _, lower_differs, _ = place(level_ref)
    local = values_ref.shape[0]
    cells_y = in_refs[0].shape[1]
    first = lax.axis_index("gy") * local
    offset = jnp.where(lower_differs, HALF_C, 0)

    targets = [link_ref[1, first + j] - offset for j in range(local)]
    needed = [(t >= 0) & (t < HALF_C) for t in targets]
    sum_ref[...] = jnp.zeros_like(sum_ref)
    slot = jnp.int32(0)
    for j in range(local):

        @pl.when(needed[j])
        def _(j=j, slot=slot):
            sum_ref[targets[j]] += jnp.dot(
                stacked(in_refs, slot), values_ref[j], preferred_element_type=F32
            )

        slot = slot + needed[j].astype(jnp.int32)
    for s, out_ref in enumerate(out_refs):
        out_ref[...] = sum_ref[:, s * cells_y : (s + 1) * cells_y, :].astype(BF16)


def to_fine_kernel(group, level_ref, link_ref, values_ref, *refs):
    in_refs, out_refs = refs[:group], refs[group : 2 * group]
    _, _, lower_differs, _ = place(level_ref)
    local = values_ref.shape[0]
    cells_y = in_refs[0].shape[1]
    first = lax.axis_index("gy") * local
    active = (first >= HALF_F) == lower_differs

    @pl.when(active)
    def _():
        for j in range(local):
            product = jnp.dot(
                stacked(in_refs, link_ref[0, first + j]),
                values_ref[j],
                preferred_element_type=F32,
            ).astype(BF16)
            for s, out_ref in enumerate(out_refs):
                out_ref[j] = product[s * cells_y : (s + 1) * cells_y, :]


def load_kernel(level_ref, link_ref, values_ref, role_ref, held_ref, sems):
    _, own, lower_differs, upper_differs = place(level_ref)
    local = values_ref.shape[1]
    first = lax.axis_index("gy") * local
    fine = own == 1
    source = jnp.where(fine, 0, 1)

    def needed(j):
        coarse = (link_ref[1, first + j] >= HALF_C) == lower_differs
        here = jnp.where(fine, (first >= HALF_F) == lower_differs, coarse)
        return here & (lower_differs | upper_differs)

    def copy(j):
        return pltpu.make_async_copy(values_ref.at[source, j], held_ref.at[j], sems.at[j])

    for j in range(local):
        pl.when(needed(j))(lambda j=j: copy(j).start())

    def most(h, worst):
        count = jnp.int32(0)
        for j in range(local):
            hit = (link_ref[1, h * local + j] >= HALF_C) == lower_differs
            count = count + hit.astype(jnp.int32)
        return jnp.maximum(worst, count)

    worst = lax.fori_loop(0, VBF // local, most, jnp.int32(0))
    coarse_role = jnp.where(worst > few(local), 2, 1)
    role = jnp.where(fine, jnp.where(lower_differs, 3, 4), coarse_role)
    role_ref[0] = jnp.where(lower_differs | upper_differs, role, 0)
    for j in range(local):
        pl.when(needed(j))(lambda j=j: copy(j).wait())


def load(levels, links, values):
    local = values.shape[1]
    return pl.pallas_call(
        load_kernel,
        name="load",
        out_shape=(
            jax.ShapeDtypeStruct((1,), jnp.int32),
            jax.ShapeDtypeStruct(values.shape[1:], BF16),
        ),
        in_specs=[SMEM, SMEM, HBM],
        out_specs=(SMEM, VMEM),
        scratch_shapes=[pltpu.SemaphoreType.DMA((local,))],
        cost_estimate=pl.CostEstimate(
            flops=0, bytes_accessed=2 * values.size, transcendentals=0
        ),
        compiler_params=pltpu.CompilerParams(vmem_limit_bytes=40 << 20),
    )(levels, links, values)


def multiply(kernel, levels, links, values, arrived, slots, scratch):
    group = len(arrived)
    local = values.shape[0]
    out = jax.ShapeDtypeStruct((slots,) + arrived[0].shape[1:], BF16)
    return pl.pallas_call(
        functools.partial(kernel, group),
        name=kernel.__name__,
        out_shape=(out,) * group,
        in_specs=[SMEM, SMEM, VMEM] + [VMEM] * group,
        out_specs=(VMEM,) * group,
        scratch_shapes=scratch,
        cost_estimate=pl.CostEstimate(
            flops=2 * local * 32 * BLK * BLK, bytes_accessed=2 * local * BLK * BLK, transcendentals=0
        ),
        compiler_params=pltpu.CompilerParams(vmem_limit_bytes=24 << 20),
    )(levels, links, values, *arrived)


def finish_kernel(role, group, level_ref, base_ref, held_ref, *refs):
    in_refs, out_ref, done_ref, sems = refs[:-3], refs[-3], refs[-2], refs[-1]
    _, _, _, upper_differs = place(level_ref)
    me = lax.axis_index("gy")
    parts = sems.shape[0]
    side, spacing, count = (
        (SC, spacing_coarse, HALF_C) if role == 1 else (SF, spacing_fine, HALF_F)
    )
    whole = count * BLK
    part = whole // parts
    centre = (side - 1) * 0.5

    def flush(index):
        start = index * part + jnp.where(upper_differs, 0, whole)
        at = pl.ds(pl.multiple_of(start, part), part)
        return pltpu.make_async_copy(
            done_ref.at[:, pl.ds(pl.multiple_of(index * part, part), part)],
            out_ref.at[:, at],
            sems.at[index],
        )

    first_plane = jnp.where(upper_differs, 0, side // 2)
    if role == 1:
        width = side * side
        for o in range(HALF_C):
            ghost = in_refs[0][o].astype(F32)
            for ref in in_refs[1:]:
                ghost = ghost + ref[o].astype(F32)
            for k in range(BLK // width):
                plane = lax.convert_element_type(first_plane + o * (BLK // width) + k, F32)
                push = cfl_ratio * spacing * jnp.abs(plane - centre)
                at = slice(o * BLK + k * width, o * BLK + (k + 1) * width)
                done_ref[:, at] = base_ref[:, at] + push * ghost[:, k * width : (k + 1) * width]
        flush(0).start()
        flush(0).wait()
        return

    offset = jnp.where(upper_differs, 0, HALF_F)
    for s, ref in zip(order(group), in_refs):
        local = ref.shape[0]
        first = peer(me, s, group) * local - offset

        @pl.when((first >= 0) & (first < HALF_F))
        def _(ref=ref, first=first, local=local):
            for j in range(local):
                slot = first + j
                plane = lax.convert_element_type(first_plane + slot // 2, F32)
                push = cfl_ratio * spacing * jnp.abs(plane - centre)
                at = pl.ds(pl.multiple_of(slot * BLK, BLK), BLK)
                done_ref[:, at] = base_ref[:, at] + push * ref[j].astype(F32)
            flush(lax.div(first, local)).start()

    for index in range(parts):
        flush(index).wait()


def finish(role, levels, base, held, arrived):
    group = len(arrived)
    rows_n = base.shape[0]
    parts = 1 if role == 1 else group // 2
    whole = NVC // 2 if role == 1 else NVF // 2
    return pl.pallas_call(
        functools.partial(finish_kernel, role, group),
        name="finish",
        out_shape=jax.ShapeDtypeStruct(held.shape, F32),
        in_specs=[SMEM, VMEM, HBM] + [VMEM] * group,
        out_specs=HBM,
        scratch_shapes=[pltpu.VMEM((rows_n, whole), F32), pltpu.SemaphoreType.DMA((parts,))],
        input_output_aliases={2: 0},
        cost_estimate=pl.CostEstimate(flops=10**6, bytes_accessed=10**6, transcendentals=0),
        compiler_params=pltpu.CompilerParams(vmem_limit_bytes=8 << 20),
    )(levels, base, held, *arrived)


def on_device(distribution, relax_rate, block_level, block_link, remap_values):
    blocks, group = lax.axis_size("gx"), lax.axis_size("gy")
    cells_y = distribution.shape[1]
    local = remap_values.shape[1]
    cells = distribution[0]

    def exchange(value, parity):
        pairs = []
        for low in range(parity, blocks - 1, 2):
            for y in range(group):
                here, there = low * group + y, (low + 1) * group + y
                pairs += [(here, there), (there, here)]
        return lax.ppermute(value, BOTH, pairs)

    everyone = range(group)

    def around(outgoing, sources=everyone, targets=everyone):
        arrived = []
        for s, value in zip(order(group), outgoing):
            pairs = [(i, peer(i, s, group)) for i in sources if peer(i, s, group) in targets]
            arrived.append(lax.ppermute(value, "gy", pairs) if s and pairs else value)
        return arrived

    even, odd = prepare(block_level, block_link, cells)
    odd = exchange(odd, 1)
    even = exchange(even, 0)
    role, held = load(block_level, block_link, remap_values)
    ahead, back = edge_rows(block_level, cells)

    def sides():
        left = lax.ppermute(ahead, "gy", [(i, i + 1) for i in range(group - 1)])
        right = lax.ppermute(back, "gy", [(i + 1, i) for i in range(group - 1)])
        return left, right

    def settle(alone, rows):
        return relax(alone, block_level, relax_rate, cells, even, odd, rows)

    def alone():
        return settle(True, sides())[0]

    def remapped(role, kernel, slots, scratch, arrived):
        arrived, rows = lax.optimization_barrier((arrived, sides()))
        made = multiply(kernel, block_level, block_link, held, arrived, slots, scratch)
        return made, settle(False, rows)

    def to_coarse(slots):
        outgoing = pieces(block_level, block_link, even, odd, group, slots)
        sums = [pltpu.VMEM((HALF_C, group * cells_y, BLK), F32)]
        made, (out, base) = remapped(1, to_coarse_kernel, HALF_C, sums, around(outgoing))
        return finish(1, block_level, base, out, around(made))

    def to_fine(active):
        outgoing = coarse_pieces(block_level, even, odd, group)
        arrived = around(outgoing, targets=active)
        made, (out, base) = remapped(2, to_fine_kernel, local, [], arrived)
        return finish(2, block_level, base, out, around(made, sources=active))

    updated = lax.switch(
        role[0],
        [
            alone,
            lambda: to_coarse(few(local)),
            lambda: to_coarse(local),
            lambda: to_fine(range(group // 2, group)),
            lambda: to_fine(range(group // 2)),
        ],
    )
    return updated[None]


def solution(mesh):
    in_specs = (P("gx", "gy", None), P("gx", "gy"), P(), P(), P(None, "gy", None, None))
    out_specs = P("gx", "gy", None)
    return jax.shard_map(
        on_device, mesh=mesh, in_specs=in_specs, out_specs=out_specs, check_vma=False
    )
```

```python
import functools
import math

import jax
import jax.numpy as jnp
from jax import lax
from jax.experimental import pallas as pl
from jax.experimental.pallas import tpu as pltpu
from jax.sharding import PartitionSpec as P

SC = 16
SF = 32
BLK = 512
NVC = 4096
NVF = 32768
VBC = NVC // BLK
VBF = NVF // BLK
HALF_F = VBF // 2
HALF_C = VBC // 2

cfl_ratio = 0.03
spacing_coarse = 0.5
spacing_fine = 0.4

BOTH = ("gx", "gy")
SMEM = pl.BlockSpec(memory_space=pltpu.SMEM)
VMEM = pl.BlockSpec(memory_space=pltpu.VMEM)
HBM = pl.BlockSpec(memory_space=pltpu.HBM)
F32 = jnp.float32
BF16 = jnp.bfloat16


def place(level_ref):
    block = lax.axis_index("gx")
    own = level_ref[block]
    lower = level_ref[jnp.maximum(block - 1, 0)]
    upper = level_ref[jnp.minimum(block + 1, level_ref.shape[0] - 1)]
    return block, own, lower != own, upper != own


def peer(me, step, group):
    if group & (group - 1):
        raise ValueError(group)
    return me ^ step


def order(group):
    return sorted(range(group), key=lambda s: (s == 1, s))


def near(group):
    return [s for s in order(group) if s and not s & (s + 1)]


def few(local):
    return max(1, (3 * local) // 4)


def block_at(ref, index):
    return ref[:, pl.ds(pl.multiple_of(index * BLK, BLK), BLK)]


def prepare_kernel(level_ref, link_ref, cells_ref, even_ref, odd_ref, index_ref):
    block, own, lower_differs, upper_differs = place(level_ref)
    fine = own == 1

    def fill(target_ref, going_up):
        differs = jnp.where(going_up, upper_differs, lower_differs)
        gathers = differs & fine

        @pl.when(gathers)
        def _():
            def look(f, count):
                index_ref[count] = f
                hit = (link_ref[1, f] >= HALF_C) == going_up
                return count + hit.astype(jnp.int32)

            lax.fori_loop(0, VBF, look, jnp.int32(0), unroll=8)

            def copy(j, carry):
                target_ref[j] = block_at(cells_ref, index_ref[j]).astype(BF16)
                return carry

            lax.fori_loop(0, HALF_F, copy, 0, unroll=8)

        @pl.when(fine & jnp.logical_not(differs))
        def _():
            start = jnp.where(going_up, HALF_F, 0)
            for j in range(HALF_F):
                target_ref[j] = block_at(cells_ref, start + j).astype(BF16)

        @pl.when(jnp.logical_not(fine))
        def _():
            start = jnp.where(going_up & jnp.logical_not(differs), HALF_C, 0)
            for j in range(VBC):
                target_ref[j] = block_at(cells_ref, start + j).astype(BF16)

    on_even = block % 2 == 0
    fill(odd_ref, jnp.logical_not(on_even))
    fill(even_ref, on_even)


def prepare(levels, links, cells):
    half = jax.ShapeDtypeStruct((HALF_F, cells.shape[0], BLK), BF16)
    return pl.pallas_call(
        prepare_kernel,
        name="prepare",
        out_shape=(half, half),
        in_specs=[SMEM, SMEM, VMEM],
        out_specs=(VMEM,) * 2,
        scratch_shapes=[pltpu.SMEM((VBF + 1,), jnp.int32)],
        cost_estimate=pl.CostEstimate(flops=10**6, bytes_accessed=2 * 10**6, transcendentals=0),
        compiler_params=pltpu.CompilerParams(vmem_limit_bytes=8 << 20),
    )(levels, links, cells)


def rows_kernel(level_ref, cells_ref, ahead_ref, back_ref, row_ref):
    _, own, _, _ = place(level_ref)
    cells_y = cells_ref.shape[0]

    def rows(target_ref, row, parity):
        @pl.when(own == 1)
        def _():
            for i in range(HALF_F):
                row_ref[i : i + 1, :] = cells_ref[
                    row : row + 1, (2 * i + parity) * BLK : (2 * i + parity + 1) * BLK
                ]

        @pl.when(own != 1)
        def _():
            for i in range(VBC):
                row_ref[i : i + 1, :] = cells_ref[row : row + 1, i * BLK : (i + 1) * BLK]

        target_ref[...] = row_ref[...].astype(BF16)

    rows(ahead_ref, cells_y - 1, 1)
    rows(back_ref, 0, 0)


def edge_rows(levels, cells):
    row = jax.ShapeDtypeStruct((HALF_F, BLK), BF16)
    return pl.pallas_call(
        rows_kernel,
        name="edge_rows",
        out_shape=(row, row),
        in_specs=[SMEM, VMEM],
        out_specs=(VMEM, VMEM),
        scratch_shapes=[pltpu.VMEM((HALF_F, BLK), F32)],
        cost_estimate=pl.CostEstimate(flops=10**6, bytes_accessed=2 * 10**6, transcendentals=0),
        compiler_params=pltpu.CompilerParams(vmem_limit_bytes=8 << 20),
    )(levels, cells)


CHUNKS = 8
PART = NVF // CHUNKS


def ghost_at(ref, index):
    return ref[index].astype(F32)


def relax_kernel(
    alone,
    level_ref,
    rate_ref,
    cells_ref,
    even_ref,
    odd_ref,
    *refs,
):
    side_ref, done_ref, sems = refs[-3:]
    results = 1 if alone else 2
    row_refs, out_ref = refs[: -3 - results], refs[-3 - results]
    block, own, lower_differs, upper_differs = place(level_ref)
    on_even = block % 2 == 0
    rows_n = cells_ref.shape[0]

    def flush(chunk):
        at = pl.ds(chunk * PART, PART)
        return pltpu.make_async_copy(done_ref.at[:, at], out_ref.at[:, at], sems.at[chunk])

    def run(side, spacing):
        width = side * side
        mid = width // 2
        middle = side // 2
        centre = (side - 1) * 0.5
        lane = lax.broadcasted_iota(jnp.int32, (rows_n, width), 1)
        along_y = spacing * ((lane // side).astype(F32) - centre)
        along_z = spacing * ((lane % side).astype(F32) - centre)

        def span(i):
            start = i * width
            return pl.ds(start if isinstance(i, int) else pl.multiple_of(start, width), width)

        def speed_at(i):
            return spacing * (lax.convert_element_type(i, F32) - centre)

        def gather(i, sums):
            total, first, second = sums
            plane = cells_ref[:, span(i)]
            speed = speed_at(i)
            return total + plane, first + plane * speed, second + plane * (speed * speed)

        zero = jnp.zeros((rows_n, width), F32)
        total, first, second = lax.fori_loop(0, side, gather, (zero, zero, zero), unroll=4)

        def over(value):
            return jnp.broadcast_to(jnp.sum(value, axis=1, keepdims=True), (rows_n, 128))

        weight = spacing * spacing * spacing
        density = weight * over(total)
        scale = weight / density
        mean_x = scale * over(first)
        mean_y = scale * over(total * along_y)
        mean_z = scale * over(total * along_z)
        square = scale * over(second + total * (along_y * along_y + along_z * along_z))
        heat = (square - mean_x * mean_x - mean_y * mean_y - mean_z * mean_z) / 3.0
        row = lax.broadcasted_iota(jnp.int32, (rows_n, 128), 0)
        rate = jnp.zeros((rows_n, 128), F32)
        for r in range(rows_n):
            rate = jnp.where(row == r, rate_ref[0, r], rate)
        spread = 2.0 * math.pi * heat
        peak = rate * density / (spread * jnp.sqrt(spread))
        inverse = -0.5 / heat

        def wide(value):
            return jnp.concatenate([value] * (width // 128), axis=1)

        off_y = along_y - wide(mean_y)
        off_z = along_z - wide(mean_z)
        across = wide(peak) * jnp.exp((off_y * off_y + off_z * off_z) * wide(inverse))
        drift = cfl_ratio * jnp.abs(along_y)
        keep = (1.0 - wide(rate)) - drift
        wide_row = lax.broadcasted_iota(jnp.int32, (rows_n, mid), 0)

        def update(i, upward):
            plane = cells_ref[:, span(i)]
            speed = speed_at(i)
            off_x = speed - mean_x
            along = wide(jnp.exp(off_x * off_x * inverse))
            take_even = on_even == upward
            if side == SF:
                right = side_ref[1, pl.ds(i, 1), :]
                left = side_ref[0, pl.ds(i, 1), :]
                slot = 2 * (i if upward else i - middle)
                ghosts = []
                for half in range(2):
                    a, b = ghost_at(even_ref, slot + half), ghost_at(odd_ref, slot + half)
                    ghosts.append(jnp.where(take_even, a, b))
                ghost = jnp.concatenate(ghosts, axis=1)
            else:
                slot, offset = i // 2, (i % 2) * width
                right = side_ref[1, slot : slot + 1, offset : offset + mid]
                left = side_ref[0, slot : slot + 1, offset + mid : offset + width]
                slot = slot if upward else slot - HALF_C
                a, b = ghost_at(even_ref, slot), ghost_at(odd_ref, slot)
                ghost = jnp.where(take_even, a, b)[:, offset : offset + width]
            if not alone:
                ghost = jnp.where(upper_differs if upward else lower_differs, 0.0, ghost)
            low, high = plane[:, :mid], plane[:, mid:]
            beyond = jnp.where(wide_row == rows_n - 1, right, pltpu.roll(low, rows_n - 1, 0))
            before = jnp.where(wide_row == 0, left, pltpu.roll(high, 1, 0))
            beside = jnp.concatenate([beyond, before], axis=1)
            push = cfl_ratio * jnp.abs(speed)
            done_ref[:, span(i)] = (
                plane * (keep - push) + push * ghost + drift * beside + along * across
            )

        if side == SF:
            each = side // CHUNKS
            for chunk in range(CHUNKS):
                upward = chunk < CHUNKS // 2

                def step(k, carry, chunk=chunk, upward=upward):
                    update(chunk * each + k, upward)
                    return carry

                lax.fori_loop(0, each, step, 0, unroll=4)
                flush(chunk).start()
        else:
            for i in range(side):
                update(i, i < middle)
            flush(0).start()
            done_ref[:, NVC:] = jnp.zeros((rows_n, NVF - NVC), F32)
            for chunk in range(1, CHUNKS):
                flush(chunk).start()

    if alone:
        for k, row_ref in enumerate(row_refs):
            side_ref[k] = row_ref[...].astype(F32)
    else:
        side_ref[...] = jnp.zeros_like(side_ref)
        me, group = lax.axis_index("gy"), lax.axis_size("gy")
        for s, ref in zip(order(group)[1:], row_refs):
            if s not in near(group):
                continue
            first = ref.shape[0] - ROWS
            for k, by in ((0, -1), (1, 1)):

                @pl.when(peer(me, s, group) == me + by)
                def _(ref=ref, k=k, first=first):
                    for j in range(ROWS):
                        side_ref[k, 8 * j : 8 * j + 8, :] = ref[first + j].astype(F32)

    @pl.when(own == 1)
    def _():
        run(SF, spacing_fine)

    @pl.when(own != 1)
    def _():
        run(SC, spacing_coarse)

    if not alone:
        base_ref = refs[-4]
        start = jnp.where(upper_differs, 0, 1)

        @pl.when(own == 1)
        def _():
            @pl.when(upper_differs)
            def _():
                base_ref[...] = done_ref[:, : NVF // 2]

            @pl.when(jnp.logical_not(upper_differs))
            def _():
                base_ref[...] = done_ref[:, NVF // 2 :]

        @pl.when(own != 1)
        def _():
            @pl.when(upper_differs)
            def _():
                base_ref[:, : NVC // 2] = done_ref[:, : NVC // 2]

            @pl.when(jnp.logical_not(upper_differs))
            def _():
                base_ref[:, : NVC // 2] = done_ref[:, NVC // 2 : NVC]

    for chunk in range(CHUNKS):
        flush(chunk).wait()


def relax(alone, levels, rate, cells, even, odd, rows):
    out = jax.ShapeDtypeStruct(cells.shape, F32)
    half = jax.ShapeDtypeStruct((cells.shape[0], NVF // 2), F32)
    return pl.pallas_call(
        functools.partial(relax_kernel, alone),
        name="relax",
        out_shape=(out,) if alone else (out, half),
        in_specs=[SMEM, SMEM, VMEM, VMEM, VMEM] + [VMEM] * len(rows),
        out_specs=(HBM,) if alone else (HBM, VMEM),
        scratch_shapes=[
            pltpu.VMEM((2, HALF_F, BLK), F32),
            pltpu.VMEM(cells.shape, F32),
            pltpu.SemaphoreType.DMA((CHUNKS,)),
        ],
        cost_estimate=pl.CostEstimate(flops=10**7, bytes_accessed=4 * 10**6, transcendentals=10**5),
        compiler_params=pltpu.CompilerParams(vmem_limit_bytes=16 << 20),
    )(levels, rate, cells, even, odd, *rows)


ROWS = HALF_F // 8


def attach(group, ahead_ref, back_ref, out_refs):
    me = lax.axis_index("gy")
    for s, out_ref in zip(order(group), out_refs):
        if s not in near(group):
            continue
        first = out_ref.shape[0] - ROWS
        for source_ref, by in ((ahead_ref, 1), (back_ref, -1)):

            @pl.when(peer(me, s, group) == me + by)
            def _(out_ref=out_ref, source_ref=source_ref, first=first):
                for j in range(ROWS):
                    out_ref[first + j] = source_ref[8 * j : 8 * j + 8, :]


def coarse_kernel(group, level_ref, even_ref, odd_ref, ahead_ref, back_ref, *out_refs):
    block, _, lower_differs, _ = place(level_ref)
    use_even = (block % 2 == 0) != lower_differs
    for j in range(VBC):
        a, b = even_ref[j].astype(F32), odd_ref[j].astype(F32)
        piece = jnp.where(use_even, a, b).astype(BF16)
        for out_ref in out_refs:
            out_ref[j] = piece
    attach(group, ahead_ref, back_ref, out_refs)


def pieces_kernel(group, level_ref, link_ref, even_ref, odd_ref, ahead_ref, back_ref, *refs):
    out_refs, start_ref = refs[:-1], refs[-1]
    block, own, lower_differs, _ = place(level_ref)
    me = lax.axis_index("gy")
    local = VBF // group
    slots = out_refs[0].shape[0]
    use_even = (block % 2 == 0) != lower_differs

    def count(h, total):
        start_ref[h] = total
        for j in range(local):
            hit = (link_ref[1, h * local + j] >= HALF_C) == lower_differs
            total = total + hit.astype(jnp.int32)
        return total

    lax.fori_loop(0, group, count, jnp.int32(0))

    def fill(source_ref):
        for s, out_ref in zip(order(group), out_refs):
            start = start_ref[peer(me, s, group)]
            for j in range(slots):
                out_ref[j] = source_ref[jnp.minimum(start + j, HALF_F - 1)]

    @pl.when(use_even)
    def _():
        fill(even_ref)

    @pl.when(jnp.logical_not(use_even))
    def _():
        fill(odd_ref)

    attach(group, ahead_ref, back_ref, out_refs)


def outgoing_shapes(slots, group, rows_n):
    return tuple(
        jax.ShapeDtypeStruct((slots + (ROWS if s in near(group) else 0), rows_n, BLK), BF16)
        for s in order(group)
    )


def coarse_pieces(levels, even, odd, edges, group):
    return pl.pallas_call(
        functools.partial(coarse_kernel, group),
        name="coarse_pieces",
        out_shape=outgoing_shapes(VBC, group, even.shape[1]),
        in_specs=[SMEM] + [VMEM] * 4,
        out_specs=(VMEM,) * group,
        cost_estimate=pl.CostEstimate(flops=10**5, bytes_accessed=10**6, transcendentals=0),
        compiler_params=pltpu.CompilerParams(vmem_limit_bytes=8 << 20),
    )(levels, even, odd, *edges)


def pieces(levels, links, even, odd, edges, group, slots):
    return pl.pallas_call(
        functools.partial(pieces_kernel, group),
        name="pieces",
        out_shape=outgoing_shapes(slots, group, even.shape[1]),
        in_specs=[SMEM, SMEM] + [VMEM] * 4,
        out_specs=(VMEM,) * group,
        scratch_shapes=[pltpu.SMEM((group,), jnp.int32)],
        cost_estimate=pl.CostEstimate(flops=10**5, bytes_accessed=10**6, transcendentals=0),
        compiler_params=pltpu.CompilerParams(vmem_limit_bytes=8 << 20),
    )(levels, links, even, odd, *edges)


def stacked(refs, index):
    return jnp.concatenate([ref[index].astype(F32) for ref in refs], axis=0).astype(BF16)


def to_coarse_kernel(group, level_ref, link_ref, head_ref, tail_ref, *refs):
    in_refs, out_refs, sum_ref = refs[:group], refs[group : 2 * group], refs[-1]
    _, _, lower_differs, _ = place(level_ref)
    half = head_ref.shape[0]
    local = half + tail_ref.shape[0]
    cells_y = in_refs[0].shape[1]
    first = lax.axis_index("gy") * local
    offset = jnp.where(lower_differs, HALF_C, 0)

    targets = [link_ref[1, first + j] - offset for j in range(local)]
    needed = [(t >= 0) & (t < HALF_C) for t in targets]
    sum_ref[...] = jnp.zeros_like(sum_ref)
    slot = jnp.int32(0)
    for j in range(local):

        @pl.when(needed[j])
        def _(j=j, slot=slot):
            sum_ref[targets[j]] += jnp.dot(
                stacked(in_refs, slot), (head_ref[j] if j < half else tail_ref[j - half]), preferred_element_type=F32
            )

        slot = slot + needed[j].astype(jnp.int32)
    for s, out_ref in enumerate(out_refs):
        out_ref[...] = sum_ref[:, s * cells_y : (s + 1) * cells_y, :].astype(BF16)


def to_fine_kernel(group, level_ref, link_ref, head_ref, tail_ref, *refs):
    in_refs, out_refs = refs[:group], refs[group : 2 * group]
    _, _, lower_differs, _ = place(level_ref)
    half = head_ref.shape[0]
    local = half + tail_ref.shape[0]
    cells_y = in_refs[0].shape[1]
    first = lax.axis_index("gy") * local
    active = (first >= HALF_F) == lower_differs

    @pl.when(active)
    def _():
        for j in range(local):
            product = jnp.dot(
                stacked(in_refs, link_ref[0, first + j]),
                (head_ref[j] if j < half else tail_ref[j - half]),
                preferred_element_type=F32,
            ).astype(BF16)
            for s, out_ref in enumerate(out_refs):
                out_ref[j] = product[s * cells_y : (s + 1) * cells_y, :]


def load_kernel(start, stop, level_ref, link_ref, values_ref, role_ref, held_ref, sems):
    _, own, lower_differs, upper_differs = place(level_ref)
    local = values_ref.shape[1]
    first = lax.axis_index("gy") * local
    fine = own == 1
    source = jnp.where(fine, 0, 1)

    def needed(j):
        coarse = (link_ref[1, first + j] >= HALF_C) == lower_differs
        here = jnp.where(fine, (first >= HALF_F) == lower_differs, coarse)
        return here & (lower_differs | upper_differs)

    def copy(j):
        at = j - start
        return pltpu.make_async_copy(values_ref.at[source, j], held_ref.at[at], sems.at[at])

    for j in range(start, stop):
        pl.when(needed(j))(lambda j=j: copy(j).start())

    if start == 0:

        def most(h, worst):
            count = jnp.int32(0)
            for j in range(local):
                hit = (link_ref[1, h * local + j] >= HALF_C) == lower_differs
                count = count + hit.astype(jnp.int32)
            return jnp.maximum(worst, count)

        worst = lax.fori_loop(0, VBF // local, most, jnp.int32(0))
        coarse_role = jnp.where(worst > few(local), 2, 1)
        role = jnp.where(fine, jnp.where(lower_differs, 3, 4), coarse_role)
        role_ref[0] = jnp.where(lower_differs | upper_differs, role, 0)
    for j in range(start, stop):
        pl.when(needed(j))(lambda j=j: copy(j).wait())


def load(levels, links, values, start, stop):
    return pl.pallas_call(
        functools.partial(load_kernel, start, stop),
        name="load",
        out_shape=(
            jax.ShapeDtypeStruct((1,), jnp.int32),
            jax.ShapeDtypeStruct((stop - start,) + values.shape[2:], BF16),
        ),
        in_specs=[SMEM, SMEM, HBM],
        out_specs=(SMEM, VMEM),
        scratch_shapes=[pltpu.SemaphoreType.DMA((stop - start,))],
        cost_estimate=pl.CostEstimate(
            flops=0, bytes_accessed=(stop - start) * BLK * BLK * 2, transcendentals=0
        ),
        compiler_params=pltpu.CompilerParams(vmem_limit_bytes=44 << 20),
    )(levels, links, values)


def multiply(kernel, levels, links, values, arrived, slots, scratch):
    group = len(arrived)
    local = sum(part.shape[0] for part in values)
    out = jax.ShapeDtypeStruct((slots,) + arrived[0].shape[1:], BF16)
    return pl.pallas_call(
        functools.partial(kernel, group),
        name=kernel.__name__,
        out_shape=(out,) * group,
        in_specs=[SMEM, SMEM, VMEM, VMEM] + [VMEM] * group,
        out_specs=(VMEM,) * group,
        scratch_shapes=scratch,
        cost_estimate=pl.CostEstimate(
            flops=2 * local * 32 * BLK * BLK, bytes_accessed=2 * local * BLK * BLK, transcendentals=0
        ),
        compiler_params=pltpu.CompilerParams(vmem_limit_bytes=24 << 20),
    )(levels, links, *values, *arrived)


def finish_kernel(role, group, level_ref, base_ref, held_ref, *refs):
    in_refs, out_ref, done_ref, sems = refs[:-3], refs[-3], refs[-2], refs[-1]
    _, _, _, upper_differs = place(level_ref)
    me = lax.axis_index("gy")
    parts = sems.shape[0]
    side, spacing, count = (
        (SC, spacing_coarse, HALF_C) if role == 1 else (SF, spacing_fine, HALF_F)
    )
    whole = count * BLK
    part = whole // parts
    centre = (side - 1) * 0.5

    def flush(index):
        start = index * part + jnp.where(upper_differs, 0, whole)
        at = pl.ds(pl.multiple_of(start, part), part)
        return pltpu.make_async_copy(
            done_ref.at[:, pl.ds(pl.multiple_of(index * part, part), part)],
            out_ref.at[:, at],
            sems.at[index],
        )

    first_plane = jnp.where(upper_differs, 0, side // 2)
    if role == 1:
        width = side * side
        for o in range(HALF_C):
            ghost = in_refs[0][o].astype(F32)
            for ref in in_refs[1:]:
                ghost = ghost + ref[o].astype(F32)
            for k in range(BLK // width):
                plane = lax.convert_element_type(first_plane + o * (BLK // width) + k, F32)
                push = cfl_ratio * spacing * jnp.abs(plane - centre)
                at = slice(o * BLK + k * width, o * BLK + (k + 1) * width)
                done_ref[:, at] = base_ref[:, at] + push * ghost[:, k * width : (k + 1) * width]
        flush(0).start()
        flush(0).wait()
        return

    offset = jnp.where(upper_differs, 0, HALF_F)
    for s, ref in zip(order(group), in_refs):
        local = ref.shape[0]
        first = peer(me, s, group) * local - offset

        @pl.when((first >= 0) & (first < HALF_F))
        def _(ref=ref, first=first, local=local):
            for j in range(local):
                slot = first + j
                plane = lax.convert_element_type(first_plane + slot // 2, F32)
                push = cfl_ratio * spacing * jnp.abs(plane - centre)
                at = pl.ds(pl.multiple_of(slot * BLK, BLK), BLK)
                done_ref[:, at] = base_ref[:, at] + push * ref[j].astype(F32)
            flush(lax.div(first, local)).start()

    for index in range(parts):
        flush(index).wait()


def finish(role, levels, base, held, arrived):
    group = len(arrived)
    rows_n = base.shape[0]
    parts = 1 if role == 1 else group // 2
    whole = NVC // 2 if role == 1 else NVF // 2
    return pl.pallas_call(
        functools.partial(finish_kernel, role, group),
        name="finish",
        out_shape=jax.ShapeDtypeStruct(held.shape, F32),
        in_specs=[SMEM, VMEM, HBM] + [VMEM] * group,
        out_specs=HBM,
        scratch_shapes=[pltpu.VMEM((rows_n, whole), F32), pltpu.SemaphoreType.DMA((parts,))],
        input_output_aliases={2: 0},
        cost_estimate=pl.CostEstimate(flops=10**6, bytes_accessed=10**6, transcendentals=0),
        compiler_params=pltpu.CompilerParams(vmem_limit_bytes=8 << 20),
    )(levels, base, held, *arrived)


def on_device(distribution, relax_rate, block_level, block_link, remap_values):
    blocks, group = lax.axis_size("gx"), lax.axis_size("gy")
    cells_y = distribution.shape[1]
    local = remap_values.shape[1]
    cells = distribution[0]

    def exchange(value, parity):
        pairs = []
        for low in range(parity, blocks - 1, 2):
            for y in range(group):
                here, there = low * group + y, (low + 1) * group + y
                pairs += [(here, there), (there, here)]
        return lax.ppermute(value, BOTH, pairs)

    everyone = range(group)

    def around(outgoing, sources=everyone, targets=everyone, rows=False):
        arrived = []
        for s, value in zip(order(group), outgoing):
            pairs = [
                (i, peer(i, s, group))
                for i in everyone
                if (i in sources and peer(i, s, group) in targets)
                or (rows and abs(i - peer(i, s, group)) == 1)
            ]
            arrived.append(lax.ppermute(value, "gy", pairs) if s and pairs else value)
        return arrived

    even, odd = prepare(block_level, block_link, cells)
    odd = exchange(odd, 1)
    even = exchange(even, 0)
    role, head = load(block_level, block_link, remap_values, 0, local // 2)
    edges = edge_rows(block_level, cells)

    def settle(alone, rows):
        return relax(alone, block_level, relax_rate, cells, even, odd, rows)

    def alone():
        left = lax.ppermute(edges[0], "gy", [(i, i + 1) for i in range(group - 1)])
        right = lax.ppermute(edges[1], "gy", [(i + 1, i) for i in range(group - 1)])
        return settle(True, [left, right])[0]

    def remapped(kernel, slots, scratch, arrived):
        tail = load(block_level, block_link, remap_values, local // 2, local)[1]
        values = [head, tail]
        made = multiply(kernel, block_level, block_link, values, arrived, slots, scratch)
        return made, settle(False, arrived[1:])

    def to_coarse(slots):
        outgoing = pieces(block_level, block_link, even, odd, edges, group, slots)
        sums = [pltpu.VMEM((HALF_C, group * cells_y, BLK), F32)]
        made, (out, base) = remapped(to_coarse_kernel, HALF_C, sums, around(outgoing))
        return finish(1, block_level, base, out, around(made))

    def to_fine(active):
        outgoing = coarse_pieces(block_level, even, odd, edges, group)
        arrived = around(outgoing, targets=active, rows=True)
        made, (out, base) = remapped(to_fine_kernel, local, [], arrived)
        return finish(2, block_level, base, out, around(made, sources=active))

    updated = lax.switch(
        role[0],
        [
            alone,
            lambda: to_coarse(few(local)),
            lambda: to_coarse(local),
            lambda: to_fine(range(group // 2, group)),
            lambda: to_fine(range(group // 2)),
        ],
    )
    return updated[None]


def solution(mesh):
    in_specs = (P("gx", "gy", None), P("gx", "gy"), P(), P(), P(None, "gy", None, None))
    out_specs = P("gx", "gy", None)
    return jax.shard_map(
        on_device, mesh=mesh, in_specs=in_specs, out_specs=out_specs, check_vma=False
    )
```

```python
import functools
import math

import jax
import jax.numpy as jnp
from jax import lax
from jax.experimental import pallas as pl
from jax.experimental.pallas import tpu as pltpu
from jax.sharding import PartitionSpec as P

SC = 16
SF = 32
BLK = 512
NVC = 4096
NVF = 32768
VBC = NVC // BLK
VBF = NVF // BLK
HALF_F = VBF // 2
HALF_C = VBC // 2

cfl_ratio = 0.03
spacing_coarse = 0.5
spacing_fine = 0.4

BOTH = ("gx", "gy")
SMEM = pl.BlockSpec(memory_space=pltpu.SMEM)
VMEM = pl.BlockSpec(memory_space=pltpu.VMEM)
HBM = pl.BlockSpec(memory_space=pltpu.HBM)
F32 = jnp.float32
BF16 = jnp.bfloat16


def place(level_ref):
    block = lax.axis_index("gx")
    own = level_ref[block]
    lower = level_ref[jnp.maximum(block - 1, 0)]
    upper = level_ref[jnp.minimum(block + 1, level_ref.shape[0] - 1)]
    return block, own, lower != own, upper != own


def peer(me, step, group):
    if group & (group - 1):
        raise ValueError(group)
    return me ^ step


def order(group):
    return sorted(range(group), key=lambda s: (s == 1, s))


def near(group):
    return [s for s in order(group) if s and not s & (s + 1)]


def sizes(local):
    return [max(1, (5 * local) // 8), max(1, (3 * local) // 4), local]


def block_at(ref, index):
    return ref[:, pl.ds(pl.multiple_of(index * BLK, BLK), BLK)]


def prepare_kernel(level_ref, link_ref, cells_ref, even_ref, odd_ref, index_ref):
    block, own, lower_differs, upper_differs = place(level_ref)
    fine = own == 1

    def fill(target_ref, going_up):
        differs = jnp.where(going_up, upper_differs, lower_differs)
        gathers = differs & fine

        @pl.when(gathers)
        def _():
            def look(f, count):
                index_ref[count] = f
                hit = (link_ref[1, f] >= HALF_C) == going_up
                return count + hit.astype(jnp.int32)

            lax.fori_loop(0, VBF, look, jnp.int32(0), unroll=8)

            def copy(j, carry):
                target_ref[j] = block_at(cells_ref, index_ref[j]).astype(BF16)
                return carry

            lax.fori_loop(0, HALF_F, copy, 0, unroll=8)

        @pl.when(fine & jnp.logical_not(differs))
        def _():
            start = jnp.where(going_up, HALF_F, 0)
            for j in range(HALF_F):
                target_ref[j] = block_at(cells_ref, start + j).astype(BF16)

        @pl.when(jnp.logical_not(fine))
        def _():
            start = jnp.where(going_up & jnp.logical_not(differs), HALF_C, 0)
            for j in range(VBC):
                target_ref[j] = block_at(cells_ref, start + j).astype(BF16)

    on_even = block % 2 == 0
    fill(odd_ref, jnp.logical_not(on_even))
    fill(even_ref, on_even)


def prepare(levels, links, cells):
    half = jax.ShapeDtypeStruct((HALF_F, cells.shape[0], BLK), BF16)
    return pl.pallas_call(
        prepare_kernel,
        name="prepare",
        out_shape=(half, half),
        in_specs=[SMEM, SMEM, VMEM],
        out_specs=(VMEM,) * 2,
        scratch_shapes=[pltpu.SMEM((VBF + 1,), jnp.int32)],
        cost_estimate=pl.CostEstimate(flops=10**6, bytes_accessed=2 * 10**6, transcendentals=0),
        compiler_params=pltpu.CompilerParams(vmem_limit_bytes=8 << 20),
    )(levels, links, cells)


def rows_kernel(level_ref, cells_ref, ahead_ref, back_ref, row_ref):
    _, own, _, _ = place(level_ref)
    cells_y = cells_ref.shape[0]

    def rows(target_ref, row, parity):
        @pl.when(own == 1)
        def _():
            for i in range(HALF_F):
                row_ref[i : i + 1, :] = cells_ref[
                    row : row + 1, (2 * i + parity) * BLK : (2 * i + parity + 1) * BLK
                ]

        @pl.when(own != 1)
        def _():
            for i in range(VBC):
                row_ref[i : i + 1, :] = cells_ref[row : row + 1, i * BLK : (i + 1) * BLK]

        target_ref[...] = row_ref[...].astype(BF16)

    rows(ahead_ref, cells_y - 1, 1)
    rows(back_ref, 0, 0)


def edge_rows(levels, cells):
    row = jax.ShapeDtypeStruct((HALF_F, BLK), BF16)
    return pl.pallas_call(
        rows_kernel,
        name="edge_rows",
        out_shape=(row, row),
        in_specs=[SMEM, VMEM],
        out_specs=(VMEM, VMEM),
        scratch_shapes=[pltpu.VMEM((HALF_F, BLK), F32)],
        cost_estimate=pl.CostEstimate(flops=10**6, bytes_accessed=2 * 10**6, transcendentals=0),
        compiler_params=pltpu.CompilerParams(vmem_limit_bytes=8 << 20),
    )(levels, cells)


CHUNKS = 8
PART = NVF // CHUNKS


def ghost_at(ref, index):
    return ref[index].astype(F32)


def relax_kernel(
    alone,
    level_ref,
    rate_ref,
    cells_ref,
    even_ref,
    odd_ref,
    *refs,
):
    side_ref, done_ref, sems = refs[-3:]
    results = 1 if alone else 2
    row_refs, out_ref = refs[: -3 - results], refs[-3 - results]
    block, own, lower_differs, upper_differs = place(level_ref)
    on_even = block % 2 == 0
    rows_n = cells_ref.shape[0]

    def flush(chunk):
        at = pl.ds(chunk * PART, PART)
        return pltpu.make_async_copy(done_ref.at[:, at], out_ref.at[:, at], sems.at[chunk])

    def run(side, spacing):
        width = side * side
        mid = width // 2
        middle = side // 2
        centre = (side - 1) * 0.5
        lane = lax.broadcasted_iota(jnp.int32, (rows_n, width), 1)
        along_y = spacing * ((lane // side).astype(F32) - centre)
        along_z = spacing * ((lane % side).astype(F32) - centre)

        def span(i):
            start = i * width
            return pl.ds(start if isinstance(i, int) else pl.multiple_of(start, width), width)

        def speed_at(i):
            return spacing * (lax.convert_element_type(i, F32) - centre)

        def gather(i, sums):
            total, first, second = sums
            plane = cells_ref[:, span(i)]
            speed = speed_at(i)
            return total + plane, first + plane * speed, second + plane * (speed * speed)

        zero = jnp.zeros((rows_n, width), F32)
        total, first, second = lax.fori_loop(0, side, gather, (zero, zero, zero), unroll=4)

        def over(value):
            return jnp.broadcast_to(jnp.sum(value, axis=1, keepdims=True), (rows_n, 128))

        weight = spacing * spacing * spacing
        density = weight * over(total)
        scale = weight / density
        mean_x = scale * over(first)
        mean_y = scale * over(total * along_y)
        mean_z = scale * over(total * along_z)
        square = scale * over(second + total * (along_y * along_y + along_z * along_z))
        heat = (square - mean_x * mean_x - mean_y * mean_y - mean_z * mean_z) / 3.0
        row = lax.broadcasted_iota(jnp.int32, (rows_n, 128), 0)
        rate = jnp.zeros((rows_n, 128), F32)
        for r in range(rows_n):
            rate = jnp.where(row == r, rate_ref[0, r], rate)
        spread = 2.0 * math.pi * heat
        peak = rate * density / (spread * jnp.sqrt(spread))
        inverse = -0.5 / heat

        def wide(value):
            return jnp.concatenate([value] * (width // 128), axis=1)

        off_y = along_y - wide(mean_y)
        off_z = along_z - wide(mean_z)
        across = wide(peak) * jnp.exp((off_y * off_y + off_z * off_z) * wide(inverse))
        drift = cfl_ratio * jnp.abs(along_y)
        keep = (1.0 - wide(rate)) - drift
        wide_row = lax.broadcasted_iota(jnp.int32, (rows_n, mid), 0)

        def update(i, upward):
            plane = cells_ref[:, span(i)]
            speed = speed_at(i)
            off_x = speed - mean_x
            along = wide(jnp.exp(off_x * off_x * inverse))
            take_even = on_even == upward
            if side == SF:
                right = side_ref[1, pl.ds(i, 1), :]
                left = side_ref[0, pl.ds(i, 1), :]
                slot = 2 * (i if upward else i - middle)
                ghosts = []
                for half in range(2):
                    a, b = ghost_at(even_ref, slot + half), ghost_at(odd_ref, slot + half)
                    ghosts.append(jnp.where(take_even, a, b))
                ghost = jnp.concatenate(ghosts, axis=1)
            else:
                slot, offset = i // 2, (i % 2) * width
                right = side_ref[1, slot : slot + 1, offset : offset + mid]
                left = side_ref[0, slot : slot + 1, offset + mid : offset + width]
                slot = slot if upward else slot - HALF_C
                a, b = ghost_at(even_ref, slot), ghost_at(odd_ref, slot)
                ghost = jnp.where(take_even, a, b)[:, offset : offset + width]
            if not alone:
                ghost = jnp.where(upper_differs if upward else lower_differs, 0.0, ghost)
            low, high = plane[:, :mid], plane[:, mid:]
            beyond = jnp.where(wide_row == rows_n - 1, right, pltpu.roll(low, rows_n - 1, 0))
            before = jnp.where(wide_row == 0, left, pltpu.roll(high, 1, 0))
            beside = jnp.concatenate([beyond, before], axis=1)
            push = cfl_ratio * jnp.abs(speed)
            done_ref[:, span(i)] = (
                plane * (keep - push) + push * ghost + drift * beside + along * across
            )

        if side == SF:
            each = side // CHUNKS
            for chunk in range(CHUNKS):
                upward = chunk < CHUNKS // 2

                def step(k, carry, chunk=chunk, upward=upward):
                    update(chunk * each + k, upward)
                    return carry

                lax.fori_loop(0, each, step, 0, unroll=4)
                flush(chunk).start()
        else:
            for i in range(side):
                update(i, i < middle)
            flush(0).start()
            done_ref[:, NVC:] = jnp.zeros((rows_n, NVF - NVC), F32)
            for chunk in range(1, CHUNKS):
                flush(chunk).start()

    if alone:
        for k, row_ref in enumerate(row_refs):
            side_ref[k] = row_ref[...].astype(F32)
    else:
        side_ref[...] = jnp.zeros_like(side_ref)
        me, group = lax.axis_index("gy"), lax.axis_size("gy")
        for s, ref in zip(near(group), row_refs):
            first = ref.shape[0] - ROWS
            for k, by in ((0, -1), (1, 1)):

                @pl.when(peer(me, s, group) == me + by)
                def _(ref=ref, k=k, first=first):
                    for j in range(ROWS):
                        side_ref[k, 8 * j : 8 * j + 8, :] = ref[first + j].astype(F32)

    @pl.when(own == 1)
    def _():
        run(SF, spacing_fine)

    @pl.when(own != 1)
    def _():
        run(SC, spacing_coarse)

    if not alone:
        base_ref = refs[-4]
        start = jnp.where(upper_differs, 0, 1)

        @pl.when(own == 1)
        def _():
            @pl.when(upper_differs)
            def _():
                base_ref[...] = done_ref[:, : NVF // 2]

            @pl.when(jnp.logical_not(upper_differs))
            def _():
                base_ref[...] = done_ref[:, NVF // 2 :]

        @pl.when(own != 1)
        def _():
            @pl.when(upper_differs)
            def _():
                base_ref[:, : NVC // 2] = done_ref[:, : NVC // 2]

            @pl.when(jnp.logical_not(upper_differs))
            def _():
                base_ref[:, : NVC // 2] = done_ref[:, NVC // 2 : NVC]

    for chunk in range(CHUNKS):
        flush(chunk).wait()


def relax(alone, levels, rate, cells, even, odd, rows):
    out = jax.ShapeDtypeStruct(cells.shape, F32)
    half = jax.ShapeDtypeStruct((cells.shape[0], NVF // 2), F32)
    return pl.pallas_call(
        functools.partial(relax_kernel, alone),
        name="relax",
        out_shape=(out,) if alone else (out, half),
        in_specs=[SMEM, SMEM, VMEM, VMEM, VMEM] + [VMEM] * len(rows),
        out_specs=(HBM,) if alone else (HBM, VMEM),
        scratch_shapes=[
            pltpu.VMEM((2, HALF_F, BLK), F32),
            pltpu.VMEM(cells.shape, F32),
            pltpu.SemaphoreType.DMA((CHUNKS,)),
        ],
        cost_estimate=pl.CostEstimate(flops=10**7, bytes_accessed=4 * 10**6, transcendentals=10**5),
        compiler_params=pltpu.CompilerParams(vmem_limit_bytes=16 << 20),
    )(levels, rate, cells, even, odd, *rows)


ROWS = HALF_F // 8


def attach(group, ahead_ref, back_ref, out_refs):
    me = lax.axis_index("gy")
    for s, out_ref in zip(order(group), out_refs):
        if s not in near(group):
            continue
        first = out_ref.shape[0] - ROWS
        for source_ref, by in ((ahead_ref, 1), (back_ref, -1)):

            @pl.when(peer(me, s, group) == me + by)
            def _(out_ref=out_ref, source_ref=source_ref, first=first):
                for j in range(ROWS):
                    out_ref[first + j] = source_ref[8 * j : 8 * j + 8, :]


def coarse_kernel(group, level_ref, even_ref, odd_ref, ahead_ref, back_ref, *out_refs):
    block, _, lower_differs, _ = place(level_ref)
    use_even = (block % 2 == 0) != lower_differs
    full = [ref for ref in out_refs if ref.shape[0] >= VBC]
    for j in range(VBC):
        a, b = even_ref[j].astype(F32), odd_ref[j].astype(F32)
        piece = jnp.where(use_even, a, b).astype(BF16)
        for out_ref in full:
            out_ref[j] = piece
    attach(group, ahead_ref, back_ref, out_refs)


def pieces_kernel(group, level_ref, link_ref, even_ref, odd_ref, ahead_ref, back_ref, *refs):
    out_refs, start_ref = refs[:-1], refs[-1]
    block, own, lower_differs, _ = place(level_ref)
    me = lax.axis_index("gy")
    local = VBF // group
    slots = out_refs[0].shape[0]
    use_even = (block % 2 == 0) != lower_differs

    def count(h, total):
        start_ref[h] = total
        for j in range(local):
            hit = (link_ref[1, h * local + j] >= HALF_C) == lower_differs
            total = total + hit.astype(jnp.int32)
        return total

    lax.fori_loop(0, group, count, jnp.int32(0))

    def fill(source_ref):
        for s, out_ref in zip(order(group), out_refs):
            start = start_ref[peer(me, s, group)]
            for j in range(slots):
                out_ref[j] = source_ref[jnp.minimum(start + j, HALF_F - 1)]

    @pl.when(use_even)
    def _():
        fill(even_ref)

    @pl.when(jnp.logical_not(use_even))
    def _():
        fill(odd_ref)

    attach(group, ahead_ref, back_ref, out_refs)


def outgoing_shapes(slots, group, rows_n):
    return tuple(
        jax.ShapeDtypeStruct((slots + (ROWS if s in near(group) else 0), rows_n, BLK), BF16)
        for s in order(group)
    )


def coarse_pieces(levels, even, odd, edges, group):
    shapes = list(outgoing_shapes(VBC, group, even.shape[1]))
    shapes[order(group).index(group - 1)] = jax.ShapeDtypeStruct((ROWS,) + even.shape[1:], BF16)
    return pl.pallas_call(
        functools.partial(coarse_kernel, group),
        name="coarse_pieces",
        out_shape=tuple(shapes),
        in_specs=[SMEM] + [VMEM] * 4,
        out_specs=(VMEM,) * group,
        cost_estimate=pl.CostEstimate(flops=10**5, bytes_accessed=10**6, transcendentals=0),
        compiler_params=pltpu.CompilerParams(vmem_limit_bytes=8 << 20),
    )(levels, even, odd, *edges)


def pieces(levels, links, even, odd, edges, group, slots):
    return pl.pallas_call(
        functools.partial(pieces_kernel, group),
        name="pieces",
        out_shape=outgoing_shapes(slots, group, even.shape[1]),
        in_specs=[SMEM, SMEM] + [VMEM] * 4,
        out_specs=(VMEM,) * group,
        scratch_shapes=[pltpu.SMEM((group,), jnp.int32)],
        cost_estimate=pl.CostEstimate(flops=10**5, bytes_accessed=10**6, transcendentals=0),
        compiler_params=pltpu.CompilerParams(vmem_limit_bytes=8 << 20),
    )(levels, links, even, odd, *edges)


def stacked(refs, index):
    return jnp.concatenate([ref[index].astype(F32) for ref in refs], axis=0).astype(BF16)


def to_coarse_kernel(group, level_ref, link_ref, values_ref, *refs):
    in_refs, out_refs, sum_ref = refs[:group], refs[group : 2 * group], refs[-1]
    _, _, lower_differs, _ = place(level_ref)
    local = values_ref.shape[0]
    cells_y = in_refs[0].shape[1]
    first = lax.axis_index("gy") * local
    offset = jnp.where(lower_differs, HALF_C, 0)

    targets = [link_ref[1, first + j] - offset for j in range(local)]
    needed = [(t >= 0) & (t < HALF_C) for t in targets]
    sum_ref[...] = jnp.zeros_like(sum_ref)
    slot = jnp.int32(0)
    for j in range(local):

        @pl.when(needed[j])
        def _(j=j, slot=slot):
            sum_ref[targets[j]] += jnp.dot(
                stacked(in_refs, slot), values_ref[j], preferred_element_type=F32
            )

        slot = slot + needed[j].astype(jnp.int32)
    for s, out_ref in enumerate(out_refs):
        out_ref[...] = sum_ref[:, s * cells_y : (s + 1) * cells_y, :].astype(BF16)


def to_fine_kernel(group, level_ref, link_ref, values_ref, *refs):
    in_refs, out_refs = refs[:group], refs[group : 2 * group]
    _, _, lower_differs, _ = place(level_ref)
    local = values_ref.shape[0]
    cells_y = in_refs[0].shape[1]
    first = lax.axis_index("gy") * local
    active = (first >= HALF_F) == lower_differs

    @pl.when(active)
    def _():
        for j in range(local):
            product = jnp.dot(
                stacked(in_refs, link_ref[0, first + j]),
                values_ref[j],
                preferred_element_type=F32,
            ).astype(BF16)
            for s, out_ref in enumerate(out_refs):
                out_ref[j] = product[s * cells_y : (s + 1) * cells_y, :]


def load_kernel(level_ref, link_ref, values_ref, role_ref, held_ref, sems):
    _, own, lower_differs, upper_differs = place(level_ref)
    local = values_ref.shape[1]
    first = lax.axis_index("gy") * local
    fine = own == 1
    source = jnp.where(fine, 0, 1)
    differs = lower_differs | upper_differs

    def needed(j):
        coarse = (link_ref[1, first + j] >= HALF_C) == lower_differs
        here = jnp.where(fine, (first >= HALF_F) == lower_differs, coarse)
        return here & differs

    def copy(j):
        return pltpu.make_async_copy(values_ref.at[source, j], held_ref.at[j], sems.at[j])

    for j in range(local):
        pl.when(needed(j))(lambda j=j: copy(j).start())

    counts = sizes(local)
    fine_role = len(counts) + jnp.where(lower_differs, 1, 2)
    role_ref[0] = jnp.where(differs & fine, fine_role, 0)

    @pl.when(differs & jnp.logical_not(fine))
    def _():
        def most(h, worst):
            count = jnp.int32(0)
            for j in range(local):
                hit = (link_ref[1, h * local + j] >= HALF_C) == lower_differs
                count = count + hit.astype(jnp.int32)
            return jnp.maximum(worst, count)

        worst = lax.fori_loop(0, VBF // local, most, jnp.int32(0))
        role = jnp.int32(1)
        for size in counts[:-1]:
            role = role + (worst > size).astype(jnp.int32)
        role_ref[0] = role

    for j in range(local):
        pl.when(needed(j))(lambda j=j: copy(j).wait())


def load(levels, links, values):
    local = values.shape[1]
    return pl.pallas_call(
        load_kernel,
        name="load",
        out_shape=(
            jax.ShapeDtypeStruct((1,), jnp.int32),
            jax.ShapeDtypeStruct(values.shape[1:], BF16),
        ),
        in_specs=[SMEM, SMEM, HBM],
        out_specs=(SMEM, VMEM),
        scratch_shapes=[pltpu.SemaphoreType.DMA((local,))],
        cost_estimate=pl.CostEstimate(
            flops=0, bytes_accessed=local * BLK * BLK * 2, transcendentals=0
        ),
        compiler_params=pltpu.CompilerParams(vmem_limit_bytes=44 << 20),
    )(levels, links, values)


def multiply(kernel, levels, links, values, arrived, slots, scratch):
    group = len(arrived)
    local = values.shape[0]
    out = jax.ShapeDtypeStruct((slots,) + arrived[0].shape[1:], BF16)
    return pl.pallas_call(
        functools.partial(kernel, group),
        name=kernel.__name__,
        out_shape=(out,) * group,
        in_specs=[SMEM, SMEM, VMEM] + [VMEM] * group,
        out_specs=(VMEM,) * group,
        scratch_shapes=scratch,
        cost_estimate=pl.CostEstimate(
            flops=2 * local * 32 * BLK * BLK, bytes_accessed=2 * local * BLK * BLK, transcendentals=0
        ),
        compiler_params=pltpu.CompilerParams(vmem_limit_bytes=24 << 20),
    )(levels, links, values, *arrived)


def finish_kernel(role, group, level_ref, base_ref, held_ref, *refs):
    in_refs, out_ref, done_ref, sems = refs[:-3], refs[-3], refs[-2], refs[-1]
    _, _, _, upper_differs = place(level_ref)
    me = lax.axis_index("gy")
    parts = sems.shape[0]
    side, spacing, count = (
        (SC, spacing_coarse, HALF_C) if role == 1 else (SF, spacing_fine, HALF_F)
    )
    whole = count * BLK
    part = whole // parts
    centre = (side - 1) * 0.5

    def flush(index):
        start = index * part + jnp.where(upper_differs, 0, whole)
        at = pl.ds(pl.multiple_of(start, part), part)
        return pltpu.make_async_copy(
            done_ref.at[:, pl.ds(pl.multiple_of(index * part, part), part)],
            out_ref.at[:, at],
            sems.at[index],
        )

    first_plane = jnp.where(upper_differs, 0, side // 2)
    if role == 1:
        width = side * side
        for o in range(HALF_C):
            ghost = in_refs[0][o].astype(F32)
            for ref in in_refs[1:]:
                ghost = ghost + ref[o].astype(F32)
            for k in range(BLK // width):
                plane = lax.convert_element_type(first_plane + o * (BLK // width) + k, F32)
                push = cfl_ratio * spacing * jnp.abs(plane - centre)
                at = slice(o * BLK + k * width, o * BLK + (k + 1) * width)
                done_ref[:, at] = base_ref[:, at] + push * ghost[:, k * width : (k + 1) * width]
        flush(0).start()
        flush(0).wait()
        return

    offset = jnp.where(upper_differs, 0, HALF_F)
    for s, ref in zip(order(group), in_refs):
        local = ref.shape[0]
        first = peer(me, s, group) * local - offset

        @pl.when((first >= 0) & (first < HALF_F))
        def _(ref=ref, first=first, local=local):
            for j in range(local):
                slot = first + j
                plane = lax.convert_element_type(first_plane + slot // 2, F32)
                push = cfl_ratio * spacing * jnp.abs(plane - centre)
                at = pl.ds(pl.multiple_of(slot * BLK, BLK), BLK)
                done_ref[:, at] = base_ref[:, at] + push * ref[j].astype(F32)
            flush(lax.div(first, local)).start()

    for index in range(parts):
        flush(index).wait()


def finish(role, levels, base, held, arrived):
    group = len(arrived)
    rows_n = base.shape[0]
    parts = 1 if role == 1 else group // 2
    whole = NVC // 2 if role == 1 else NVF // 2
    return pl.pallas_call(
        functools.partial(finish_kernel, role, group),
        name="finish",
        out_shape=jax.ShapeDtypeStruct(held.shape, F32),
        in_specs=[SMEM, VMEM, HBM] + [VMEM] * group,
        out_specs=HBM,
        scratch_shapes=[pltpu.VMEM((rows_n, whole), F32), pltpu.SemaphoreType.DMA((parts,))],
        input_output_aliases={2: 0},
        cost_estimate=pl.CostEstimate(flops=10**6, bytes_accessed=10**6, transcendentals=0),
        compiler_params=pltpu.CompilerParams(vmem_limit_bytes=8 << 20),
    )(levels, base, held, *arrived)


def on_device(distribution, relax_rate, block_level, block_link, remap_values):
    blocks, group = lax.axis_size("gx"), lax.axis_size("gy")
    cells_y = distribution.shape[1]
    local = remap_values.shape[1]
    cells = distribution[0]

    def exchange(value, parity):
        pairs = []
        for low in range(parity, blocks - 1, 2):
            for y in range(group):
                here, there = low * group + y, (low + 1) * group + y
                pairs += [(here, there), (there, here)]
        return lax.ppermute(value, BOTH, pairs)

    everyone = range(group)

    def step(value, s, keep):
        pairs = [(i, peer(i, s, group)) for i in everyone if keep(i, peer(i, s, group))]
        return lax.ppermute(value, "gy", pairs) if s and pairs else value

    def around(outgoing, sources=everyone):
        return [
            step(value, s, lambda i, j: i in sources) for s, value in zip(order(group), outgoing)
        ]

    def gather(outgoing, active):
        outgoing = dict(zip(order(group), outgoing))
        middle = group // 2
        crossed = step(outgoing[middle], middle, lambda i, j: j in active)
        arrived = {0: outgoing[0], middle: crossed}
        for s in range(1, middle):
            arrived[s] = step(
                outgoing[s], s, lambda i, j: j in active and i in active or abs(i - j) == 1
            )
        rows = {s: arrived[s] for s in near(group) if s < middle}
        lone = group - 1
        rows[lone] = step(outgoing[lone], lone, lambda i, j: abs(i - j) == 1)
        for s in range(1, middle):
            arrived[s ^ middle] = step(crossed, s, lambda i, j: j in active and i in active)
        return lax.optimization_barrier(
            ([arrived[s] for s in order(group)], [rows[s] for s in near(group)])
        )

    even, odd = prepare(block_level, block_link, cells)
    odd = exchange(odd, 1)
    even = exchange(even, 0)
    role, held = load(block_level, block_link, remap_values)
    edges = edge_rows(block_level, cells)

    def settle(alone, rows):
        return relax(alone, block_level, relax_rate, cells, even, odd, rows)

    def alone():
        left = lax.ppermute(edges[0], "gy", [(i, i + 1) for i in range(group - 1)])
        right = lax.ppermute(edges[1], "gy", [(i + 1, i) for i in range(group - 1)])
        return settle(True, [left, right])[0]

    def multiplied(kernel, slots, scratch, arrived):
        return multiply(kernel, block_level, block_link, held, arrived, slots, scratch)

    def to_coarse(slots):
        outgoing = pieces(block_level, block_link, even, odd, edges, group, slots)
        arrived = around(outgoing)
        sums = [pltpu.VMEM((HALF_C, group * cells_y, BLK), F32)]
        made = multiplied(to_coarse_kernel, HALF_C, sums, arrived)
        out, base = settle(
            False, [piece for s, piece in zip(order(group), arrived) if s in near(group)]
        )
        return finish(1, block_level, base, out, around(made))

    def to_fine(active):
        outgoing = coarse_pieces(block_level, even, odd, edges, group)
        arrived, rows = gather(outgoing, active)
        made = multiplied(to_fine_kernel, local, [], arrived)
        out, base = settle(False, rows)
        return finish(2, block_level, base, out, around(made, sources=active))

    branches = [alone]
    for slots in sizes(local):
        branches.append(functools.partial(to_coarse, slots))
    for active in (range(group // 2, group), range(group // 2)):
        branches.append(functools.partial(to_fine, active))
    updated = lax.switch(role[0], branches)
    return updated[None]


def solution(mesh):
    in_specs = (P("gx", "gy", None), P("gx", "gy"), P(), P(), P(None, "gy", None, None))
    out_specs = P("gx", "gy", None)
    return jax.shard_map(
        on_device, mesh=mesh, in_specs=in_specs, out_specs=out_specs, check_vma=False
    )
```

```python
import functools
import math

import jax
import jax.numpy as jnp
from jax import lax
from jax.experimental import pallas as pl
from jax.experimental.pallas import tpu as pltpu
from jax.sharding import PartitionSpec as P

SC = 16
SF = 32
BLK = 512
NVC = 4096
NVF = 32768
VBC = NVC // BLK
VBF = NVF // BLK
HALF_F = VBF // 2
HALF_C = VBC // 2

cfl_ratio = 0.03
spacing_coarse = 0.5
spacing_fine = 0.4

BOTH = ("gx", "gy")
SMEM = pl.BlockSpec(memory_space=pltpu.SMEM)
VMEM = pl.BlockSpec(memory_space=pltpu.VMEM)
HBM = pl.BlockSpec(memory_space=pltpu.HBM)
F32 = jnp.float32
BF16 = jnp.bfloat16


def place(level_ref):
    block = lax.axis_index("gx")
    own = level_ref[block]
    lower = level_ref[jnp.maximum(block - 1, 0)]
    upper = level_ref[jnp.minimum(block + 1, level_ref.shape[0] - 1)]
    return block, own, lower != own, upper != own


def peer(me, step, group):
    if group & (group - 1):
        raise ValueError(group)
    return me ^ step


def order(group):
    return sorted(range(group), key=lambda s: (s == 1, s))


def near(group):
    return [s for s in order(group) if s and not s & (s + 1)]


def sizes(local):
    return [max(1, (5 * local) // 8), max(1, (3 * local) // 4), local]


def block_at(ref, index):
    return ref[:, pl.ds(pl.multiple_of(index * BLK, BLK), BLK)]


def prepare_kernel(level_ref, link_ref, cells_ref, even_ref, odd_ref, index_ref):
    block, own, lower_differs, upper_differs = place(level_ref)
    fine = own == 1

    def fill(target_ref, going_up):
        differs = jnp.where(going_up, upper_differs, lower_differs)
        gathers = differs & fine

        @pl.when(gathers)
        def _():
            def look(f, count):
                index_ref[count] = f
                hit = (link_ref[1, f] >= HALF_C) == going_up
                return count + hit.astype(jnp.int32)

            lax.fori_loop(0, VBF, look, jnp.int32(0), unroll=8)

            def copy(j, carry):
                target_ref[j] = block_at(cells_ref, index_ref[j]).astype(BF16)
                return carry

            lax.fori_loop(0, HALF_F, copy, 0, unroll=8)

        @pl.when(fine & jnp.logical_not(differs))
        def _():
            start = jnp.where(going_up, HALF_F, 0)
            for j in range(HALF_F):
                target_ref[j] = block_at(cells_ref, start + j).astype(BF16)

        @pl.when(jnp.logical_not(fine))
        def _():
            start = jnp.where(going_up & jnp.logical_not(differs), HALF_C, 0)
            for j in range(VBC):
                target_ref[j] = block_at(cells_ref, start + j).astype(BF16)

    on_even = block % 2 == 0
    fill(odd_ref, jnp.logical_not(on_even))
    fill(even_ref, on_even)


def prepare(levels, links, cells):
    half = jax.ShapeDtypeStruct((HALF_F, cells.shape[0], BLK), BF16)
    return pl.pallas_call(
        prepare_kernel,
        name="prepare",
        out_shape=(half, half),
        in_specs=[SMEM, SMEM, VMEM],
        out_specs=(VMEM,) * 2,
        scratch_shapes=[pltpu.SMEM((VBF + 1,), jnp.int32)],
        cost_estimate=pl.CostEstimate(flops=10**6, bytes_accessed=2 * 10**6, transcendentals=0),
        compiler_params=pltpu.CompilerParams(vmem_limit_bytes=8 << 20),
    )(levels, links, cells)


def rows_kernel(level_ref, cells_ref, ahead_ref, back_ref, row_ref):
    _, own, _, _ = place(level_ref)
    cells_y = cells_ref.shape[0]

    def rows(target_ref, row, parity):
        @pl.when(own == 1)
        def _():
            for i in range(HALF_F):
                row_ref[i : i + 1, :] = cells_ref[
                    row : row + 1, (2 * i + parity) * BLK : (2 * i + parity + 1) * BLK
                ]

        @pl.when(own != 1)
        def _():
            for i in range(VBC):
                row_ref[i : i + 1, :] = cells_ref[row : row + 1, i * BLK : (i + 1) * BLK]

        target_ref[...] = row_ref[...].astype(BF16)

    rows(ahead_ref, cells_y - 1, 1)
    rows(back_ref, 0, 0)


def edge_rows(levels, cells):
    row = jax.ShapeDtypeStruct((HALF_F, BLK), BF16)
    return pl.pallas_call(
        rows_kernel,
        name="edge_rows",
        out_shape=(row, row),
        in_specs=[SMEM, VMEM],
        out_specs=(VMEM, VMEM),
        scratch_shapes=[pltpu.VMEM((HALF_F, BLK), F32)],
        cost_estimate=pl.CostEstimate(flops=10**6, bytes_accessed=2 * 10**6, transcendentals=0),
        compiler_params=pltpu.CompilerParams(vmem_limit_bytes=8 << 20),
    )(levels, cells)


CHUNKS = 8
PART = NVF // CHUNKS


def ghost_at(ref, index):
    return ref[index].astype(F32)


def relax_kernel(
    alone,
    level_ref,
    rate_ref,
    cells_ref,
    even_ref,
    odd_ref,
    *refs,
):
    side_ref, done_ref, sems = refs[-3:]
    results = 1 if alone else 2
    row_refs, out_ref = refs[: -3 - results], refs[-3 - results]
    block, own, lower_differs, upper_differs = place(level_ref)
    on_even = block % 2 == 0
    rows_n = cells_ref.shape[0]

    def flush(chunk):
        at = pl.ds(chunk * PART, PART)
        return pltpu.make_async_copy(done_ref.at[:, at], out_ref.at[:, at], sems.at[chunk])

    def run(side, spacing):
        width = side * side
        mid = width // 2
        middle = side // 2
        centre = (side - 1) * 0.5
        lane = lax.broadcasted_iota(jnp.int32, (rows_n, width), 1)
        along_y = spacing * ((lane // side).astype(F32) - centre)
        along_z = spacing * ((lane % side).astype(F32) - centre)

        def span(i):
            start = i * width
            return pl.ds(start if isinstance(i, int) else pl.multiple_of(start, width), width)

        def speed_at(i):
            return spacing * (lax.convert_element_type(i, F32) - centre)

        def gather(i, sums):
            total, first, second = sums
            plane = cells_ref[:, span(i)]
            speed = speed_at(i)
            return total + plane, first + plane * speed, second + plane * (speed * speed)

        zero = jnp.zeros((rows_n, width), F32)
        total, first, second = lax.fori_loop(0, side, gather, (zero, zero, zero), unroll=4)

        def over(value):
            return jnp.broadcast_to(jnp.sum(value, axis=1, keepdims=True), (rows_n, 128))

        weight = spacing * spacing * spacing
        density = weight * over(total)
        scale = weight / density
        mean_x = scale * over(first)
        mean_y = scale * over(total * along_y)
        mean_z = scale * over(total * along_z)
        square = scale * over(second + total * (along_y * along_y + along_z * along_z))
        heat = (square - mean_x * mean_x - mean_y * mean_y - mean_z * mean_z) / 3.0
        row = lax.broadcasted_iota(jnp.int32, (rows_n, 128), 0)
        rate = jnp.zeros((rows_n, 128), F32)
        for r in range(rows_n):
            rate = jnp.where(row == r, rate_ref[0, r], rate)
        spread = 2.0 * math.pi * heat
        peak = rate * density / (spread * jnp.sqrt(spread))
        inverse = -0.5 / heat

        def wide(value):
            return jnp.concatenate([value] * (width // 128), axis=1)

        off_y = along_y - wide(mean_y)
        off_z = along_z - wide(mean_z)
        across = wide(peak) * jnp.exp((off_y * off_y + off_z * off_z) * wide(inverse))
        drift = cfl_ratio * jnp.abs(along_y)
        keep = (1.0 - wide(rate)) - drift
        wide_row = lax.broadcasted_iota(jnp.int32, (rows_n, mid), 0)

        def update(i, upward):
            plane = cells_ref[:, span(i)]
            speed = speed_at(i)
            off_x = speed - mean_x
            along = wide(jnp.exp(off_x * off_x * inverse))
            take_even = on_even == upward
            if side == SF:
                right = side_ref[1, pl.ds(i, 1), :]
                left = side_ref[0, pl.ds(i, 1), :]
                slot = 2 * (i if upward else i - middle)
                ghosts = []
                for half in range(2):
                    a, b = ghost_at(even_ref, slot + half), ghost_at(odd_ref, slot + half)
                    ghosts.append(jnp.where(take_even, a, b))
                ghost = jnp.concatenate(ghosts, axis=1)
            else:
                slot, offset = i // 2, (i % 2) * width
                right = side_ref[1, slot : slot + 1, offset : offset + mid]
                left = side_ref[0, slot : slot + 1, offset + mid : offset + width]
                slot = slot if upward else slot - HALF_C
                a, b = ghost_at(even_ref, slot), ghost_at(odd_ref, slot)
                ghost = jnp.where(take_even, a, b)[:, offset : offset + width]
            if not alone:
                ghost = jnp.where(upper_differs if upward else lower_differs, 0.0, ghost)
            low, high = plane[:, :mid], plane[:, mid:]
            beyond = jnp.where(wide_row == rows_n - 1, right, pltpu.roll(low, rows_n - 1, 0))
            before = jnp.where(wide_row == 0, left, pltpu.roll(high, 1, 0))
            beside = jnp.concatenate([beyond, before], axis=1)
            push = cfl_ratio * jnp.abs(speed)
            done_ref[:, span(i)] = (
                plane * (keep - push) + push * ghost + drift * beside + along * across
            )

        if side == SF:
            each = side // CHUNKS
            for chunk in range(CHUNKS):
                upward = chunk < CHUNKS // 2

                def step(k, carry, chunk=chunk, upward=upward):
                    update(chunk * each + k, upward)
                    return carry

                lax.fori_loop(0, each, step, 0, unroll=4)
                flush(chunk).start()
        else:
            for i in range(side):
                update(i, i < middle)
            flush(0).start()
            done_ref[:, NVC:] = jnp.zeros((rows_n, NVF - NVC), F32)
            for chunk in range(1, CHUNKS):
                flush(chunk).start()

    if alone:
        for k, row_ref in enumerate(row_refs):
            side_ref[k] = row_ref[...].astype(F32)
    else:
        side_ref[...] = jnp.zeros_like(side_ref)
        me, group = lax.axis_index("gy"), lax.axis_size("gy")
        for s, ref in zip(near(group), row_refs):
            first = ref.shape[0] - ROWS
            for k, by in ((0, -1), (1, 1)):

                @pl.when(peer(me, s, group) == me + by)
                def _(ref=ref, k=k, first=first):
                    for j in range(ROWS):
                        side_ref[k, 8 * j : 8 * j + 8, :] = ref[first + j].astype(F32)

    @pl.when(own == 1)
    def _():
        run(SF, spacing_fine)

    @pl.when(own != 1)
    def _():
        run(SC, spacing_coarse)

    if not alone:
        base_ref = refs[-4]
        start = jnp.where(upper_differs, 0, 1)

        @pl.when(own == 1)
        def _():
            @pl.when(upper_differs)
            def _():
                base_ref[...] = done_ref[:, : NVF // 2]

            @pl.when(jnp.logical_not(upper_differs))
            def _():
                base_ref[...] = done_ref[:, NVF // 2 :]

        @pl.when(own != 1)
        def _():
            @pl.when(upper_differs)
            def _():
                base_ref[:, : NVC // 2] = done_ref[:, : NVC // 2]

            @pl.when(jnp.logical_not(upper_differs))
            def _():
                base_ref[:, : NVC // 2] = done_ref[:, NVC // 2 : NVC]

    for chunk in range(CHUNKS):
        flush(chunk).wait()


def relax(alone, levels, rate, cells, even, odd, rows):
    out = jax.ShapeDtypeStruct(cells.shape, F32)
    half = jax.ShapeDtypeStruct((cells.shape[0], NVF // 2), F32)
    return pl.pallas_call(
        functools.partial(relax_kernel, alone),
        name="relax",
        out_shape=(out,) if alone else (out, half),
        in_specs=[SMEM, SMEM, VMEM, VMEM, VMEM] + [VMEM] * len(rows),
        out_specs=(HBM,) if alone else (HBM, VMEM),
        scratch_shapes=[
            pltpu.VMEM((2, HALF_F, BLK), F32),
            pltpu.VMEM(cells.shape, F32),
            pltpu.SemaphoreType.DMA((CHUNKS,)),
        ],
        cost_estimate=pl.CostEstimate(flops=10**7, bytes_accessed=4 * 10**6, transcendentals=10**5),
        compiler_params=pltpu.CompilerParams(vmem_limit_bytes=16 << 20),
    )(levels, rate, cells, even, odd, *rows)


ROWS = HALF_F // 8


def attach(group, ahead_ref, back_ref, out_refs):
    me = lax.axis_index("gy")
    for s, out_ref in zip(order(group), out_refs):
        if s not in near(group):
            continue
        first = out_ref.shape[0] - ROWS
        for source_ref, by in ((ahead_ref, 1), (back_ref, -1)):

            @pl.when(peer(me, s, group) == me + by)
            def _(out_ref=out_ref, source_ref=source_ref, first=first):
                for j in range(ROWS):
                    out_ref[first + j] = source_ref[8 * j : 8 * j + 8, :]


def coarse_kernel(group, level_ref, even_ref, odd_ref, ahead_ref, back_ref, *out_refs):
    block, _, lower_differs, _ = place(level_ref)
    use_even = (block % 2 == 0) != lower_differs
    for j in range(VBC):
        a, b = even_ref[j].astype(F32), odd_ref[j].astype(F32)
        piece = jnp.where(use_even, a, b).astype(BF16)
        for out_ref in out_refs:
            out_ref[j] = piece
    attach(group, ahead_ref, back_ref, out_refs)


def pieces_kernel(group, level_ref, link_ref, even_ref, odd_ref, ahead_ref, back_ref, *refs):
    out_refs, start_ref = refs[:-1], refs[-1]
    block, own, lower_differs, _ = place(level_ref)
    me = lax.axis_index("gy")
    local = VBF // group
    slots = out_refs[0].shape[0]
    use_even = (block % 2 == 0) != lower_differs

    def count(h, total):
        start_ref[h] = total
        for j in range(local):
            hit = (link_ref[1, h * local + j] >= HALF_C) == lower_differs
            total = total + hit.astype(jnp.int32)
        return total

    lax.fori_loop(0, group, count, jnp.int32(0))

    def fill(source_ref):
        for s, out_ref in zip(order(group), out_refs):
            start = start_ref[peer(me, s, group)]
            for j in range(slots):
                out_ref[j] = source_ref[jnp.minimum(start + j, HALF_F - 1)]

    @pl.when(use_even)
    def _():
        fill(even_ref)

    @pl.when(jnp.logical_not(use_even))
    def _():
        fill(odd_ref)

    attach(group, ahead_ref, back_ref, out_refs)


def outgoing_shapes(slots, group, rows_n):
    return tuple(
        jax.ShapeDtypeStruct((slots + (ROWS if s in near(group) else 0), rows_n, BLK), BF16)
        for s in order(group)
    )


def coarse_pieces(levels, even, odd, edges, group):
    return pl.pallas_call(
        functools.partial(coarse_kernel, group),
        name="coarse_pieces",
        out_shape=outgoing_shapes(VBC, group, even.shape[1]),
        in_specs=[SMEM] + [VMEM] * 4,
        out_specs=(VMEM,) * group,
        cost_estimate=pl.CostEstimate(flops=10**5, bytes_accessed=10**6, transcendentals=0),
        compiler_params=pltpu.CompilerParams(vmem_limit_bytes=8 << 20),
    )(levels, even, odd, *edges)


def pieces(levels, links, even, odd, edges, group, slots):
    return pl.pallas_call(
        functools.partial(pieces_kernel, group),
        name="pieces",
        out_shape=outgoing_shapes(slots, group, even.shape[1]),
        in_specs=[SMEM, SMEM] + [VMEM] * 4,
        out_specs=(VMEM,) * group,
        scratch_shapes=[pltpu.SMEM((group,), jnp.int32)],
        cost_estimate=pl.CostEstimate(flops=10**5, bytes_accessed=10**6, transcendentals=0),
        compiler_params=pltpu.CompilerParams(vmem_limit_bytes=8 << 20),
    )(levels, links, even, odd, *edges)


def stacked(refs, index):
    return jnp.concatenate([ref[index].astype(F32) for ref in refs], axis=0).astype(BF16)


def to_coarse_kernel(group, level_ref, link_ref, head_ref, tail_ref, *refs):
    in_refs, out_refs, sum_ref = refs[:group], refs[group : 2 * group], refs[-1]
    _, _, lower_differs, _ = place(level_ref)
    half = head_ref.shape[0]
    local = half + tail_ref.shape[0]
    cells_y = in_refs[0].shape[1]
    first = lax.axis_index("gy") * local
    offset = jnp.where(lower_differs, HALF_C, 0)

    targets = [link_ref[1, first + j] - offset for j in range(local)]
    needed = [(t >= 0) & (t < HALF_C) for t in targets]
    sum_ref[...] = jnp.zeros_like(sum_ref)
    slot = jnp.int32(0)
    for j in range(local):

        @pl.when(needed[j])
        def _(j=j, slot=slot):
            sum_ref[targets[j]] += jnp.dot(
                stacked(in_refs, slot), (head_ref[j] if j < half else tail_ref[j - half]), preferred_element_type=F32
            )

        slot = slot + needed[j].astype(jnp.int32)
    for s, out_ref in enumerate(out_refs):
        out_ref[...] = sum_ref[:, s * cells_y : (s + 1) * cells_y, :].astype(BF16)


def to_fine_kernel(group, level_ref, link_ref, head_ref, tail_ref, *refs):
    in_refs, out_refs = refs[:group], refs[group : 2 * group]
    _, _, lower_differs, _ = place(level_ref)
    half = head_ref.shape[0]
    local = half + tail_ref.shape[0]
    cells_y = in_refs[0].shape[1]
    first = lax.axis_index("gy") * local
    active = (first >= HALF_F) == lower_differs

    @pl.when(active)
    def _():
        for j in range(local):
            product = jnp.dot(
                stacked(in_refs, link_ref[0, first + j]),
                (head_ref[j] if j < half else tail_ref[j - half]),
                preferred_element_type=F32,
            ).astype(BF16)
            for s, out_ref in enumerate(out_refs):
                out_ref[j] = product[s * cells_y : (s + 1) * cells_y, :]


def load_kernel(start, stop, level_ref, link_ref, values_ref, role_ref, held_ref, sems):
    _, own, lower_differs, upper_differs = place(level_ref)
    local = values_ref.shape[1]
    first = lax.axis_index("gy") * local
    fine = own == 1
    source = jnp.where(fine, 0, 1)
    differs = lower_differs | upper_differs

    def needed(j):
        coarse = (link_ref[1, first + j] >= HALF_C) == lower_differs
        here = jnp.where(fine, (first >= HALF_F) == lower_differs, coarse)
        return here & differs

    def copy(j):
        at = j - start
        return pltpu.make_async_copy(values_ref.at[source, j], held_ref.at[at], sems.at[at])

    for j in range(start, stop):
        pl.when(needed(j))(lambda j=j: copy(j).start())

    counts = sizes(local)
    fine_role = len(counts) + jnp.where(lower_differs, 1, 2)
    role_ref[0] = jnp.where(differs & fine, fine_role, 0)

    @pl.when(differs & jnp.logical_not(fine) & (start == 0))
    def _():
        def most(h, worst):
            count = jnp.int32(0)
            for j in range(local):
                hit = (link_ref[1, h * local + j] >= HALF_C) == lower_differs
                count = count + hit.astype(jnp.int32)
            return jnp.maximum(worst, count)

        worst = lax.fori_loop(0, VBF // local, most, jnp.int32(0))
        role = jnp.int32(1)
        for size in counts[:-1]:
            role = role + (worst > size).astype(jnp.int32)
        role_ref[0] = role

    for j in range(start, stop):
        pl.when(needed(j))(lambda j=j: copy(j).wait())


def load(levels, links, values, start, stop):
    return pl.pallas_call(
        functools.partial(load_kernel, start, stop),
        name="load",
        out_shape=(
            jax.ShapeDtypeStruct((1,), jnp.int32),
            jax.ShapeDtypeStruct((stop - start,) + values.shape[2:], BF16),
        ),
        in_specs=[SMEM, SMEM, HBM],
        out_specs=(SMEM, VMEM),
        scratch_shapes=[pltpu.SemaphoreType.DMA((stop - start,))],
        cost_estimate=pl.CostEstimate(
            flops=0, bytes_accessed=(stop - start) * BLK * BLK * 2, transcendentals=0
        ),
        compiler_params=pltpu.CompilerParams(vmem_limit_bytes=44 << 20),
    )(levels, links, values)


def multiply(kernel, levels, links, values, arrived, slots, scratch):
    group = len(arrived)
    local = sum(part.shape[0] for part in values)
    out = jax.ShapeDtypeStruct((slots,) + arrived[0].shape[1:], BF16)
    return pl.pallas_call(
        functools.partial(kernel, group),
        name=kernel.__name__,
        out_shape=(out,) * group,
        in_specs=[SMEM, SMEM, VMEM, VMEM] + [VMEM] * group,
        out_specs=(VMEM,) * group,
        scratch_shapes=scratch,
        cost_estimate=pl.CostEstimate(
            flops=2 * local * 32 * BLK * BLK, bytes_accessed=2 * local * BLK * BLK, transcendentals=0
        ),
        compiler_params=pltpu.CompilerParams(vmem_limit_bytes=24 << 20),
    )(levels, links, *values, *arrived)


def finish_kernel(role, group, level_ref, base_ref, held_ref, *refs):
    in_refs, out_ref, done_ref, sems = refs[:-3], refs[-3], refs[-2], refs[-1]
    _, _, _, upper_differs = place(level_ref)
    me = lax.axis_index("gy")
    parts = sems.shape[0]
    side, spacing, count = (
        (SC, spacing_coarse, HALF_C) if role == 1 else (SF, spacing_fine, HALF_F)
    )
    whole = count * BLK
    part = whole // parts
    centre = (side - 1) * 0.5

    def flush(index):
        start = index * part + jnp.where(upper_differs, 0, whole)
        at = pl.ds(pl.multiple_of(start, part), part)
        return pltpu.make_async_copy(
            done_ref.at[:, pl.ds(pl.multiple_of(index * part, part), part)],
            out_ref.at[:, at],
            sems.at[index],
        )

    first_plane = jnp.where(upper_differs, 0, side // 2)
    if role == 1:
        width = side * side
        for o in range(HALF_C):
            ghost = in_refs[0][o].astype(F32)
            for ref in in_refs[1:]:
                ghost = ghost + ref[o].astype(F32)
            for k in range(BLK // width):
                plane = lax.convert_element_type(first_plane + o * (BLK // width) + k, F32)
                push = cfl_ratio * spacing * jnp.abs(plane - centre)
                at = slice(o * BLK + k * width, o * BLK + (k + 1) * width)
                done_ref[:, at] = base_ref[:, at] + push * ghost[:, k * width : (k + 1) * width]
        flush(0).start()
        flush(0).wait()
        return

    offset = jnp.where(upper_differs, 0, HALF_F)
    for s, ref in zip(order(group), in_refs):
        local = ref.shape[0]
        first = peer(me, s, group) * local - offset

        @pl.when((first >= 0) & (first < HALF_F))
        def _(ref=ref, first=first, local=local):
            for j in range(local):
                slot = first + j
                plane = lax.convert_element_type(first_plane + slot // 2, F32)
                push = cfl_ratio * spacing * jnp.abs(plane - centre)
                at = pl.ds(pl.multiple_of(slot * BLK, BLK), BLK)
                done_ref[:, at] = base_ref[:, at] + push * ref[j].astype(F32)
            flush(lax.div(first, local)).start()

    for index in range(parts):
        flush(index).wait()


def finish(role, levels, base, held, arrived):
    group = len(arrived)
    rows_n = base.shape[0]
    parts = 1 if role == 1 else group // 2
    whole = NVC // 2 if role == 1 else NVF // 2
    return pl.pallas_call(
        functools.partial(finish_kernel, role, group),
        name="finish",
        out_shape=jax.ShapeDtypeStruct(held.shape, F32),
        in_specs=[SMEM, VMEM, HBM] + [VMEM] * group,
        out_specs=HBM,
        scratch_shapes=[pltpu.VMEM((rows_n, whole), F32), pltpu.SemaphoreType.DMA((parts,))],
        input_output_aliases={2: 0},
        cost_estimate=pl.CostEstimate(flops=10**6, bytes_accessed=10**6, transcendentals=0),
        compiler_params=pltpu.CompilerParams(vmem_limit_bytes=8 << 20),
    )(levels, base, held, *arrived)


def on_device(distribution, relax_rate, block_level, block_link, remap_values):
    blocks, group = lax.axis_size("gx"), lax.axis_size("gy")
    cells_y = distribution.shape[1]
    local = remap_values.shape[1]
    cells = distribution[0]

    def exchange(value, parity):
        pairs = []
        for low in range(parity, blocks - 1, 2):
            for y in range(group):
                here, there = low * group + y, (low + 1) * group + y
                pairs += [(here, there), (there, here)]
        return lax.ppermute(value, BOTH, pairs)

    everyone = range(group)

    def around(outgoing, sources=everyone, targets=everyone, rows=False):
        arrived = []
        for s, value in zip(order(group), outgoing):
            pairs = [
                (i, peer(i, s, group))
                for i in everyone
                if (i in sources and peer(i, s, group) in targets)
                or (rows and abs(i - peer(i, s, group)) == 1)
            ]
            arrived.append(lax.ppermute(value, "gy", pairs) if s and pairs else value)
        return arrived

    even, odd = prepare(block_level, block_link, cells)
    odd = exchange(odd, 1)
    even = exchange(even, 0)
    role, head = load(block_level, block_link, remap_values, 0, local // 2)
    edges = edge_rows(block_level, cells)

    def settle(alone, rows):
        return relax(alone, block_level, relax_rate, cells, even, odd, rows)

    def alone():
        left = lax.ppermute(edges[0], "gy", [(i, i + 1) for i in range(group - 1)])
        right = lax.ppermute(edges[1], "gy", [(i + 1, i) for i in range(group - 1)])
        return settle(True, [left, right])[0]

    def remapped(kernel, slots, scratch, arrived):
        tail = load(block_level, block_link, remap_values, local // 2, local)[1]
        values = [head, tail]
        made = multiply(kernel, block_level, block_link, values, arrived, slots, scratch)
        rows = [piece for s, piece in zip(order(group), arrived) if s in near(group)]
        return made, settle(False, rows)

    def to_coarse(slots):
        outgoing = pieces(block_level, block_link, even, odd, edges, group, slots)
        sums = [pltpu.VMEM((HALF_C, group * cells_y, BLK), F32)]
        made, (out, base) = remapped(to_coarse_kernel, HALF_C, sums, around(outgoing))
        return finish(1, block_level, base, out, around(made))

    def to_fine(active):
        outgoing = coarse_pieces(block_level, even, odd, edges, group)
        arrived = around(outgoing, targets=active, rows=True)
        made, (out, base) = remapped(to_fine_kernel, local, [], arrived)
        return finish(2, block_level, base, out, around(made, sources=active))

    branches = [alone]
    for slots in sizes(local):
        branches.append(functools.partial(to_coarse, slots))
    for active in (range(group // 2, group), range(group // 2)):
        branches.append(functools.partial(to_fine, active))
    updated = lax.switch(role[0], branches)
    return updated[None]


def solution(mesh):
    in_specs = (P("gx", "gy", None), P("gx", "gy"), P(), P(), P(None, "gy", None, None))
    out_specs = P("gx", "gy", None)
    return jax.shard_map(
        on_device, mesh=mesh, in_specs=in_specs, out_specs=out_specs, check_vma=False
    )
```

```python
import functools
import math

import jax
import jax.numpy as jnp
from jax import lax
from jax.experimental import pallas as pl
from jax.experimental.pallas import tpu as pltpu
from jax.sharding import PartitionSpec as P

SC = 16
SF = 32
BLK = 512
NVC = 4096
NVF = 32768
VBC = NVC // BLK
VBF = NVF // BLK
HALF_F = VBF // 2
HALF_C = VBC // 2
CHUNKS = 8
PART = NVF // CHUNKS

cfl_ratio = 0.03
spacing_coarse = 0.5
spacing_fine = 0.4

BOTH = ("gx", "gy")
SMEM = pl.BlockSpec(memory_space=pltpu.SMEM)
VMEM = pl.BlockSpec(memory_space=pltpu.VMEM)
HBM = pl.BlockSpec(memory_space=pltpu.HBM)
F32 = jnp.float32
BF16 = jnp.bfloat16


def place(level_ref):
    block = lax.axis_index("gx")
    own = level_ref[block]
    lower = level_ref[jnp.maximum(block - 1, 0)]
    upper = level_ref[jnp.minimum(block + 1, level_ref.shape[0] - 1)]
    return block, own, lower != own, upper != own


def peer(me, step, group):
    if group & (group - 1):
        raise ValueError(group)
    return me ^ step


def order(group):
    return sorted(range(group), key=lambda s: (s == 1, s))


def entry(group):
    return sorted(range(group), key=lambda s: (s > 0, s == group - 1, s != group // 2, s))


def near(group):
    return [s for s in entry(group) if s and not s & (s + 1)]


def sizes(local):
    return [max(1, (5 * local) // 8), max(1, (3 * local) // 4), local]


def block_at(ref, index):
    return ref[:, pl.ds(pl.multiple_of(index * BLK, BLK), BLK)]


def prepare_kernel(
    level_ref, link_ref, cells_ref, even_ref, odd_ref, index_ref, held_ref, sems
):
    block, own, lower_differs, upper_differs = place(level_ref)
    fine = own == 1
    on_even = block % 2 == 0
    per = VBF // CHUNKS

    def fetch(chunk):
        at = pl.ds(chunk * PART, PART)
        return pltpu.make_async_copy(cells_ref.at[:, at], held_ref.at[:, at], sems.at[chunk])

    def put(target_ref, slot, index):
        target_ref[slot] = block_at(held_ref, index).astype(BF16)

    fetch(0).start()

    @pl.when(jnp.logical_not(fine))
    def _():
        fetch(0).wait()
        for target_ref, going_up in ((odd_ref, jnp.logical_not(on_even)), (even_ref, on_even)):
            differs = jnp.where(going_up, upper_differs, lower_differs)
            start = jnp.where(going_up & jnp.logical_not(differs), HALF_C, 0)
            for j in range(VBC):
                put(target_ref, j, jnp.minimum(start + j, VBC - 1))

    @pl.when(fine)
    def _():
        for chunk in range(1, CHUNKS):
            fetch(chunk).start()

        @pl.when(lower_differs | upper_differs)
        def _():
            def look(f, count):
                index_ref[count] = f
                hit = (link_ref[1, f] >= HALF_C) == upper_differs
                return count + hit.astype(jnp.int32)

            lax.fori_loop(0, VBF, look, jnp.int32(0), unroll=8)

        for chunk in range(CHUNKS):
            fetch(chunk).wait()
            lower_half = chunk < CHUNKS // 2
            for target_ref, going_up in (
                (odd_ref, jnp.logical_not(on_even)),
                (even_ref, on_even),
            ):
                differs = jnp.where(going_up, upper_differs, lower_differs)

                @pl.when(jnp.logical_not(differs) & (going_up != lower_half))
                def _(target_ref=target_ref, chunk=chunk):
                    for j in range(per):
                        put(target_ref, (chunk * per + j) % HALF_F, chunk * per + j)

        for target_ref, going_up in ((odd_ref, jnp.logical_not(on_even)), (even_ref, on_even)):

            @pl.when(jnp.where(going_up, upper_differs, lower_differs))
            def _(target_ref=target_ref):
                def copy(j, carry):
                    put(target_ref, j, index_ref[j])
                    return carry

                lax.fori_loop(0, HALF_F, copy, 0, unroll=8)


def prepare(levels, links, cells):
    half = jax.ShapeDtypeStruct((HALF_F, cells.shape[0], BLK), BF16)
    return pl.pallas_call(
        prepare_kernel,
        name="prepare",
        out_shape=(half, half),
        in_specs=[SMEM, SMEM, HBM],
        out_specs=(VMEM,) * 2,
        scratch_shapes=[
            pltpu.SMEM((VBF + 1,), jnp.int32),
            pltpu.VMEM(cells.shape, F32),
            pltpu.SemaphoreType.DMA((CHUNKS,)),
        ],
        cost_estimate=pl.CostEstimate(flops=10**6, bytes_accessed=2 * 10**6, transcendentals=0),
        compiler_params=pltpu.CompilerParams(vmem_limit_bytes=44 << 20),
    )(levels, links, cells)


def rows_kernel(level_ref, cells_ref, ahead_ref, back_ref, row_ref):
    _, own, _, _ = place(level_ref)
    cells_y = cells_ref.shape[0]

    def rows(target_ref, row, parity):
        @pl.when(own == 1)
        def _():
            for i in range(HALF_F):
                row_ref[i : i + 1, :] = cells_ref[
                    row : row + 1, (2 * i + parity) * BLK : (2 * i + parity + 1) * BLK
                ]

        @pl.when(own != 1)
        def _():
            for i in range(VBC):
                row_ref[i : i + 1, :] = cells_ref[row : row + 1, i * BLK : (i + 1) * BLK]

        target_ref[...] = row_ref[...].astype(BF16)

    rows(ahead_ref, cells_y - 1, 1)
    rows(back_ref, 0, 0)


def edge_rows(levels, cells):
    row = jax.ShapeDtypeStruct((HALF_F, BLK), BF16)
    return pl.pallas_call(
        rows_kernel,
        name="edge_rows",
        out_shape=(row, row),
        in_specs=[SMEM, VMEM],
        out_specs=(VMEM, VMEM),
        scratch_shapes=[pltpu.VMEM((HALF_F, BLK), F32)],
        cost_estimate=pl.CostEstimate(flops=10**6, bytes_accessed=2 * 10**6, transcendentals=0),
        compiler_params=pltpu.CompilerParams(vmem_limit_bytes=8 << 20),
    )(levels, cells)


def ghost_at(ref, index):
    return ref[index].astype(F32)


def relax_kernel(
    level,
    level_ref,
    rate_ref,
    cells_ref,
    even_ref,
    odd_ref,
    *refs,
):
    side_ref, done_ref, sems = refs[-3:]
    results = 1 if level is None else 2
    row_refs, out_ref = refs[: -3 - results], refs[-3 - results]
    block, own, lower_differs, upper_differs = place(level_ref)
    on_even = block % 2 == 0
    rows_n = cells_ref.shape[0]

    def flush(chunk):
        at = pl.ds(chunk * PART, PART)
        return pltpu.make_async_copy(done_ref.at[:, at], out_ref.at[:, at], sems.at[chunk])

    def run(side, spacing):
        width = side * side
        mid = width // 2
        middle = side // 2
        centre = (side - 1) * 0.5
        lane = lax.broadcasted_iota(jnp.int32, (rows_n, width), 1)
        along_y = spacing * ((lane // side).astype(F32) - centre)
        along_z = spacing * ((lane % side).astype(F32) - centre)

        def span(i):
            start = i * width
            return pl.ds(start if isinstance(i, int) else pl.multiple_of(start, width), width)

        def speed_at(i):
            return spacing * (lax.convert_element_type(i, F32) - centre)

        def gather(i, sums):
            total, first, second = sums
            plane = cells_ref[:, span(i)]
            speed = speed_at(i)
            return total + plane, first + plane * speed, second + plane * (speed * speed)

        zero = jnp.zeros((rows_n, width), F32)
        total, first, second = lax.fori_loop(0, side, gather, (zero, zero, zero), unroll=4)

        def over(value):
            return jnp.broadcast_to(jnp.sum(value, axis=1, keepdims=True), (rows_n, 128))

        weight = spacing * spacing * spacing
        density = weight * over(total)
        scale = weight / density
        mean_x = scale * over(first)
        mean_y = scale * over(total * along_y)
        mean_z = scale * over(total * along_z)
        square = scale * over(second + total * (along_y * along_y + along_z * along_z))
        heat = (square - mean_x * mean_x - mean_y * mean_y - mean_z * mean_z) / 3.0
        row = lax.broadcasted_iota(jnp.int32, (rows_n, 128), 0)
        rate = jnp.zeros((rows_n, 128), F32)
        for r in range(rows_n):
            rate = jnp.where(row == r, rate_ref[0, r], rate)
        spread = 2.0 * math.pi * heat
        peak = rate * density / (spread * jnp.sqrt(spread))
        inverse = -0.5 / heat

        def wide(value):
            return jnp.concatenate([value] * (width // 128), axis=1)

        off_y = along_y - wide(mean_y)
        off_z = along_z - wide(mean_z)
        across = wide(peak) * jnp.exp((off_y * off_y + off_z * off_z) * wide(inverse))
        drift = cfl_ratio * jnp.abs(along_y)
        keep = (1.0 - wide(rate)) - drift
        wide_row = lax.broadcasted_iota(jnp.int32, (rows_n, mid), 0)

        def update(i, upward):
            plane = cells_ref[:, span(i)]
            speed = speed_at(i)
            off_x = speed - mean_x
            along = wide(jnp.exp(off_x * off_x * inverse))
            take_even = on_even == upward
            if side == SF:
                right = side_ref[1, pl.ds(i, 1), :]
                left = side_ref[0, pl.ds(i, 1), :]
                slot = 2 * (i if upward else i - middle)
                ghosts = []
                for half in range(2):
                    a, b = ghost_at(even_ref, slot + half), ghost_at(odd_ref, slot + half)
                    ghosts.append(jnp.where(take_even, a, b))
                ghost = jnp.concatenate(ghosts, axis=1)
            else:
                slot, offset = i // 2, (i % 2) * width
                right = side_ref[1, slot : slot + 1, offset : offset + mid]
                left = side_ref[0, slot : slot + 1, offset + mid : offset + width]
                slot = slot if upward else slot - HALF_C
                a, b = ghost_at(even_ref, slot), ghost_at(odd_ref, slot)
                ghost = jnp.where(take_even, a, b)[:, offset : offset + width]
            if level is not None:
                ghost = jnp.where(upper_differs if upward else lower_differs, 0.0, ghost)
            low, high = plane[:, :mid], plane[:, mid:]
            beyond = jnp.where(wide_row == rows_n - 1, right, pltpu.roll(low, rows_n - 1, 0))
            before = jnp.where(wide_row == 0, left, pltpu.roll(high, 1, 0))
            beside = jnp.concatenate([beyond, before], axis=1)
            push = cfl_ratio * jnp.abs(speed)
            done_ref[:, span(i)] = (
                plane * (keep - push) + push * ghost + drift * beside + along * across
            )

        if side == SF:
            each = side // CHUNKS
            for chunk in range(CHUNKS):
                upward = chunk < CHUNKS // 2

                def step(k, carry, chunk=chunk, upward=upward):
                    update(chunk * each + k, upward)
                    return carry

                lax.fori_loop(0, each, step, 0, unroll=4)
                flush(chunk).start()
        else:
            for i in range(side):
                update(i, i < middle)
            flush(0).start()
            done_ref[:, NVC:] = jnp.zeros((rows_n, NVF - NVC), F32)
            for chunk in range(1, CHUNKS):
                flush(chunk).start()

    if level is None:
        for k, row_ref in enumerate(row_refs):
            side_ref[k] = row_ref[...].astype(F32)
    else:
        side_ref[...] = jnp.zeros_like(side_ref)
        me, group = lax.axis_index("gy"), lax.axis_size("gy")
        for s, ref in zip(entry(group)[1:], row_refs):
            if s not in near(group):
                continue
            first = ref.shape[0] - ROWS
            for k, by in ((0, -1), (1, 1)):

                @pl.when(peer(me, s, group) == me + by)
                def _(ref=ref, k=k, first=first):
                    for j in range(ROWS):
                        side_ref[k, 8 * j : 8 * j + 8, :] = ref[first + j].astype(F32)

    if level is None:

        @pl.when(own == 1)
        def _():
            run(SF, spacing_fine)

        @pl.when(own != 1)
        def _():
            run(SC, spacing_coarse)

    elif level == 1:
        run(SF, spacing_fine)
    else:
        run(SC, spacing_coarse)

    if level is not None:
        base_ref = refs[-4]
        split = (NVF if level == 1 else NVC) // 2

        @pl.when(upper_differs)
        def _():
            base_ref[...] = done_ref[:, :split]

        @pl.when(jnp.logical_not(upper_differs))
        def _():
            base_ref[...] = done_ref[:, split : 2 * split]

    for chunk in range(CHUNKS):
        flush(chunk).wait()


def relax(level, levels, rate, cells, even, odd, rows):
    out = jax.ShapeDtypeStruct(cells.shape, F32)
    half = jax.ShapeDtypeStruct((cells.shape[0], (NVF if level == 1 else NVC) // 2), F32)
    return pl.pallas_call(
        functools.partial(relax_kernel, level),
        name="relax",
        out_shape=(out,) if level is None else (out, half),
        in_specs=[SMEM, SMEM, VMEM, VMEM, VMEM] + [VMEM] * len(rows),
        out_specs=(HBM,) if level is None else (HBM, VMEM),
        scratch_shapes=[
            pltpu.VMEM((2, HALF_F, BLK), F32),
            pltpu.VMEM(cells.shape, F32),
            pltpu.SemaphoreType.DMA((CHUNKS,)),
        ],
        cost_estimate=pl.CostEstimate(flops=10**7, bytes_accessed=4 * 10**6, transcendentals=10**5),
        compiler_params=pltpu.CompilerParams(vmem_limit_bytes=16 << 20),
    )(levels, rate, cells, even, odd, *rows)


ROWS = HALF_F // 8


def attach(group, ahead_ref, back_ref, out_refs):
    me = lax.axis_index("gy")
    for s, out_ref in zip(entry(group), out_refs):
        if s not in near(group):
            continue
        first = out_ref.shape[0] - ROWS
        for source_ref, by in ((ahead_ref, 1), (back_ref, -1)):

            @pl.when(peer(me, s, group) == me + by)
            def _(out_ref=out_ref, source_ref=source_ref, first=first):
                for j in range(ROWS):
                    out_ref[first + j] = source_ref[8 * j : 8 * j + 8, :]


def coarse_kernel(group, level_ref, even_ref, odd_ref, ahead_ref, back_ref, *out_refs):
    block, _, lower_differs, _ = place(level_ref)
    use_even = (block % 2 == 0) != lower_differs
    for j in range(VBC):
        a, b = even_ref[j].astype(F32), odd_ref[j].astype(F32)
        piece = jnp.where(use_even, a, b).astype(BF16)
        for out_ref in out_refs:
            out_ref[j] = piece
    attach(group, ahead_ref, back_ref, out_refs)


def pieces_kernel(group, level_ref, link_ref, even_ref, odd_ref, ahead_ref, back_ref, *refs):
    out_refs, start_ref = refs[:-1], refs[-1]
    block, own, lower_differs, _ = place(level_ref)
    me = lax.axis_index("gy")
    local = VBF // group
    slots = out_refs[0].shape[0]
    use_even = (block % 2 == 0) != lower_differs

    def count(h, total):
        start_ref[h] = total
        for j in range(local):
            hit = (link_ref[1, h * local + j] >= HALF_C) == lower_differs
            total = total + hit.astype(jnp.int32)
        return total

    lax.fori_loop(0, group, count, jnp.int32(0))

    def fill(source_ref):
        for s, out_ref in zip(entry(group), out_refs):
            start = start_ref[peer(me, s, group)]
            for j in range(slots):
                out_ref[j] = source_ref[jnp.minimum(start + j, HALF_F - 1)]

    @pl.when(use_even)
    def _():
        fill(even_ref)

    @pl.when(jnp.logical_not(use_even))
    def _():
        fill(odd_ref)

    attach(group, ahead_ref, back_ref, out_refs)


def outgoing_shapes(slots, group, rows_n):
    return tuple(
        jax.ShapeDtypeStruct((slots + (ROWS if s else 0), rows_n, BLK), BF16)
        for s in entry(group)
    )


def coarse_pieces(levels, even, odd, edges, group):
    return pl.pallas_call(
        functools.partial(coarse_kernel, group),
        name="coarse_pieces",
        out_shape=outgoing_shapes(VBC, group, even.shape[1]),
        in_specs=[SMEM] + [VMEM] * 4,
        out_specs=(VMEM,) * group,
        cost_estimate=pl.CostEstimate(flops=10**5, bytes_accessed=10**6, transcendentals=0),
        compiler_params=pltpu.CompilerParams(vmem_limit_bytes=8 << 20),
    )(levels, even, odd, *edges)


def pieces(levels, links, even, odd, edges, group, slots):
    return pl.pallas_call(
        functools.partial(pieces_kernel, group),
        name="pieces",
        out_shape=outgoing_shapes(slots, group, even.shape[1]),
        in_specs=[SMEM, SMEM] + [VMEM] * 4,
        out_specs=(VMEM,) * group,
        scratch_shapes=[pltpu.SMEM((group,), jnp.int32)],
        cost_estimate=pl.CostEstimate(flops=10**5, bytes_accessed=10**6, transcendentals=0),
        compiler_params=pltpu.CompilerParams(vmem_limit_bytes=8 << 20),
    )(levels, links, even, odd, *edges)


def stacked(refs, index):
    return jnp.concatenate([ref[index].astype(F32) for ref in refs], axis=0).astype(BF16)


def to_coarse_kernel(group, level_ref, link_ref, head_ref, tail_ref, *refs):
    in_refs, out_refs, sum_ref = refs[:group], refs[group : 2 * group], refs[-1]
    _, _, lower_differs, _ = place(level_ref)
    half = head_ref.shape[0]
    local = half + tail_ref.shape[0]
    cells_y = in_refs[0].shape[1]
    first = lax.axis_index("gy") * local
    offset = jnp.where(lower_differs, HALF_C, 0)

    targets = [link_ref[1, first + j] - offset for j in range(local)]
    needed = [(t >= 0) & (t < HALF_C) for t in targets]
    sum_ref[...] = jnp.zeros_like(sum_ref)
    slot = jnp.int32(0)
    for j in range(local):

        @pl.when(needed[j])
        def _(j=j, slot=slot):
            sum_ref[targets[j]] += jnp.dot(
                stacked(in_refs, slot), (head_ref[j] if j < half else tail_ref[j - half]), preferred_element_type=F32
            )

        slot = slot + needed[j].astype(jnp.int32)
    for s, out_ref in enumerate(out_refs):
        out_ref[...] = sum_ref[:, s * cells_y : (s + 1) * cells_y, :].astype(BF16)


def to_fine_kernel(group, level_ref, link_ref, head_ref, tail_ref, *refs):
    in_refs, out_refs = refs[:group], refs[group : 2 * group]
    _, _, lower_differs, _ = place(level_ref)
    half = head_ref.shape[0]
    local = half + tail_ref.shape[0]
    cells_y = in_refs[0].shape[1]
    first = lax.axis_index("gy") * local
    active = (first >= HALF_F) == lower_differs

    @pl.when(active)
    def _():
        for j in range(local):
            product = jnp.dot(
                stacked(in_refs, link_ref[0, first + j]),
                (head_ref[j] if j < half else tail_ref[j - half]),
                preferred_element_type=F32,
            ).astype(BF16)
            for s, out_ref in enumerate(out_refs):
                out_ref[j] = product[s * cells_y : (s + 1) * cells_y, :]


def load_kernel(start, stop, level_ref, link_ref, values_ref, role_ref, held_ref, sems):
    _, own, lower_differs, upper_differs = place(level_ref)
    local = values_ref.shape[1]
    first = lax.axis_index("gy") * local
    fine = own == 1
    source = jnp.where(fine, 0, 1)
    differs = lower_differs | upper_differs

    def needed(j):
        coarse = (link_ref[1, first + j] >= HALF_C) == lower_differs
        here = jnp.where(fine, (first >= HALF_F) == lower_differs, coarse)
        return here & differs

    def copy(j):
        at = j - start
        return pltpu.make_async_copy(values_ref.at[source, j], held_ref.at[at], sems.at[at])

    for j in range(start, stop):
        pl.when(needed(j))(lambda j=j: copy(j).start())

    counts = sizes(local)
    fine_role = len(counts) + jnp.where(lower_differs, 1, 2)
    role_ref[0] = jnp.where(differs & fine, fine_role, 0)

    @pl.when(differs & jnp.logical_not(fine) & (start == 0))
    def _():
        def most(h, worst):
            count = jnp.int32(0)
            for j in range(local):
                hit = (link_ref[1, h * local + j] >= HALF_C) == lower_differs
                count = count + hit.astype(jnp.int32)
            return jnp.maximum(worst, count)

        worst = lax.fori_loop(0, VBF // local, most, jnp.int32(0))
        role = jnp.int32(1)
        for size in counts[:-1]:
            role = role + (worst > size).astype(jnp.int32)
        role_ref[0] = role

    for j in range(start, stop):
        pl.when(needed(j))(lambda j=j: copy(j).wait())


def load(levels, links, values, start, stop):
    return pl.pallas_call(
        functools.partial(load_kernel, start, stop),
        name="load",
        out_shape=(
            jax.ShapeDtypeStruct((1,), jnp.int32),
            jax.ShapeDtypeStruct((stop - start,) + values.shape[2:], BF16),
        ),
        in_specs=[SMEM, SMEM, HBM],
        out_specs=(SMEM, VMEM),
        scratch_shapes=[pltpu.SemaphoreType.DMA((stop - start,))],
        cost_estimate=pl.CostEstimate(
            flops=0, bytes_accessed=(stop - start) * BLK * BLK * 2, transcendentals=0
        ),
        compiler_params=pltpu.CompilerParams(vmem_limit_bytes=44 << 20),
    )(levels, links, values)


def multiply(kernel, levels, links, values, arrived, slots, scratch):
    group = len(arrived)
    local = sum(part.shape[0] for part in values)
    out = jax.ShapeDtypeStruct((slots,) + arrived[0].shape[1:], BF16)
    return pl.pallas_call(
        functools.partial(kernel, group),
        name=kernel.__name__,
        out_shape=(out,) * group,
        in_specs=[SMEM, SMEM, VMEM, VMEM] + [VMEM] * group,
        out_specs=(VMEM,) * group,
        scratch_shapes=scratch,
        cost_estimate=pl.CostEstimate(
            flops=2 * local * 32 * BLK * BLK, bytes_accessed=2 * local * BLK * BLK, transcendentals=0
        ),
        compiler_params=pltpu.CompilerParams(vmem_limit_bytes=24 << 20),
    )(levels, links, *values, *arrived)


def finish_kernel(role, group, level_ref, base_ref, held_ref, *refs):
    in_refs, out_ref, done_ref, sems = refs[:-3], refs[-3], refs[-2], refs[-1]
    _, _, _, upper_differs = place(level_ref)
    me = lax.axis_index("gy")
    parts = sems.shape[0]
    side, spacing, count = (
        (SC, spacing_coarse, HALF_C) if role == 1 else (SF, spacing_fine, HALF_F)
    )
    whole = count * BLK
    part = whole // parts
    centre = (side - 1) * 0.5

    def flush(index):
        start = index * part + jnp.where(upper_differs, 0, whole)
        at = pl.ds(pl.multiple_of(start, part), part)
        return pltpu.make_async_copy(
            done_ref.at[:, pl.ds(pl.multiple_of(index * part, part), part)],
            out_ref.at[:, at],
            sems.at[index],
        )

    first_plane = jnp.where(upper_differs, 0, side // 2)
    if role == 1:
        width = side * side
        for o in range(HALF_C):
            ghost = in_refs[0][o].astype(F32)
            for ref in in_refs[1:]:
                ghost = ghost + ref[o].astype(F32)
            for k in range(BLK // width):
                plane = lax.convert_element_type(first_plane + o * (BLK // width) + k, F32)
                push = cfl_ratio * spacing * jnp.abs(plane - centre)
                at = slice(o * BLK + k * width, o * BLK + (k + 1) * width)
                done_ref[:, at] = base_ref[:, at] + push * ghost[:, k * width : (k + 1) * width]
        flush(0).start()
        flush(0).wait()
        return

    offset = jnp.where(upper_differs, 0, HALF_F)
    for s, ref in zip(order(group), in_refs):
        local = ref.shape[0]
        first = peer(me, s, group) * local - offset

        @pl.when((first >= 0) & (first < HALF_F))
        def _(ref=ref, first=first, local=local):
            for j in range(local):
                slot = first + j
                plane = lax.convert_element_type(first_plane + slot // 2, F32)
                push = cfl_ratio * spacing * jnp.abs(plane - centre)
                at = pl.ds(pl.multiple_of(slot * BLK, BLK), BLK)
                done_ref[:, at] = base_ref[:, at] + push * ref[j].astype(F32)
            flush(lax.div(first, local)).start()

    for index in range(parts):
        flush(index).wait()


def finish(role, levels, base, held, arrived):
    group = len(arrived)
    rows_n = base.shape[0]
    parts = 1 if role == 1 else group // 2
    whole = NVC // 2 if role == 1 else NVF // 2
    return pl.pallas_call(
        functools.partial(finish_kernel, role, group),
        name="finish",
        out_shape=jax.ShapeDtypeStruct(held.shape, F32),
        in_specs=[SMEM, VMEM, HBM] + [VMEM] * group,
        out_specs=HBM,
        scratch_shapes=[pltpu.VMEM((rows_n, whole), F32), pltpu.SemaphoreType.DMA((parts,))],
        input_output_aliases={2: 0},
        cost_estimate=pl.CostEstimate(flops=10**6, bytes_accessed=10**6, transcendentals=0),
        compiler_params=pltpu.CompilerParams(vmem_limit_bytes=8 << 20),
    )(levels, base, held, *arrived)


def on_device(distribution, relax_rate, block_level, block_link, remap_values):
    blocks, group = lax.axis_size("gx"), lax.axis_size("gy")
    cells_y = distribution.shape[1]
    local = remap_values.shape[1]
    cells = distribution[0]

    def exchange(value, parity):
        pairs = []
        for low in range(parity, blocks - 1, 2):
            for y in range(group):
                here, there = low * group + y, (low + 1) * group + y
                pairs += [(here, there), (there, here)]
        return lax.ppermute(value, BOTH, pairs)

    everyone = range(group)

    def around(steps, outgoing, sources=everyone, targets=everyone, rows=False):
        arrived = []
        for s, value in zip(steps, outgoing):
            pairs = [
                (i, peer(i, s, group))
                for i in everyone
                if (i in sources and peer(i, s, group) in targets)
                or (rows and abs(i - peer(i, s, group)) == 1)
            ]
            arrived.append(lax.ppermute(value, "gy", pairs) if s and pairs else value)
        return arrived

    even, odd = prepare(block_level, block_link, cells)
    odd = exchange(odd, 1)
    even = exchange(even, 0)
    role, head = load(block_level, block_link, remap_values, 0, local // 2)
    edges = edge_rows(block_level, cells)

    def settle(level, rows):
        return relax(level, block_level, relax_rate, cells, even, odd, rows)

    def alone():
        left = lax.ppermute(edges[0], "gy", [(i, i + 1) for i in range(group - 1)])
        right = lax.ppermute(edges[1], "gy", [(i + 1, i) for i in range(group - 1)])
        return settle(None, [left, right])[0]

    def remapped(level, kernel, slots, scratch, arrived):
        tail = load(block_level, block_link, remap_values, local // 2, local)[1]
        values = [head, tail]
        made = multiply(kernel, block_level, block_link, values, arrived, slots, scratch)
        made = dict(zip(entry(group), made))
        return [made[s] for s in order(group)], settle(level, arrived[1:])

    def to_coarse(slots):
        outgoing = pieces(block_level, block_link, even, odd, edges, group, slots)
        sums = [pltpu.VMEM((HALF_C, group * cells_y, BLK), F32)]
        made, (out, base) = remapped(0, to_coarse_kernel, HALF_C, sums, around(entry(group), outgoing))
        return finish(1, block_level, base, out, around(order(group), made))

    def to_fine(active):
        outgoing = coarse_pieces(block_level, even, odd, edges, group)
        arrived = around(entry(group), outgoing, targets=active, rows=True)
        made, (out, base) = remapped(1, to_fine_kernel, local, [], arrived)
        return finish(2, block_level, base, out, around(order(group), made, sources=active))

    branches = [alone]
    for slots in sizes(local):
        branches.append(functools.partial(to_coarse, slots))
    for active in (range(group // 2, group), range(group // 2)):
        branches.append(functools.partial(to_fine, active))
    updated = lax.switch(role[0], branches)
    return updated[None]


def solution(mesh):
    in_specs = (P("gx", "gy", None), P("gx", "gy"), P(), P(), P(None, "gy", None, None))
    out_specs = P("gx", "gy", None)
    return jax.shard_map(
        on_device, mesh=mesh, in_specs=in_specs, out_specs=out_specs, check_vma=False
    )
```

```python
import functools
import math

import jax
import jax.numpy as jnp
from jax import lax
from jax.experimental import pallas as pl
from jax.experimental.pallas import tpu as pltpu
from jax.sharding import PartitionSpec as P

SC = 16
SF = 32
BLK = 512
NVC = 4096
NVF = 32768
VBC = NVC // BLK
VBF = NVF // BLK
HALF_F = VBF // 2
HALF_C = VBC // 2
CHUNKS = 8
PART = NVF // CHUNKS

cfl_ratio = 0.03
spacing_coarse = 0.5
spacing_fine = 0.4

BOTH = ("gx", "gy")
SMEM = pl.BlockSpec(memory_space=pltpu.SMEM)
VMEM = pl.BlockSpec(memory_space=pltpu.VMEM)
HBM = pl.BlockSpec(memory_space=pltpu.HBM)
F32 = jnp.float32
BF16 = jnp.bfloat16


def place(level_ref):
    block = lax.axis_index("gx")
    own = level_ref[block]
    lower = level_ref[jnp.maximum(block - 1, 0)]
    upper = level_ref[jnp.minimum(block + 1, level_ref.shape[0] - 1)]
    return block, own, lower != own, upper != own


def peer(me, step, group):
    if group & (group - 1):
        raise ValueError(group)
    return me ^ step


def order(group):
    return sorted(range(group), key=lambda s: (s == 1, s))


def entry(group):
    return sorted(range(group), key=lambda s: (s > 0, s == group - 1, s != group // 2, s))


def near(group):
    return [s for s in entry(group) if s and not s & (s + 1)]


def sizes(local):
    return [max(1, (5 * local) // 8), max(1, (3 * local) // 4), local]


def block_at(ref, index):
    return ref[:, pl.ds(pl.multiple_of(index * BLK, BLK), BLK)]


def prepare_kernel(level_ref, link_ref, cells_ref, even_ref, odd_ref, index_ref):
    block, own, lower_differs, upper_differs = place(level_ref)
    fine = own == 1

    def fill(target_ref, going_up):
        differs = jnp.where(going_up, upper_differs, lower_differs)
        gathers = differs & fine

        @pl.when(gathers)
        def _():
            def look(f, count):
                index_ref[count] = f
                hit = (link_ref[1, f] >= HALF_C) == going_up
                return count + hit.astype(jnp.int32)

            lax.fori_loop(0, VBF, look, jnp.int32(0), unroll=8)

            def copy(j, carry):
                target_ref[j] = block_at(cells_ref, index_ref[j]).astype(BF16)
                return carry

            lax.fori_loop(0, HALF_F, copy, 0, unroll=8)

        @pl.when(fine & jnp.logical_not(differs))
        def _():
            start = jnp.where(going_up, HALF_F, 0)
            for j in range(HALF_F):
                target_ref[j] = block_at(cells_ref, start + j).astype(BF16)

        @pl.when(jnp.logical_not(fine))
        def _():
            start = jnp.where(going_up & jnp.logical_not(differs), HALF_C, 0)
            for j in range(VBC):
                target_ref[j] = block_at(cells_ref, start + j).astype(BF16)

    on_even = block % 2 == 0
    fill(odd_ref, jnp.logical_not(on_even))
    fill(even_ref, on_even)


def prepare(levels, links, cells):
    half = jax.ShapeDtypeStruct((HALF_F, cells.shape[0], BLK), BF16)
    return pl.pallas_call(
        prepare_kernel,
        name="prepare",
        out_shape=(half, half),
        in_specs=[SMEM, SMEM, VMEM],
        out_specs=(VMEM,) * 2,
        scratch_shapes=[pltpu.SMEM((VBF + 1,), jnp.int32)],
        cost_estimate=pl.CostEstimate(flops=10**6, bytes_accessed=2 * 10**6, transcendentals=0),
        compiler_params=pltpu.CompilerParams(vmem_limit_bytes=8 << 20),
    )(levels, links, cells)


def rows_kernel(level_ref, cells_ref, ahead_ref, back_ref, row_ref):
    _, own, _, _ = place(level_ref)
    cells_y = cells_ref.shape[0]

    def rows(target_ref, row, parity):
        @pl.when(own == 1)
        def _():
            for i in range(HALF_F):
                row_ref[i : i + 1, :] = cells_ref[
                    row : row + 1, (2 * i + parity) * BLK : (2 * i + parity + 1) * BLK
                ]

        @pl.when(own != 1)
        def _():
            for i in range(VBC):
                row_ref[i : i + 1, :] = cells_ref[row : row + 1, i * BLK : (i + 1) * BLK]

        target_ref[...] = row_ref[...].astype(BF16)

    rows(ahead_ref, cells_y - 1, 1)
    rows(back_ref, 0, 0)


def edge_rows(levels, cells):
    row = jax.ShapeDtypeStruct((HALF_F, BLK), BF16)
    return pl.pallas_call(
        rows_kernel,
        name="edge_rows",
        out_shape=(row, row),
        in_specs=[SMEM, VMEM],
        out_specs=(VMEM, VMEM),
        scratch_shapes=[pltpu.VMEM((HALF_F, BLK), F32)],
        cost_estimate=pl.CostEstimate(flops=10**6, bytes_accessed=2 * 10**6, transcendentals=0),
        compiler_params=pltpu.CompilerParams(vmem_limit_bytes=8 << 20),
    )(levels, cells)


def ghost_at(ref, index):
    return ref[index].astype(F32)


def relax_kernel(
    level,
    level_ref,
    rate_ref,
    cells_ref,
    even_ref,
    odd_ref,
    *refs,
):
    side_ref, done_ref, sems = refs[-3:]
    results = 1 if level is None else 2
    row_refs, out_ref = refs[: -3 - results], refs[-3 - results]
    block, own, lower_differs, upper_differs = place(level_ref)
    on_even = block % 2 == 0
    rows_n = cells_ref.shape[0]

    def flush(chunk):
        at = pl.ds(chunk * PART, PART)
        return pltpu.make_async_copy(done_ref.at[:, at], out_ref.at[:, at], sems.at[chunk])

    def run(side, spacing):
        width = side * side
        mid = width // 2
        middle = side // 2
        centre = (side - 1) * 0.5
        lane = lax.broadcasted_iota(jnp.int32, (rows_n, width), 1)
        along_y = spacing * ((lane // side).astype(F32) - centre)
        along_z = spacing * ((lane % side).astype(F32) - centre)

        def span(i):
            start = i * width
            return pl.ds(start if isinstance(i, int) else pl.multiple_of(start, width), width)

        def speed_at(i):
            return spacing * (lax.convert_element_type(i, F32) - centre)

        def gather(i, sums):
            total, first, second = sums
            plane = cells_ref[:, span(i)]
            speed = speed_at(i)
            return total + plane, first + plane * speed, second + plane * (speed * speed)

        zero = jnp.zeros((rows_n, width), F32)
        total, first, second = lax.fori_loop(0, side, gather, (zero, zero, zero), unroll=4)

        def over(value):
            return jnp.broadcast_to(jnp.sum(value, axis=1, keepdims=True), (rows_n, 128))

        weight = spacing * spacing * spacing
        density = weight * over(total)
        scale = weight / density
        mean_x = scale * over(first)
        mean_y = scale * over(total * along_y)
        mean_z = scale * over(total * along_z)
        square = scale * over(second + total * (along_y * along_y + along_z * along_z))
        heat = (square - mean_x * mean_x - mean_y * mean_y - mean_z * mean_z) / 3.0
        row = lax.broadcasted_iota(jnp.int32, (rows_n, 128), 0)
        rate = jnp.zeros((rows_n, 128), F32)
        for r in range(rows_n):
            rate = jnp.where(row == r, rate_ref[0, r], rate)
        spread = 2.0 * math.pi * heat
        peak = rate * density / (spread * jnp.sqrt(spread))
        inverse = -0.5 / heat

        def wide(value):
            return jnp.concatenate([value] * (width // 128), axis=1)

        off_y = along_y - wide(mean_y)
        off_z = along_z - wide(mean_z)
        across = wide(peak) * jnp.exp((off_y * off_y + off_z * off_z) * wide(inverse))
        drift = cfl_ratio * jnp.abs(along_y)
        keep = (1.0 - wide(rate)) - drift
        wide_row = lax.broadcasted_iota(jnp.int32, (rows_n, mid), 0)

        def update(i, upward):
            plane = cells_ref[:, span(i)]
            speed = speed_at(i)
            off_x = speed - mean_x
            along = wide(jnp.exp(off_x * off_x * inverse))
            take_even = on_even == upward
            if side == SF:
                right = side_ref[1, pl.ds(i, 1), :]
                left = side_ref[0, pl.ds(i, 1), :]
                slot = 2 * (i if upward else i - middle)
                ghosts = []
                for half in range(2):
                    a, b = ghost_at(even_ref, slot + half), ghost_at(odd_ref, slot + half)
                    ghosts.append(jnp.where(take_even, a, b))
                ghost = jnp.concatenate(ghosts, axis=1)
            else:
                slot, offset = i // 2, (i % 2) * width
                right = side_ref[1, slot : slot + 1, offset : offset + mid]
                left = side_ref[0, slot : slot + 1, offset + mid : offset + width]
                slot = slot if upward else slot - HALF_C
                a, b = ghost_at(even_ref, slot), ghost_at(odd_ref, slot)
                ghost = jnp.where(take_even, a, b)[:, offset : offset + width]
            if level is not None:
                ghost = jnp.where(upper_differs if upward else lower_differs, 0.0, ghost)
            low, high = plane[:, :mid], plane[:, mid:]
            beyond = jnp.where(wide_row == rows_n - 1, right, pltpu.roll(low, rows_n - 1, 0))
            before = jnp.where(wide_row == 0, left, pltpu.roll(high, 1, 0))
            beside = jnp.concatenate([beyond, before], axis=1)
            push = cfl_ratio * jnp.abs(speed)
            done_ref[:, span(i)] = (
                plane * (keep - push) + push * ghost + drift * beside + along * across
            )

        if side == SF:
            each = side // CHUNKS
            for chunk in range(CHUNKS):
                upward = chunk < CHUNKS // 2

                def step(k, carry, chunk=chunk, upward=upward):
                    update(chunk * each + k, upward)
                    return carry

                lax.fori_loop(0, each, step, 0, unroll=4)
                flush(chunk).start()
        else:
            for i in range(side):
                update(i, i < middle)
            flush(0).start()
            done_ref[:, NVC:] = jnp.zeros((rows_n, NVF - NVC), F32)
            for chunk in range(1, CHUNKS):
                flush(chunk).start()

    if level is None:
        for k, row_ref in enumerate(row_refs):
            side_ref[k] = row_ref[...].astype(F32)
    else:
        side_ref[...] = jnp.zeros_like(side_ref)
        me, group = lax.axis_index("gy"), lax.axis_size("gy")
        for s, ref in zip(entry(group)[1:], row_refs):
            if s not in near(group):
                continue
            first = ref.shape[0] - ROWS
            for k, by in ((0, -1), (1, 1)):

                @pl.when(peer(me, s, group) == me + by)
                def _(ref=ref, k=k, first=first):
                    for j in range(ROWS):
                        side_ref[k, 8 * j : 8 * j + 8, :] = ref[first + j].astype(F32)

    if level is None:

        @pl.when(own == 1)
        def _():
            run(SF, spacing_fine)

        @pl.when(own != 1)
        def _():
            run(SC, spacing_coarse)

    elif level == 1:
        run(SF, spacing_fine)
    else:
        run(SC, spacing_coarse)

    if level is not None:
        base_ref = refs[-4]
        split = (NVF if level == 1 else NVC) // 2

        @pl.when(upper_differs)
        def _():
            base_ref[...] = done_ref[:, :split]

        @pl.when(jnp.logical_not(upper_differs))
        def _():
            base_ref[...] = done_ref[:, split : 2 * split]

    for chunk in range(CHUNKS):
        flush(chunk).wait()


def relax(level, levels, rate, cells, even, odd, rows):
    out = jax.ShapeDtypeStruct(cells.shape, F32)
    half = jax.ShapeDtypeStruct((cells.shape[0], (NVF if level == 1 else NVC) // 2), F32)
    return pl.pallas_call(
        functools.partial(relax_kernel, level),
        name="relax",
        out_shape=(out,) if level is None else (out, half),
        in_specs=[SMEM, SMEM, VMEM, VMEM, VMEM] + [VMEM] * len(rows),
        out_specs=(HBM,) if level is None else (HBM, VMEM),
        scratch_shapes=[
            pltpu.VMEM((2, HALF_F, BLK), F32),
            pltpu.VMEM(cells.shape, F32),
            pltpu.SemaphoreType.DMA((CHUNKS,)),
        ],
        cost_estimate=pl.CostEstimate(flops=10**7, bytes_accessed=4 * 10**6, transcendentals=10**5),
        compiler_params=pltpu.CompilerParams(vmem_limit_bytes=16 << 20),
    )(levels, rate, cells, even, odd, *rows)


ROWS = HALF_F // 8


def attach(group, ahead_ref, back_ref, out_refs):
    me = lax.axis_index("gy")
    for s, out_ref in zip(entry(group), out_refs):
        if s not in near(group):
            continue
        first = out_ref.shape[0] - ROWS
        for source_ref, by in ((ahead_ref, 1), (back_ref, -1)):

            @pl.when(peer(me, s, group) == me + by)
            def _(out_ref=out_ref, source_ref=source_ref, first=first):
                for j in range(ROWS):
                    out_ref[first + j] = source_ref[8 * j : 8 * j + 8, :]


def coarse_kernel(group, level_ref, even_ref, odd_ref, ahead_ref, back_ref, *out_refs):
    block, _, lower_differs, _ = place(level_ref)
    use_even = (block % 2 == 0) != lower_differs
    for j in range(VBC):
        a, b = even_ref[j].astype(F32), odd_ref[j].astype(F32)
        piece = jnp.where(use_even, a, b).astype(BF16)
        for out_ref in out_refs:
            out_ref[j] = piece
    attach(group, ahead_ref, back_ref, out_refs)


def pieces_kernel(group, level_ref, link_ref, even_ref, odd_ref, ahead_ref, back_ref, *refs):
    out_refs, start_ref = refs[:-1], refs[-1]
    block, own, lower_differs, _ = place(level_ref)
    me = lax.axis_index("gy")
    local = VBF // group
    slots = out_refs[0].shape[0]
    use_even = (block % 2 == 0) != lower_differs

    def count(h, total):
        start_ref[h] = total
        for j in range(local):
            hit = (link_ref[1, h * local + j] >= HALF_C) == lower_differs
            total = total + hit.astype(jnp.int32)
        return total

    lax.fori_loop(0, group, count, jnp.int32(0))

    def fill(source_ref):
        for s, out_ref in zip(entry(group), out_refs):
            start = start_ref[peer(me, s, group)]
            for j in range(slots):
                out_ref[j] = source_ref[jnp.minimum(start + j, HALF_F - 1)]

    @pl.when(use_even)
    def _():
        fill(even_ref)

    @pl.when(jnp.logical_not(use_even))
    def _():
        fill(odd_ref)

    attach(group, ahead_ref, back_ref, out_refs)


def outgoing_shapes(slots, group, rows_n):
    return tuple(
        jax.ShapeDtypeStruct((slots + (ROWS if s else 0), rows_n, BLK), BF16)
        for s in entry(group)
    )


def coarse_pieces(levels, even, odd, edges, group):
    return pl.pallas_call(
        functools.partial(coarse_kernel, group),
        name="coarse_pieces",
        out_shape=outgoing_shapes(VBC, group, even.shape[1]),
        in_specs=[SMEM] + [VMEM] * 4,
        out_specs=(VMEM,) * group,
        cost_estimate=pl.CostEstimate(flops=10**5, bytes_accessed=10**6, transcendentals=0),
        compiler_params=pltpu.CompilerParams(vmem_limit_bytes=8 << 20),
    )(levels, even, odd, *edges)


def pieces(levels, links, even, odd, edges, group, slots):
    return pl.pallas_call(
        functools.partial(pieces_kernel, group),
        name="pieces",
        out_shape=outgoing_shapes(slots, group, even.shape[1]),
        in_specs=[SMEM, SMEM] + [VMEM] * 4,
        out_specs=(VMEM,) * group,
        scratch_shapes=[pltpu.SMEM((group,), jnp.int32)],
        cost_estimate=pl.CostEstimate(flops=10**5, bytes_accessed=10**6, transcendentals=0),
        compiler_params=pltpu.CompilerParams(vmem_limit_bytes=8 << 20),
    )(levels, links, even, odd, *edges)


def stacked(refs, index):
    return jnp.concatenate([ref[index].astype(F32) for ref in refs], axis=0).astype(BF16)


def to_coarse_kernel(group, level_ref, link_ref, values_ref, *refs):
    in_refs, out_refs, sum_ref = refs[:group], refs[group : 2 * group], refs[-1]
    _, _, lower_differs, _ = place(level_ref)
    local = values_ref.shape[0]
    cells_y = in_refs[0].shape[1]
    first = lax.axis_index("gy") * local
    offset = jnp.where(lower_differs, HALF_C, 0)

    targets = [link_ref[1, first + j] - offset for j in range(local)]
    needed = [(t >= 0) & (t < HALF_C) for t in targets]
    sum_ref[...] = jnp.zeros_like(sum_ref)
    slot = jnp.int32(0)
    for j in range(local):

        @pl.when(needed[j])
        def _(j=j, slot=slot):
            sum_ref[targets[j]] += jnp.dot(
                stacked(in_refs, slot), values_ref[j], preferred_element_type=F32
            )

        slot = slot + needed[j].astype(jnp.int32)
    for s, out_ref in enumerate(out_refs):
        out_ref[...] = sum_ref[:, s * cells_y : (s + 1) * cells_y, :].astype(BF16)


def to_fine_kernel(group, level_ref, link_ref, values_ref, *refs):
    in_refs, out_refs = refs[:group], refs[group : 2 * group]
    _, _, lower_differs, _ = place(level_ref)
    local = values_ref.shape[0]
    cells_y = in_refs[0].shape[1]
    first = lax.axis_index("gy") * local
    active = (first >= HALF_F) == lower_differs

    @pl.when(active)
    def _():
        for j in range(local):
            product = jnp.dot(
                stacked(in_refs, link_ref[0, first + j]),
                values_ref[j],
                preferred_element_type=F32,
            ).astype(BF16)
            for s, out_ref in enumerate(out_refs):
                out_ref[j] = product[s * cells_y : (s + 1) * cells_y, :]


def load_kernel(level_ref, link_ref, values_ref, role_ref, held_ref, sems):
    _, own, lower_differs, upper_differs = place(level_ref)
    local = values_ref.shape[1]
    first = lax.axis_index("gy") * local
    fine = own == 1
    differs = lower_differs | upper_differs
    counts = sizes(local)
    fine_role = len(counts) + jnp.where(lower_differs, 1, 2)
    role_ref[0] = jnp.where(differs & fine, fine_role, 0)

    @pl.when(differs & fine & ((first >= HALF_F) == lower_differs))
    def _():
        whole = pltpu.make_async_copy(values_ref.at[0], held_ref, sems.at[0])
        whole.start()
        whole.wait()

    @pl.when(differs & jnp.logical_not(fine))
    def _():
        def hit(f):
            return (link_ref[1, f] >= HALF_C) == lower_differs

        def copy(j):
            return pltpu.make_async_copy(values_ref.at[1, j], held_ref.at[j], sems.at[j])

        needed = [hit(first + j) for j in range(local)]
        for j in range(local):
            pl.when(needed[j])(lambda j=j: copy(j).start())

        def most(h, worst):
            count = jnp.int32(0)
            for j in range(local):
                count = count + hit(h * local + j).astype(jnp.int32)
            return jnp.maximum(worst, count)

        worst = lax.fori_loop(0, VBF // local, most, jnp.int32(0))
        role = jnp.int32(1)
        for size in counts[:-1]:
            role = role + (worst > size).astype(jnp.int32)
        role_ref[0] = role
        for j in range(local):
            pl.when(needed[j])(lambda j=j: copy(j).wait())


def load(levels, links, values):
    local = values.shape[1]
    return pl.pallas_call(
        load_kernel,
        name="load",
        out_shape=(
            jax.ShapeDtypeStruct((1,), jnp.int32),
            jax.ShapeDtypeStruct(values.shape[1:], BF16),
        ),
        in_specs=[SMEM, SMEM, HBM],
        out_specs=(SMEM, VMEM),
        scratch_shapes=[pltpu.SemaphoreType.DMA((local,))],
        cost_estimate=pl.CostEstimate(
            flops=0, bytes_accessed=local * BLK * BLK * 2, transcendentals=0
        ),
        compiler_params=pltpu.CompilerParams(vmem_limit_bytes=44 << 20),
    )(levels, links, values)


def multiply(kernel, levels, links, values, arrived, slots, scratch):
    group = len(arrived)
    local = values.shape[0]
    out = jax.ShapeDtypeStruct((slots,) + arrived[0].shape[1:], BF16)
    return pl.pallas_call(
        functools.partial(kernel, group),
        name=kernel.__name__,
        out_shape=(out,) * group,
        in_specs=[SMEM, SMEM, VMEM] + [VMEM] * group,
        out_specs=(VMEM,) * group,
        scratch_shapes=scratch,
        cost_estimate=pl.CostEstimate(
            flops=2 * local * 32 * BLK * BLK, bytes_accessed=2 * local * BLK * BLK, transcendentals=0
        ),
        compiler_params=pltpu.CompilerParams(vmem_limit_bytes=24 << 20),
    )(levels, links, values, *arrived)


def finish_kernel(role, group, level_ref, base_ref, held_ref, *refs):
    in_refs, out_ref, done_ref, sems = refs[:-3], refs[-3], refs[-2], refs[-1]
    _, _, _, upper_differs = place(level_ref)
    me = lax.axis_index("gy")
    parts = sems.shape[0]
    side, spacing, count = (
        (SC, spacing_coarse, HALF_C) if role == 1 else (SF, spacing_fine, HALF_F)
    )
    whole = count * BLK
    part = whole // parts
    centre = (side - 1) * 0.5

    def flush(index):
        start = index * part + jnp.where(upper_differs, 0, whole)
        at = pl.ds(pl.multiple_of(start, part), part)
        return pltpu.make_async_copy(
            done_ref.at[:, pl.ds(pl.multiple_of(index * part, part), part)],
            out_ref.at[:, at],
            sems.at[index],
        )

    first_plane = jnp.where(upper_differs, 0, side // 2)
    if role == 1:
        width = side * side
        for o in range(HALF_C):
            ghost = in_refs[0][o].astype(F32)
            for ref in in_refs[1:]:
                ghost = ghost + ref[o].astype(F32)
            for k in range(BLK // width):
                plane = lax.convert_element_type(first_plane + o * (BLK // width) + k, F32)
                push = cfl_ratio * spacing * jnp.abs(plane - centre)
                at = slice(o * BLK + k * width, o * BLK + (k + 1) * width)
                done_ref[:, at] = base_ref[:, at] + push * ghost[:, k * width : (k + 1) * width]
        flush(0).start()
        flush(0).wait()
        return

    offset = jnp.where(upper_differs, 0, HALF_F)
    for s, ref in zip(order(group), in_refs):
        local = ref.shape[0]
        first = peer(me, s, group) * local - offset

        @pl.when((first >= 0) & (first < HALF_F))
        def _(ref=ref, first=first, local=local):
            for j in range(local):
                slot = first + j
                plane = lax.convert_element_type(first_plane + slot // 2, F32)
                push = cfl_ratio * spacing * jnp.abs(plane - centre)
                at = pl.ds(pl.multiple_of(slot * BLK, BLK), BLK)
                done_ref[:, at] = base_ref[:, at] + push * ref[j].astype(F32)
            flush(lax.div(first, local)).start()

    for index in range(parts):
        flush(index).wait()


def finish(role, levels, base, held, arrived):
    group = len(arrived)
    rows_n = base.shape[0]
    parts = 1 if role == 1 else group // 2
    whole = NVC // 2 if role == 1 else NVF // 2
    return pl.pallas_call(
        functools.partial(finish_kernel, role, group),
        name="finish",
        out_shape=jax.ShapeDtypeStruct(held.shape, F32),
        in_specs=[SMEM, VMEM, HBM] + [VMEM] * group,
        out_specs=HBM,
        scratch_shapes=[pltpu.VMEM((rows_n, whole), F32), pltpu.SemaphoreType.DMA((parts,))],
        input_output_aliases={2: 0},
        cost_estimate=pl.CostEstimate(flops=10**6, bytes_accessed=10**6, transcendentals=0),
        compiler_params=pltpu.CompilerParams(vmem_limit_bytes=8 << 20),
    )(levels, base, held, *arrived)


def on_device(distribution, relax_rate, block_level, block_link, remap_values):
    blocks, group = lax.axis_size("gx"), lax.axis_size("gy")
    cells_y = distribution.shape[1]
    local = remap_values.shape[1]
    cells = distribution[0]

    def exchange(value, parity):
        pairs = []
        for low in range(parity, blocks - 1, 2):
            for y in range(group):
                here, there = low * group + y, (low + 1) * group + y
                pairs += [(here, there), (there, here)]
        return lax.ppermute(value, BOTH, pairs)

    everyone = range(group)

    def around(steps, outgoing, sources=everyone, targets=everyone, rows=False):
        arrived = []
        for s, value in zip(steps, outgoing):
            pairs = [
                (i, peer(i, s, group))
                for i in everyone
                if (i in sources and peer(i, s, group) in targets)
                or (rows and abs(i - peer(i, s, group)) == 1)
            ]
            arrived.append(lax.ppermute(value, "gy", pairs) if s and pairs else value)
        return arrived

    even, odd = prepare(block_level, block_link, cells)
    odd = exchange(odd, 1)
    even = exchange(even, 0)
    role, held = load(block_level, block_link, remap_values)
    edges = edge_rows(block_level, cells)

    def settle(level, rows):
        return relax(level, block_level, relax_rate, cells, even, odd, rows)

    def alone():
        left = lax.ppermute(edges[0], "gy", [(i, i + 1) for i in range(group - 1)])
        right = lax.ppermute(edges[1], "gy", [(i + 1, i) for i in range(group - 1)])
        return settle(None, [left, right])[0]

    def remapped(level, kernel, slots, scratch, arrived):
        made = multiply(kernel, block_level, block_link, held, arrived, slots, scratch)
        made = dict(zip(entry(group), made))
        return [made[s] for s in order(group)], settle(level, arrived[1:])

    def to_coarse(slots):
        outgoing = pieces(block_level, block_link, even, odd, edges, group, slots)
        sums = [pltpu.VMEM((HALF_C, group * cells_y, BLK), F32)]
        made, (out, base) = remapped(0, to_coarse_kernel, HALF_C, sums, around(entry(group), outgoing))
        return finish(1, block_level, base, out, around(order(group), made))

    def to_fine(active):
        outgoing = coarse_pieces(block_level, even, odd, edges, group)
        arrived = around(entry(group), outgoing, targets=active, rows=True)
        made, (out, base) = remapped(1, to_fine_kernel, local, [], arrived)
        return finish(2, block_level, base, out, around(order(group), made, sources=active))

    branches = [alone]
    for slots in sizes(local):
        branches.append(functools.partial(to_coarse, slots))
    for active in (range(group // 2, group), range(group // 2)):
        branches.append(functools.partial(to_fine, active))
    updated = lax.switch(role[0], branches)
    return updated[None]


def solution(mesh):
    in_specs = (P("gx", "gy", None), P("gx", "gy"), P(), P(), P(None, "gy", None, None))
    out_specs = P("gx", "gy", None)
    return jax.shard_map(
        on_device, mesh=mesh, in_specs=in_specs, out_specs=out_specs, check_vma=False
    )
```

```python
import functools
import math

import jax
import jax.numpy as jnp
from jax import lax
from jax.experimental import pallas as pl
from jax.experimental.pallas import tpu as pltpu
from jax.sharding import PartitionSpec as P

SC = 16
SF = 32
BLK = 512
NVC = 4096
NVF = 32768
VBC = NVC // BLK
VBF = NVF // BLK
HALF_F = VBF // 2
HALF_C = VBC // 2
CHUNKS = 8
PART = NVF // CHUNKS

cfl_ratio = 0.03
spacing_coarse = 0.5
spacing_fine = 0.4

BOTH = ("gx", "gy")
SMEM = pl.BlockSpec(memory_space=pltpu.SMEM)
VMEM = pl.BlockSpec(memory_space=pltpu.VMEM)
HBM = pl.BlockSpec(memory_space=pltpu.HBM)
F32 = jnp.float32
BF16 = jnp.bfloat16


def place(level_ref):
    block = lax.axis_index("gx")
    own = level_ref[block]
    lower = level_ref[jnp.maximum(block - 1, 0)]
    upper = level_ref[jnp.minimum(block + 1, level_ref.shape[0] - 1)]
    return block, own, lower != own, upper != own


def peer(me, step, group):
    if group & (group - 1):
        raise ValueError(group)
    return me ^ step


def order(group):
    return sorted(range(group), key=lambda s: (s == 1, s))


def entry(group):
    return order(group)


def near(group):
    return [s for s in entry(group) if s and not s & (s + 1)]


def sizes(local):
    return [max(1, (5 * local) // 8), max(1, (3 * local) // 4), local]


def block_at(ref, index):
    return ref[:, pl.ds(pl.multiple_of(index * BLK, BLK), BLK)]


def prepare_kernel(level_ref, link_ref, cells_ref, even_ref, odd_ref, index_ref):
    block, own, lower_differs, upper_differs = place(level_ref)
    fine = own == 1

    def fill(target_ref, going_up):
        differs = jnp.where(going_up, upper_differs, lower_differs)
        gathers = differs & fine

        @pl.when(gathers)
        def _():
            def look(f, count):
                index_ref[count] = f
                hit = (link_ref[1, f] >= HALF_C) == going_up
                return count + hit.astype(jnp.int32)

            lax.fori_loop(0, VBF, look, jnp.int32(0), unroll=8)

            def copy(j, carry):
                target_ref[j] = block_at(cells_ref, index_ref[j]).astype(BF16)
                return carry

            lax.fori_loop(0, HALF_F, copy, 0, unroll=8)

        @pl.when(fine & jnp.logical_not(differs))
        def _():
            start = jnp.where(going_up, HALF_F, 0)
            for j in range(HALF_F):
                target_ref[j] = block_at(cells_ref, start + j).astype(BF16)

        @pl.when(jnp.logical_not(fine))
        def _():
            start = jnp.where(going_up & jnp.logical_not(differs), HALF_C, 0)
            for j in range(VBC):
                target_ref[j] = block_at(cells_ref, start + j).astype(BF16)

    on_even = block % 2 == 0
    fill(odd_ref, jnp.logical_not(on_even))
    fill(even_ref, on_even)


def prepare(levels, links, cells):
    half = jax.ShapeDtypeStruct((HALF_F, cells.shape[0], BLK), BF16)
    return pl.pallas_call(
        prepare_kernel,
        name="prepare",
        out_shape=(half, half),
        in_specs=[SMEM, SMEM, VMEM],
        out_specs=(VMEM,) * 2,
        scratch_shapes=[pltpu.SMEM((VBF + 1,), jnp.int32)],
        cost_estimate=pl.CostEstimate(flops=10**6, bytes_accessed=2 * 10**6, transcendentals=0),
        compiler_params=pltpu.CompilerParams(vmem_limit_bytes=8 << 20),
    )(levels, links, cells)


def rows_kernel(level_ref, cells_ref, ahead_ref, back_ref, row_ref):
    _, own, _, _ = place(level_ref)
    cells_y = cells_ref.shape[0]

    def rows(target_ref, row, parity):
        @pl.when(own == 1)
        def _():
            for i in range(HALF_F):
                row_ref[i : i + 1, :] = cells_ref[
                    row : row + 1, (2 * i + parity) * BLK : (2 * i + parity + 1) * BLK
                ]

        @pl.when(own != 1)
        def _():
            for i in range(VBC):
                row_ref[i : i + 1, :] = cells_ref[row : row + 1, i * BLK : (i + 1) * BLK]

        target_ref[...] = row_ref[...].astype(BF16)

    rows(ahead_ref, cells_y - 1, 1)
    rows(back_ref, 0, 0)


def edge_rows(levels, cells):
    row = jax.ShapeDtypeStruct((HALF_F, BLK), BF16)
    return pl.pallas_call(
        rows_kernel,
        name="edge_rows",
        out_shape=(row, row),
        in_specs=[SMEM, VMEM],
        out_specs=(VMEM, VMEM),
        scratch_shapes=[pltpu.VMEM((HALF_F, BLK), F32)],
        cost_estimate=pl.CostEstimate(flops=10**6, bytes_accessed=2 * 10**6, transcendentals=0),
        compiler_params=pltpu.CompilerParams(vmem_limit_bytes=8 << 20),
    )(levels, cells)


def ghost_at(ref, index):
    return ref[index].astype(F32)


def relax_kernel(
    level,
    level_ref,
    rate_ref,
    cells_ref,
    even_ref,
    odd_ref,
    *refs,
):
    side_ref, done_ref, sems = refs[-3:]
    results = 1 if level is None else 2
    row_refs, out_ref = refs[: -3 - results], refs[-3 - results]
    block, own, lower_differs, upper_differs = place(level_ref)
    on_even = block % 2 == 0
    rows_n = cells_ref.shape[0]

    def flush(chunk):
        at = pl.ds(chunk * PART, PART)
        return pltpu.make_async_copy(done_ref.at[:, at], out_ref.at[:, at], sems.at[chunk])

    def run(side, spacing):
        width = side * side
        mid = width // 2
        middle = side // 2
        centre = (side - 1) * 0.5
        lane = lax.broadcasted_iota(jnp.int32, (rows_n, width), 1)
        along_y = spacing * ((lane // side).astype(F32) - centre)
        along_z = spacing * ((lane % side).astype(F32) - centre)

        def span(i):
            start = i * width
            return pl.ds(start if isinstance(i, int) else pl.multiple_of(start, width), width)

        def speed_at(i):
            return spacing * (lax.convert_element_type(i, F32) - centre)

        def gather(i, sums):
            total, first, second = sums
            plane = cells_ref[:, span(i)]
            speed = speed_at(i)
            return total + plane, first + plane * speed, second + plane * (speed * speed)

        zero = jnp.zeros((rows_n, width), F32)
        total, first, second = lax.fori_loop(0, side, gather, (zero, zero, zero), unroll=4)

        def over(value):
            return jnp.broadcast_to(jnp.sum(value, axis=1, keepdims=True), (rows_n, 128))

        weight = spacing * spacing * spacing
        density = weight * over(total)
        scale = weight / density
        mean_x = scale * over(first)
        mean_y = scale * over(total * along_y)
        mean_z = scale * over(total * along_z)
        square = scale * over(second + total * (along_y * along_y + along_z * along_z))
        heat = (square - mean_x * mean_x - mean_y * mean_y - mean_z * mean_z) / 3.0
        row = lax.broadcasted_iota(jnp.int32, (rows_n, 128), 0)
        rate = jnp.zeros((rows_n, 128), F32)
        for r in range(rows_n):
            rate = jnp.where(row == r, rate_ref[0, r], rate)
        spread = 2.0 * math.pi * heat
        peak = rate * density / (spread * jnp.sqrt(spread))
        inverse = -0.5 / heat

        def wide(value):
            return jnp.concatenate([value] * (width // 128), axis=1)

        off_y = along_y - wide(mean_y)
        off_z = along_z - wide(mean_z)
        across = wide(peak) * jnp.exp((off_y * off_y + off_z * off_z) * wide(inverse))
        drift = cfl_ratio * jnp.abs(along_y)
        keep = (1.0 - wide(rate)) - drift
        wide_row = lax.broadcasted_iota(jnp.int32, (rows_n, mid), 0)

        def update(i, upward):
            plane = cells_ref[:, span(i)]
            speed = speed_at(i)
            off_x = speed - mean_x
            along = wide(jnp.exp(off_x * off_x * inverse))
            take_even = on_even == upward
            if side == SF:
                right = side_ref[1, pl.ds(i, 1), :]
                left = side_ref[0, pl.ds(i, 1), :]
                slot = 2 * (i if upward else i - middle)
                ghosts = []
                for half in range(2):
                    a, b = ghost_at(even_ref, slot + half), ghost_at(odd_ref, slot + half)
                    ghosts.append(jnp.where(take_even, a, b))
                ghost = jnp.concatenate(ghosts, axis=1)
            else:
                slot, offset = i // 2, (i % 2) * width
                right = side_ref[1, slot : slot + 1, offset : offset + mid]
                left = side_ref[0, slot : slot + 1, offset + mid : offset + width]
                slot = slot if upward else slot - HALF_C
                a, b = ghost_at(even_ref, slot), ghost_at(odd_ref, slot)
                ghost = jnp.where(take_even, a, b)[:, offset : offset + width]
            if level is not None:
                ghost = jnp.where(upper_differs if upward else lower_differs, 0.0, ghost)
            low, high = plane[:, :mid], plane[:, mid:]
            beyond = jnp.where(wide_row == rows_n - 1, right, pltpu.roll(low, rows_n - 1, 0))
            before = jnp.where(wide_row == 0, left, pltpu.roll(high, 1, 0))
            beside = jnp.concatenate([beyond, before], axis=1)
            push = cfl_ratio * jnp.abs(speed)
            done_ref[:, span(i)] = (
                plane * (keep - push) + push * ghost + drift * beside + along * across
            )

        if side == SF:
            each = side // CHUNKS
            for chunk in range(CHUNKS):
                upward = chunk < CHUNKS // 2

                def step(k, carry, chunk=chunk, upward=upward):
                    update(chunk * each + k, upward)
                    return carry

                lax.fori_loop(0, each, step, 0, unroll=4)
                flush(chunk).start()
        else:
            for i in range(side):
                update(i, i < middle)
            flush(0).start()
            done_ref[:, NVC:] = jnp.zeros((rows_n, NVF - NVC), F32)
            for chunk in range(1, CHUNKS):
                flush(chunk).start()

    if level is None:
        for k, row_ref in enumerate(row_refs):
            side_ref[k] = row_ref[...].astype(F32)
    else:
        side_ref[...] = jnp.zeros_like(side_ref)
        me, group = lax.axis_index("gy"), lax.axis_size("gy")
        for s, ref in zip(near(group), row_refs):
            first = ref.shape[0] - ROWS
            for k, by in ((0, -1), (1, 1)):

                @pl.when(peer(me, s, group) == me + by)
                def _(ref=ref, k=k, first=first):
                    for j in range(ROWS):
                        side_ref[k, 8 * j : 8 * j + 8, :] = ref[first + j].astype(F32)

    if level is None:

        @pl.when(own == 1)
        def _():
            run(SF, spacing_fine)

        @pl.when(own != 1)
        def _():
            run(SC, spacing_coarse)

    elif level == 1:
        run(SF, spacing_fine)
    else:
        run(SC, spacing_coarse)

    if level is not None:
        base_ref = refs[-4]
        split = (NVF if level == 1 else NVC) // 2

        @pl.when(upper_differs)
        def _():
            base_ref[...] = done_ref[:, :split]

        @pl.when(jnp.logical_not(upper_differs))
        def _():
            base_ref[...] = done_ref[:, split : 2 * split]

    for chunk in range(CHUNKS):
        flush(chunk).wait()


def relax(level, levels, rate, cells, even, odd, rows):
    out = jax.ShapeDtypeStruct(cells.shape, F32)
    half = jax.ShapeDtypeStruct((cells.shape[0], (NVF if level == 1 else NVC) // 2), F32)
    return pl.pallas_call(
        functools.partial(relax_kernel, level),
        name="relax",
        out_shape=(out,) if level is None else (out, half),
        in_specs=[SMEM, SMEM, VMEM, VMEM, VMEM] + [VMEM] * len(rows),
        out_specs=(HBM,) if level is None else (HBM, VMEM),
        scratch_shapes=[
            pltpu.VMEM((2, HALF_F, BLK), F32),
            pltpu.VMEM(cells.shape, F32),
            pltpu.SemaphoreType.DMA((CHUNKS,)),
        ],
        cost_estimate=pl.CostEstimate(flops=10**7, bytes_accessed=4 * 10**6, transcendentals=10**5),
        compiler_params=pltpu.CompilerParams(vmem_limit_bytes=16 << 20),
    )(levels, rate, cells, even, odd, *rows)


ROWS = HALF_F // 8


def attach(group, ahead_ref, back_ref, out_refs):
    me = lax.axis_index("gy")
    for s, out_ref in zip(entry(group), out_refs):
        if s not in near(group):
            continue
        first = out_ref.shape[0] - ROWS
        for source_ref, by in ((ahead_ref, 1), (back_ref, -1)):

            @pl.when(peer(me, s, group) == me + by)
            def _(out_ref=out_ref, source_ref=source_ref, first=first):
                for j in range(ROWS):
                    out_ref[first + j] = source_ref[8 * j : 8 * j + 8, :]


def coarse_kernel(group, from_lower, even_ref, odd_ref, ahead_ref, back_ref, *out_refs):
    use_even = (lax.axis_index("gx") % 2 == 0) != from_lower
    for j in range(VBC):
        a, b = even_ref[j].astype(F32), odd_ref[j].astype(F32)
        piece = jnp.where(use_even, a, b).astype(BF16)
        for out_ref in out_refs:
            out_ref[j] = piece
    attach(group, ahead_ref, back_ref, out_refs)


def pieces_kernel(group, level_ref, link_ref, even_ref, odd_ref, ahead_ref, back_ref, *refs):
    out_refs, start_ref = refs[:-1], refs[-1]
    block, own, lower_differs, _ = place(level_ref)
    me = lax.axis_index("gy")
    local = VBF // group
    slots = out_refs[0].shape[0]
    use_even = (block % 2 == 0) != lower_differs

    def count(h, total):
        start_ref[h] = total
        for j in range(local):
            hit = (link_ref[1, h * local + j] >= HALF_C) == lower_differs
            total = total + hit.astype(jnp.int32)
        return total

    lax.fori_loop(0, group, count, jnp.int32(0))

    def fill(source_ref):
        for s, out_ref in zip(entry(group), out_refs):
            start = start_ref[peer(me, s, group)]
            for j in range(slots):
                out_ref[j] = source_ref[jnp.minimum(start + j, HALF_F - 1)]

    @pl.when(use_even)
    def _():
        fill(even_ref)

    @pl.when(jnp.logical_not(use_even))
    def _():
        fill(odd_ref)

    attach(group, ahead_ref, back_ref, out_refs)


def outgoing_shapes(slots, group, rows_n):
    return tuple(
        jax.ShapeDtypeStruct((slots + (ROWS if s in near(group) else 0), rows_n, BLK), BF16)
        for s in entry(group)
    )


def coarse_pieces(from_lower, even, odd, edges, group):
    return pl.pallas_call(
        functools.partial(coarse_kernel, group, from_lower),
        name="coarse_pieces",
        out_shape=outgoing_shapes(VBC, group, even.shape[1]),
        in_specs=[VMEM] * 4,
        out_specs=(VMEM,) * group,
        cost_estimate=pl.CostEstimate(flops=10**5, bytes_accessed=10**6, transcendentals=0),
        compiler_params=pltpu.CompilerParams(vmem_limit_bytes=8 << 20),
    )(even, odd, *edges)


def pieces(levels, links, even, odd, edges, group, slots):
    return pl.pallas_call(
        functools.partial(pieces_kernel, group),
        name="pieces",
        out_shape=outgoing_shapes(slots, group, even.shape[1]),
        in_specs=[SMEM, SMEM] + [VMEM] * 4,
        out_specs=(VMEM,) * group,
        scratch_shapes=[pltpu.SMEM((group,), jnp.int32)],
        cost_estimate=pl.CostEstimate(flops=10**5, bytes_accessed=10**6, transcendentals=0),
        compiler_params=pltpu.CompilerParams(vmem_limit_bytes=8 << 20),
    )(levels, links, even, odd, *edges)


def stacked(refs, index):
    return jnp.concatenate([ref[index].astype(F32) for ref in refs], axis=0).astype(BF16)


def to_coarse_kernel(group, level_ref, link_ref, head_ref, tail_ref, *refs):
    in_refs, out_refs, sum_ref = refs[:group], refs[group : 2 * group], refs[-1]
    _, _, lower_differs, _ = place(level_ref)
    half = head_ref.shape[0]
    local = half + tail_ref.shape[0]
    cells_y = in_refs[0].shape[1]
    first = lax.axis_index("gy") * local
    offset = jnp.where(lower_differs, HALF_C, 0)

    targets = [link_ref[1, first + j] - offset for j in range(local)]
    needed = [(t >= 0) & (t < HALF_C) for t in targets]
    sum_ref[...] = jnp.zeros_like(sum_ref)
    slot = jnp.int32(0)
    for j in range(local):

        @pl.when(needed[j])
        def _(j=j, slot=slot):
            sum_ref[targets[j]] += jnp.dot(
                stacked(in_refs, slot), (head_ref[j] if j < half else tail_ref[j - half]), preferred_element_type=F32
            )

        slot = slot + needed[j].astype(jnp.int32)
    for s, out_ref in enumerate(out_refs):
        out_ref[...] = sum_ref[:, s * cells_y : (s + 1) * cells_y, :].astype(BF16)


def to_fine_kernel(group, level_ref, link_ref, head_ref, tail_ref, *refs):
    in_refs, out_refs = refs[:group], refs[group : 2 * group]
    _, _, lower_differs, _ = place(level_ref)
    half = head_ref.shape[0]
    local = half + tail_ref.shape[0]
    cells_y = in_refs[0].shape[1]
    first = lax.axis_index("gy") * local
    active = (first >= HALF_F) == lower_differs

    @pl.when(active)
    def _():
        for j in range(local):
            product = jnp.dot(
                stacked(in_refs, link_ref[0, first + j]),
                (head_ref[j] if j < half else tail_ref[j - half]),
                preferred_element_type=F32,
            ).astype(BF16)
            for s, out_ref in enumerate(out_refs):
                out_ref[j] = product[s * cells_y : (s + 1) * cells_y, :]


def load_kernel(start, stop, level_ref, link_ref, values_ref, role_ref, held_ref, sems):
    _, own, lower_differs, upper_differs = place(level_ref)
    local = values_ref.shape[1]
    first = lax.axis_index("gy") * local
    fine = own == 1
    source = jnp.where(fine, 0, 1)
    differs = lower_differs | upper_differs

    def needed(j):
        coarse = (link_ref[1, first + j] >= HALF_C) == lower_differs
        here = jnp.where(fine, (first >= HALF_F) == lower_differs, coarse)
        return here & differs

    def copy(j):
        at = j - start
        return pltpu.make_async_copy(values_ref.at[source, j], held_ref.at[at], sems.at[at])

    for j in range(start, stop):
        pl.when(needed(j))(lambda j=j: copy(j).start())

    counts = sizes(local)
    fine_role = len(counts) + jnp.where(lower_differs, 1, 2)
    role_ref[0] = jnp.where(differs & fine, fine_role, 0)

    @pl.when(differs & jnp.logical_not(fine) & (start == 0))
    def _():
        def most(h, worst):
            count = jnp.int32(0)
            for j in range(local):
                hit = (link_ref[1, h * local + j] >= HALF_C) == lower_differs
                count = count + hit.astype(jnp.int32)
            return jnp.maximum(worst, count)

        worst = lax.fori_loop(0, VBF // local, most, jnp.int32(0))
        role = jnp.int32(1)
        for size in counts[:-1]:
            role = role + (worst > size).astype(jnp.int32)
        role_ref[0] = role

    for j in range(start, stop):
        pl.when(needed(j))(lambda j=j: copy(j).wait())


def load(levels, links, values, start, stop):
    return pl.pallas_call(
        functools.partial(load_kernel, start, stop),
        name="load",
        out_shape=(
            jax.ShapeDtypeStruct((1,), jnp.int32),
            jax.ShapeDtypeStruct((stop - start,) + values.shape[2:], BF16),
        ),
        in_specs=[SMEM, SMEM, HBM],
        out_specs=(SMEM, VMEM),
        scratch_shapes=[pltpu.SemaphoreType.DMA((stop - start,))],
        cost_estimate=pl.CostEstimate(
            flops=0, bytes_accessed=(stop - start) * BLK * BLK * 2, transcendentals=0
        ),
        compiler_params=pltpu.CompilerParams(vmem_limit_bytes=44 << 20),
    )(levels, links, values)


def multiply(kernel, levels, links, values, arrived, slots, scratch):
    group = len(arrived)
    local = sum(part.shape[0] for part in values)
    out = jax.ShapeDtypeStruct((slots,) + arrived[0].shape[1:], BF16)
    return pl.pallas_call(
        functools.partial(kernel, group),
        name=kernel.__name__,
        out_shape=(out,) * group,
        in_specs=[SMEM, SMEM, VMEM, VMEM] + [VMEM] * group,
        out_specs=(VMEM,) * group,
        scratch_shapes=scratch,
        cost_estimate=pl.CostEstimate(
            flops=2 * local * 32 * BLK * BLK, bytes_accessed=2 * local * BLK * BLK, transcendentals=0
        ),
        compiler_params=pltpu.CompilerParams(vmem_limit_bytes=24 << 20),
    )(levels, links, *values, *arrived)


def finish_kernel(role, group, from_lower, *refs):
    if from_lower is None:
        upper_differs, refs = place(refs[0])[3], refs[1:]
    else:
        upper_differs = not from_lower
    base_ref, in_refs = refs[0], refs[2:-3]
    out_ref, done_ref, sems = refs[-3:]
    me = lax.axis_index("gy")
    parts = sems.shape[0]
    side, spacing, count = (
        (SC, spacing_coarse, HALF_C) if role == 1 else (SF, spacing_fine, HALF_F)
    )
    whole = count * BLK
    part = whole // parts
    centre = (side - 1) * 0.5

    def flush(index):
        start = index * part + jnp.where(upper_differs, 0, whole)
        at = pl.ds(pl.multiple_of(start, part), part)
        return pltpu.make_async_copy(
            done_ref.at[:, pl.ds(pl.multiple_of(index * part, part), part)],
            out_ref.at[:, at],
            sems.at[index],
        )

    first_plane = jnp.where(upper_differs, 0, side // 2)
    if role == 1:
        width = side * side
        for o in range(HALF_C):
            ghost = in_refs[0][o].astype(F32)
            for ref in in_refs[1:]:
                ghost = ghost + ref[o].astype(F32)
            for k in range(BLK // width):
                plane = lax.convert_element_type(first_plane + o * (BLK // width) + k, F32)
                push = cfl_ratio * spacing * jnp.abs(plane - centre)
                at = slice(o * BLK + k * width, o * BLK + (k + 1) * width)
                done_ref[:, at] = base_ref[:, at] + push * ghost[:, k * width : (k + 1) * width]
        flush(0).start()
        flush(0).wait()
        return

    offset = jnp.where(upper_differs, 0, HALF_F)
    per = HALF_F // parts
    for s, ref in zip(order(group), in_refs):
        local = ref.shape[0]
        first = peer(me, s, group) * local - offset

        @pl.when((first >= 0) & (first < HALF_F))
        def _(ref=ref, first=first, local=local):
            for j in range(local):
                slot = first + j
                if j and j % per == 0:
                    flush(lax.div(slot, per) - 1).start()
                plane = lax.convert_element_type(first_plane + slot // 2, F32)
                push = cfl_ratio * spacing * jnp.abs(plane - centre)
                at = pl.ds(pl.multiple_of(slot * BLK, BLK), BLK)
                done_ref[:, at] = base_ref[:, at] + push * ref[j].astype(F32)
            flush(lax.div(first + local, per) - 1).start()

    for index in range(parts):
        flush(index).wait()


def finish(role, from_lower, levels, base, held, arrived):
    group = len(arrived)
    rows_n = base.shape[0]
    parts = 1 if role == 1 else HALF_F // min(4, VBF // group)
    whole = NVC // 2 if role == 1 else NVF // 2
    scalars = [levels] if from_lower is None else []
    return pl.pallas_call(
        functools.partial(finish_kernel, role, group, from_lower),
        name="finish",
        out_shape=jax.ShapeDtypeStruct(held.shape, F32),
        in_specs=[SMEM] * len(scalars) + [VMEM, HBM] + [VMEM] * group,
        out_specs=HBM,
        scratch_shapes=[pltpu.VMEM((rows_n, whole), F32), pltpu.SemaphoreType.DMA((parts,))],
        input_output_aliases={len(scalars) + 1: 0},
        cost_estimate=pl.CostEstimate(flops=10**6, bytes_accessed=10**6, transcendentals=0),
        compiler_params=pltpu.CompilerParams(vmem_limit_bytes=8 << 20),
    )(*scalars, base, held, *arrived)


def on_device(distribution, relax_rate, block_level, block_link, remap_values):
    blocks, group = lax.axis_size("gx"), lax.axis_size("gy")
    cells_y = distribution.shape[1]
    local = remap_values.shape[1]
    cells = distribution[0]

    def exchange(value, parity):
        pairs = []
        for low in range(parity, blocks - 1, 2):
            for y in range(group):
                here, there = low * group + y, (low + 1) * group + y
                pairs += [(here, there), (there, here)]
        return lax.ppermute(value, BOTH, pairs)

    everyone = range(group)

    def around(steps, outgoing, sources=everyone, targets=everyone, rows=False):
        arrived = []
        for s, value in zip(steps, outgoing):
            pairs = [
                (i, peer(i, s, group))
                for i in everyone
                if (i in sources and peer(i, s, group) in targets)
                or (rows and abs(i - peer(i, s, group)) == 1)
            ]
            arrived.append(lax.ppermute(value, "gy", pairs) if s and pairs else value)
        return arrived

    even, odd = prepare(block_level, block_link, cells)
    odd = exchange(odd, 1)
    even = exchange(even, 0)
    role, head = load(block_level, block_link, remap_values, 0, local // 2)
    edges = edge_rows(block_level, cells)

    def settle(level, rows):
        return relax(level, block_level, relax_rate, cells, even, odd, rows)

    def alone():
        left = lax.ppermute(edges[0], "gy", [(i, i + 1) for i in range(group - 1)])
        right = lax.ppermute(edges[1], "gy", [(i + 1, i) for i in range(group - 1)])
        return settle(None, [left, right])[0]

    def remapped(level, kernel, slots, scratch, arrived):
        tail = load(block_level, block_link, remap_values, local // 2, local)[1]
        values = [head, tail]
        made = multiply(kernel, block_level, block_link, values, arrived, slots, scratch)
        made = dict(zip(entry(group), made))
        return [made[s] for s in order(group)], settle(level, [p for s, p in zip(entry(group), arrived) if s in near(group)])

    def to_coarse(slots):
        outgoing = pieces(block_level, block_link, even, odd, edges, group, slots)
        sums = [pltpu.VMEM((HALF_C, group * cells_y, BLK), F32)]
        made, (out, base) = remapped(0, to_coarse_kernel, HALF_C, sums, around(entry(group), outgoing))
        return finish(1, None, block_level, base, out, around(order(group), made))

    def to_fine(active):
        outgoing = coarse_pieces(active[0] > 0, even, odd, edges, group)
        arrived = around(entry(group), outgoing, targets=active, rows=True)
        made, (out, base) = remapped(1, to_fine_kernel, local, [], arrived)
        return finish(2, active[0] > 0, block_level, base, out, around(order(group), made, sources=active))

    branches = [alone]
    for slots in sizes(local):
        branches.append(functools.partial(to_coarse, slots))
    for active in (range(group // 2, group), range(group // 2)):
        branches.append(functools.partial(to_fine, active))
    updated = lax.switch(role[0], branches)
    return updated[None]


def solution(mesh):
    in_specs = (P("gx", "gy", None), P("gx", "gy"), P(), P(), P(None, "gy", None, None))
    out_specs = P("gx", "gy", None)
    return jax.shard_map(
        on_device, mesh=mesh, in_specs=in_specs, out_specs=out_specs, check_vma=False
    )
```

```python
import functools
import math

import jax
import jax.numpy as jnp
from jax import lax
from jax.experimental import pallas as pl
from jax.experimental.pallas import tpu as pltpu
from jax.sharding import PartitionSpec as P

SC = 16
SF = 32
BLK = 512
NVC = 4096
NVF = 32768
VBC = NVC // BLK
VBF = NVF // BLK
HALF_F = VBF // 2
HALF_C = VBC // 2
CHUNKS = 8
PART = NVF // CHUNKS

cfl_ratio = 0.03
spacing_coarse = 0.5
spacing_fine = 0.4

BOTH = ("gx", "gy")
SMEM = pl.BlockSpec(memory_space=pltpu.SMEM)
VMEM = pl.BlockSpec(memory_space=pltpu.VMEM)
HBM = pl.BlockSpec(memory_space=pltpu.HBM)
F32 = jnp.float32
BF16 = jnp.bfloat16


def place(level_ref):
    block = lax.axis_index("gx")
    own = level_ref[block]
    lower = level_ref[jnp.maximum(block - 1, 0)]
    upper = level_ref[jnp.minimum(block + 1, level_ref.shape[0] - 1)]
    return block, own, lower != own, upper != own


def pick(values, row, column):
    rows = lax.broadcasted_iota(jnp.int32, values.shape, 0)
    columns = lax.broadcasted_iota(jnp.int32, values.shape, 1)
    return jnp.sum(jnp.where((rows == row) & (columns == column), values, 0.0))


def faces_lower(level_ref):
    levels = level_ref[...].astype(F32)
    block = lax.axis_index("gx")
    return pick(levels, 0, block) != pick(levels, 0, jnp.maximum(block - 1, 0))


def peer(me, step, group):
    if group & (group - 1):
        raise ValueError(group)
    return me ^ step


def order(group):
    return sorted(range(group), key=lambda s: (s == 1, s))


def entry(group):
    return order(group)


def near(group):
    return [s for s in entry(group) if s and not s & (s + 1)]


def sizes(local):
    return [max(1, (5 * local) // 8), max(1, (3 * local) // 4), local]


def block_at(ref, index):
    return ref[:, pl.ds(pl.multiple_of(index * BLK, BLK), BLK)]


def prepare_kernel(level_ref, link_ref, cells_ref, even_ref, odd_ref, index_ref):
    block, own, lower_differs, upper_differs = place(level_ref)
    fine = own == 1

    def fill(target_ref, going_up):
        differs = jnp.where(going_up, upper_differs, lower_differs)
        gathers = differs & fine

        @pl.when(gathers)
        def _():
            def look(f, count):
                index_ref[count] = f
                hit = (link_ref[1, f] >= HALF_C) == going_up
                return count + hit.astype(jnp.int32)

            lax.fori_loop(0, VBF, look, jnp.int32(0), unroll=8)

            def copy(j, carry):
                target_ref[j] = block_at(cells_ref, index_ref[j]).astype(BF16)
                return carry

            lax.fori_loop(0, HALF_F, copy, 0, unroll=8)

        @pl.when(fine & jnp.logical_not(differs))
        def _():
            start = jnp.where(going_up, HALF_F, 0)
            for j in range(HALF_F):
                target_ref[j] = block_at(cells_ref, start + j).astype(BF16)

        @pl.when(jnp.logical_not(fine))
        def _():
            start = jnp.where(going_up & jnp.logical_not(differs), HALF_C, 0)
            for j in range(VBC):
                target_ref[j] = block_at(cells_ref, start + j).astype(BF16)

    on_even = block % 2 == 0
    fill(odd_ref, jnp.logical_not(on_even))
    fill(even_ref, on_even)


def prepare(levels, links, cells):
    half = jax.ShapeDtypeStruct((HALF_F, cells.shape[0], BLK), BF16)
    return pl.pallas_call(
        prepare_kernel,
        name="prepare",
        out_shape=(half, half),
        in_specs=[SMEM, SMEM, VMEM],
        out_specs=(VMEM,) * 2,
        scratch_shapes=[pltpu.SMEM((VBF + 1,), jnp.int32)],
        cost_estimate=pl.CostEstimate(flops=10**6, bytes_accessed=2 * 10**6, transcendentals=0),
        compiler_params=pltpu.CompilerParams(vmem_limit_bytes=8 << 20),
    )(levels, links, cells)


def rows_kernel(level_ref, cells_ref, ahead_ref, back_ref, row_ref):
    _, own, _, _ = place(level_ref)
    cells_y = cells_ref.shape[0]

    def rows(target_ref, row, parity):
        @pl.when(own == 1)
        def _():
            for i in range(HALF_F):
                row_ref[i : i + 1, :] = cells_ref[
                    row : row + 1, (2 * i + parity) * BLK : (2 * i + parity + 1) * BLK
                ]

        @pl.when(own != 1)
        def _():
            for i in range(VBC):
                row_ref[i : i + 1, :] = cells_ref[row : row + 1, i * BLK : (i + 1) * BLK]

        target_ref[...] = row_ref[...].astype(BF16)

    rows(ahead_ref, cells_y - 1, 1)
    rows(back_ref, 0, 0)


def edge_rows(levels, cells):
    row = jax.ShapeDtypeStruct((HALF_F, BLK), BF16)
    return pl.pallas_call(
        rows_kernel,
        name="edge_rows",
        out_shape=(row, row),
        in_specs=[SMEM, VMEM],
        out_specs=(VMEM, VMEM),
        scratch_shapes=[pltpu.VMEM((HALF_F, BLK), F32)],
        cost_estimate=pl.CostEstimate(flops=10**6, bytes_accessed=2 * 10**6, transcendentals=0),
        compiler_params=pltpu.CompilerParams(vmem_limit_bytes=8 << 20),
    )(levels, cells)


def ghost_at(ref, index):
    return ref[index].astype(F32)


def relax_kernel(
    level,
    level_ref,
    rate_ref,
    cells_ref,
    even_ref,
    odd_ref,
    *refs,
):
    side_ref, done_ref, sems = refs[-3:]
    results = 1 if level is None else 2
    row_refs, out_ref = refs[: -3 - results], refs[-3 - results]
    block, own, lower_differs, upper_differs = place(level_ref)
    on_even = block % 2 == 0
    rows_n = cells_ref.shape[0]

    def flush(chunk):
        at = pl.ds(chunk * PART, PART)
        return pltpu.make_async_copy(done_ref.at[:, at], out_ref.at[:, at], sems.at[chunk])

    def run(side, spacing):
        width = side * side
        mid = width // 2
        middle = side // 2
        centre = (side - 1) * 0.5
        lane = lax.broadcasted_iota(jnp.int32, (rows_n, width), 1)
        along_y = spacing * ((lane // side).astype(F32) - centre)
        along_z = spacing * ((lane % side).astype(F32) - centre)

        def span(i):
            start = i * width
            return pl.ds(start if isinstance(i, int) else pl.multiple_of(start, width), width)

        def speed_at(i):
            return spacing * (lax.convert_element_type(i, F32) - centre)

        def gather(i, sums):
            total, first, second = sums
            plane = cells_ref[:, span(i)]
            speed = speed_at(i)
            return total + plane, first + plane * speed, second + plane * (speed * speed)

        zero = jnp.zeros((rows_n, width), F32)
        total, first, second = lax.fori_loop(0, side, gather, (zero, zero, zero), unroll=4)

        def over(value):
            return jnp.broadcast_to(jnp.sum(value, axis=1, keepdims=True), (rows_n, 128))

        weight = spacing * spacing * spacing
        density = weight * over(total)
        scale = weight / density
        mean_x = scale * over(first)
        mean_y = scale * over(total * along_y)
        mean_z = scale * over(total * along_z)
        square = scale * over(second + total * (along_y * along_y + along_z * along_z))
        heat = (square - mean_x * mean_x - mean_y * mean_y - mean_z * mean_z) / 3.0
        row = lax.broadcasted_iota(jnp.int32, (rows_n, 128), 0)
        rate = jnp.zeros((rows_n, 128), F32)
        for r in range(rows_n):
            rate = jnp.where(row == r, rate_ref[0, r], rate)
        spread = 2.0 * math.pi * heat
        peak = rate * density / (spread * jnp.sqrt(spread))
        inverse = -0.5 / heat

        def wide(value):
            return jnp.concatenate([value] * (width // 128), axis=1)

        off_y = along_y - wide(mean_y)
        off_z = along_z - wide(mean_z)
        across = wide(peak) * jnp.exp((off_y * off_y + off_z * off_z) * wide(inverse))
        drift = cfl_ratio * jnp.abs(along_y)
        keep = (1.0 - wide(rate)) - drift
        wide_row = lax.broadcasted_iota(jnp.int32, (rows_n, mid), 0)

        def update(i, upward):
            plane = cells_ref[:, span(i)]
            speed = speed_at(i)
            off_x = speed - mean_x
            along = wide(jnp.exp(off_x * off_x * inverse))
            take_even = on_even == upward
            if side == SF:
                right = side_ref[1, pl.ds(i, 1), :]
                left = side_ref[0, pl.ds(i, 1), :]
                slot = 2 * (i if upward else i - middle)
                ghosts = []
                for half in range(2):
                    a, b = ghost_at(even_ref, slot + half), ghost_at(odd_ref, slot + half)
                    ghosts.append(jnp.where(take_even, a, b))
                ghost = jnp.concatenate(ghosts, axis=1)
            else:
                slot, offset = i // 2, (i % 2) * width
                right = side_ref[1, slot : slot + 1, offset : offset + mid]
                left = side_ref[0, slot : slot + 1, offset + mid : offset + width]
                slot = slot if upward else slot - HALF_C
                a, b = ghost_at(even_ref, slot), ghost_at(odd_ref, slot)
                ghost = jnp.where(take_even, a, b)[:, offset : offset + width]
            if level is not None:
                ghost = jnp.where(upper_differs if upward else lower_differs, 0.0, ghost)
            low, high = plane[:, :mid], plane[:, mid:]
            beyond = jnp.where(wide_row == rows_n - 1, right, pltpu.roll(low, rows_n - 1, 0))
            before = jnp.where(wide_row == 0, left, pltpu.roll(high, 1, 0))
            beside = jnp.concatenate([beyond, before], axis=1)
            push = cfl_ratio * jnp.abs(speed)
            done_ref[:, span(i)] = (
                plane * (keep - push) + push * ghost + drift * beside + along * across
            )

        if side == SF:
            each = side // CHUNKS
            for chunk in range(CHUNKS):
                upward = chunk < CHUNKS // 2

                def step(k, carry, chunk=chunk, upward=upward):
                    update(chunk * each + k, upward)
                    return carry

                lax.fori_loop(0, each, step, 0, unroll=4)
                flush(chunk).start()
        else:
            for i in range(side):
                update(i, i < middle)
            flush(0).start()
            done_ref[:, NVC:] = jnp.zeros((rows_n, NVF - NVC), F32)
            for chunk in range(1, CHUNKS):
                flush(chunk).start()

    if level is None:
        for k, row_ref in enumerate(row_refs):
            side_ref[k] = row_ref[...].astype(F32)
    else:
        side_ref[...] = jnp.zeros_like(side_ref)
        me, group = lax.axis_index("gy"), lax.axis_size("gy")
        for s, ref in zip(near(group), row_refs):
            first = ref.shape[0] - ROWS
            for k, by in ((0, -1), (1, 1)):

                @pl.when(peer(me, s, group) == me + by)
                def _(ref=ref, k=k, first=first):
                    for j in range(ROWS):
                        side_ref[k, 8 * j : 8 * j + 8, :] = ref[first + j].astype(F32)

    if level is None:

        @pl.when(own == 1)
        def _():
            run(SF, spacing_fine)

        @pl.when(own != 1)
        def _():
            run(SC, spacing_coarse)

    elif level == 1:
        run(SF, spacing_fine)
    else:
        run(SC, spacing_coarse)

    if level is not None:
        base_ref = refs[-4]
        split = (NVF if level == 1 else NVC) // 2

        @pl.when(upper_differs)
        def _():
            base_ref[...] = done_ref[:, :split]

        @pl.when(jnp.logical_not(upper_differs))
        def _():
            base_ref[...] = done_ref[:, split : 2 * split]

    for chunk in range(CHUNKS):
        flush(chunk).wait()


def relax(level, levels, rate, cells, even, odd, rows):
    out = jax.ShapeDtypeStruct(cells.shape, F32)
    half = jax.ShapeDtypeStruct((cells.shape[0], (NVF if level == 1 else NVC) // 2), F32)
    return pl.pallas_call(
        functools.partial(relax_kernel, level),
        name="relax",
        out_shape=(out,) if level is None else (out, half),
        in_specs=[SMEM, SMEM, VMEM, VMEM, VMEM] + [VMEM] * len(rows),
        out_specs=(HBM,) if level is None else (HBM, VMEM),
        scratch_shapes=[
            pltpu.VMEM((2, HALF_F, BLK), F32),
            pltpu.VMEM(cells.shape, F32),
            pltpu.SemaphoreType.DMA((CHUNKS,)),
        ],
        cost_estimate=pl.CostEstimate(flops=10**7, bytes_accessed=4 * 10**6, transcendentals=10**5),
        compiler_params=pltpu.CompilerParams(vmem_limit_bytes=16 << 20),
    )(levels, rate, cells, even, odd, *rows)


ROWS = HALF_F // 8


def attach(group, ahead_ref, back_ref, out_refs):
    me = lax.axis_index("gy")
    for s, out_ref in zip(entry(group), out_refs):
        if s not in near(group):
            continue
        first = out_ref.shape[0] - ROWS
        for source_ref, by in ((ahead_ref, 1), (back_ref, -1)):

            @pl.when(peer(me, s, group) == me + by)
            def _(out_ref=out_ref, source_ref=source_ref, first=first):
                for j in range(ROWS):
                    out_ref[first + j] = source_ref[8 * j : 8 * j + 8, :]


def coarse_kernel(group, from_lower, even_ref, odd_ref, ahead_ref, back_ref, *out_refs):
    use_even = (lax.axis_index("gx") % 2 == 0) != from_lower
    for j in range(VBC):
        a, b = even_ref[j].astype(F32), odd_ref[j].astype(F32)
        piece = jnp.where(use_even, a, b).astype(BF16)
        for out_ref in out_refs:
            out_ref[j] = piece
    attach(group, ahead_ref, back_ref, out_refs)


def pieces_kernel(group, level_ref, link_ref, even_ref, odd_ref, ahead_ref, back_ref, *out_refs):
    me = lax.axis_index("gy")
    local = VBF // group
    slots = out_refs[0].shape[0]
    from_lower = faces_lower(level_ref)
    use_even = (lax.axis_index("gx") % 2 == 0) != from_lower
    links = link_ref[...].astype(F32)
    rows = lax.broadcasted_iota(jnp.int32, links.shape, 0)
    columns = lax.broadcasted_iota(jnp.int32, links.shape, 1)
    high = jnp.where(links >= HALF_C, 1.0, 0.0)
    hits = jnp.where(rows == 1, jnp.where(from_lower, high, 1.0 - high), 0.0)

    def start_of(holder):
        return jnp.sum(jnp.where(columns < holder * local, hits, 0.0)).astype(jnp.int32)

    starts = {s: start_of(peer(me, s, group)) for s in order(group)}

    def fill(source_ref):
        for s, out_ref in zip(entry(group), out_refs):
            start = starts[s]
            for j in range(slots):
                out_ref[j] = source_ref[jnp.minimum(start + j, HALF_F - 1)]

    @pl.when(use_even)
    def _():
        fill(even_ref)

    @pl.when(jnp.logical_not(use_even))
    def _():
        fill(odd_ref)

    attach(group, ahead_ref, back_ref, out_refs)


def outgoing_shapes(slots, group, rows_n):
    return tuple(
        jax.ShapeDtypeStruct((slots + (ROWS if s in near(group) else 0), rows_n, BLK), BF16)
        for s in entry(group)
    )


def coarse_pieces(from_lower, even, odd, edges, group):
    return pl.pallas_call(
        functools.partial(coarse_kernel, group, from_lower),
        name="coarse_pieces",
        out_shape=outgoing_shapes(VBC, group, even.shape[1]),
        in_specs=[VMEM] * 4,
        out_specs=(VMEM,) * group,
        cost_estimate=pl.CostEstimate(flops=10**5, bytes_accessed=10**6, transcendentals=0),
        compiler_params=pltpu.CompilerParams(vmem_limit_bytes=8 << 20),
    )(even, odd, *edges)


def pieces(levels, links, even, odd, edges, group, slots):
    return pl.pallas_call(
        functools.partial(pieces_kernel, group),
        name="pieces",
        out_shape=outgoing_shapes(slots, group, even.shape[1]),
        in_specs=[VMEM] * 6,
        out_specs=(VMEM,) * group,
        cost_estimate=pl.CostEstimate(flops=10**5, bytes_accessed=10**6, transcendentals=0),
        compiler_params=pltpu.CompilerParams(vmem_limit_bytes=8 << 20),
    )(levels, links, even, odd, *edges)


def stacked(refs, index):
    return jnp.concatenate([ref[index].astype(F32) for ref in refs], axis=0).astype(BF16)


def to_coarse_kernel(group, level_ref, link_ref, head_ref, tail_ref, *refs):
    in_refs, out_refs, sum_ref = refs[:group], refs[group : 2 * group], refs[-1]
    lower_differs = faces_lower(level_ref)
    links = link_ref[...].astype(F32)
    half = head_ref.shape[0]
    local = half + tail_ref.shape[0]
    cells_y = in_refs[0].shape[1]
    first = lax.axis_index("gy") * local
    offset = jnp.where(lower_differs, HALF_C, 0)

    targets = [pick(links, 1, first + j).astype(jnp.int32) - offset for j in range(local)]
    needed = [(t >= 0) & (t < HALF_C) for t in targets]
    sum_ref[...] = jnp.zeros_like(sum_ref)
    slot = jnp.int32(0)
    for j in range(local):

        @pl.when(needed[j])
        def _(j=j, slot=slot):
            sum_ref[targets[j]] += jnp.dot(
                stacked(in_refs, slot), (head_ref[j] if j < half else tail_ref[j - half]), preferred_element_type=F32
            )

        slot = slot + needed[j].astype(jnp.int32)
    for s, out_ref in enumerate(out_refs):
        out_ref[...] = sum_ref[:, s * cells_y : (s + 1) * cells_y, :].astype(BF16)


def to_fine_kernel(group, from_lower, link_ref, head_ref, tail_ref, *refs):
    in_refs, out_refs = refs[:group], refs[group : 2 * group]
    half = head_ref.shape[0]
    local = half + tail_ref.shape[0]
    cells_y = in_refs[0].shape[1]
    first = lax.axis_index("gy") * local
    active = (first >= HALF_F) == from_lower

    @pl.when(active)
    def _():
        links = link_ref[...].astype(F32)
        picks = [pick(links, 0, first + j).astype(jnp.int32) for j in range(local)]
        for j in range(local):
            product = jnp.dot(
                stacked(in_refs, picks[j]),
                (head_ref[j] if j < half else tail_ref[j - half]),
                preferred_element_type=F32,
            ).astype(BF16)
            for s, out_ref in enumerate(out_refs):
                out_ref[j] = product[s * cells_y : (s + 1) * cells_y, :]


def load_kernel(start, stop, level_ref, link_ref, values_ref, role_ref, held_ref, sems):
    _, own, lower_differs, upper_differs = place(level_ref)
    local = values_ref.shape[1]
    first = lax.axis_index("gy") * local
    fine = own == 1
    source = jnp.where(fine, 0, 1)
    differs = lower_differs | upper_differs

    def needed(j):
        coarse = (link_ref[1, first + j] >= HALF_C) == lower_differs
        here = jnp.where(fine, (first >= HALF_F) == lower_differs, coarse)
        return here & differs

    def copy(j):
        at = j - start
        return pltpu.make_async_copy(values_ref.at[source, j], held_ref.at[at], sems.at[at])

    for j in range(start, stop):
        pl.when(needed(j))(lambda j=j: copy(j).start())

    counts = sizes(local)
    fine_role = len(counts) + jnp.where(lower_differs, 1, 2)
    role_ref[0] = jnp.where(differs & fine, fine_role, 0)

    @pl.when(differs & jnp.logical_not(fine) & (start == 0))
    def _():
        def most(h, worst):
            count = jnp.int32(0)
            for j in range(local):
                hit = (link_ref[1, h * local + j] >= HALF_C) == lower_differs
                count = count + hit.astype(jnp.int32)
            return jnp.maximum(worst, count)

        worst = lax.fori_loop(0, VBF // local, most, jnp.int32(0))
        role = jnp.int32(1)
        for size in counts[:-1]:
            role = role + (worst > size).astype(jnp.int32)
        role_ref[0] = role

    for j in range(start, stop):
        pl.when(needed(j))(lambda j=j: copy(j).wait())


def load(levels, links, values, start, stop):
    return pl.pallas_call(
        functools.partial(load_kernel, start, stop),
        name="load",
        out_shape=(
            jax.ShapeDtypeStruct((1,), jnp.int32),
            jax.ShapeDtypeStruct((stop - start,) + values.shape[2:], BF16),
        ),
        in_specs=[SMEM, SMEM, HBM],
        out_specs=(SMEM, VMEM),
        scratch_shapes=[pltpu.SemaphoreType.DMA((stop - start,))],
        cost_estimate=pl.CostEstimate(
            flops=0, bytes_accessed=(stop - start) * BLK * BLK * 2, transcendentals=0
        ),
        compiler_params=pltpu.CompilerParams(vmem_limit_bytes=44 << 20),
    )(levels, links, values)


def multiply(kernel, tables, values, arrived, slots, scratch):
    group = len(arrived)
    local = sum(part.shape[0] for part in values)
    out = jax.ShapeDtypeStruct((slots,) + arrived[0].shape[1:], BF16)
    return pl.pallas_call(
        kernel,
        name=kernel.func.__name__,
        out_shape=(out,) * group,
        in_specs=[VMEM] * (len(tables) + 2 + group),
        out_specs=(VMEM,) * group,
        scratch_shapes=scratch,
        cost_estimate=pl.CostEstimate(
            flops=2 * local * 32 * BLK * BLK, bytes_accessed=2 * local * BLK * BLK, transcendentals=0
        ),
        compiler_params=pltpu.CompilerParams(vmem_limit_bytes=24 << 20),
    )(*tables, *values, *arrived)


def finish_kernel(role, group, from_lower, *refs):
    if from_lower is None:
        upper_differs, refs = jnp.logical_not(faces_lower(refs[0])), refs[1:]
    else:
        upper_differs = not from_lower
    base_ref, in_refs = refs[0], refs[2:-3]
    out_ref, done_ref, sems = refs[-3:]
    me = lax.axis_index("gy")
    parts = sems.shape[0]
    side, spacing, count = (
        (SC, spacing_coarse, HALF_C) if role == 1 else (SF, spacing_fine, HALF_F)
    )
    whole = count * BLK
    part = whole // parts
    centre = (side - 1) * 0.5

    def flush(index):
        start = index * part + jnp.where(upper_differs, 0, whole)
        at = pl.ds(pl.multiple_of(start, part), part)
        return pltpu.make_async_copy(
            done_ref.at[:, pl.ds(pl.multiple_of(index * part, part), part)],
            out_ref.at[:, at],
            sems.at[index],
        )

    first_plane = jnp.where(upper_differs, 0, side // 2)
    if role == 1:
        width = side * side
        for o in range(HALF_C):
            ghost = in_refs[0][o].astype(F32)
            for ref in in_refs[1:]:
                ghost = ghost + ref[o].astype(F32)
            for k in range(BLK // width):
                plane = lax.convert_element_type(first_plane + o * (BLK // width) + k, F32)
                push = cfl_ratio * spacing * jnp.abs(plane - centre)
                at = slice(o * BLK + k * width, o * BLK + (k + 1) * width)
                done_ref[:, at] = base_ref[:, at] + push * ghost[:, k * width : (k + 1) * width]
        flush(0).start()
        flush(0).wait()
        return

    offset = jnp.where(upper_differs, 0, HALF_F)
    per = HALF_F // parts
    for s, ref in zip(order(group), in_refs):
        local = ref.shape[0]
        first = peer(me, s, group) * local - offset

        @pl.when((first >= 0) & (first < HALF_F))
        def _(ref=ref, first=first, local=local):
            for j in range(local):
                slot = first + j
                if j and j % per == 0:
                    flush(lax.div(slot, per) - 1).start()
                plane = lax.convert_element_type(first_plane + slot // 2, F32)
                push = cfl_ratio * spacing * jnp.abs(plane - centre)
                at = pl.ds(pl.multiple_of(slot * BLK, BLK), BLK)
                done_ref[:, at] = base_ref[:, at] + push * ref[j].astype(F32)
            flush(lax.div(first + local, per) - 1).start()

    for index in range(parts):
        flush(index).wait()


def finish(role, from_lower, levels, base, held, arrived):
    group = len(arrived)
    rows_n = base.shape[0]
    parts = 1 if role == 1 else HALF_F // min(4, VBF // group)
    whole = NVC // 2 if role == 1 else NVF // 2
    scalars = [levels] if from_lower is None else []
    return pl.pallas_call(
        functools.partial(finish_kernel, role, group, from_lower),
        name="finish",
        out_shape=jax.ShapeDtypeStruct(held.shape, F32),
        in_specs=[VMEM] * len(scalars) + [VMEM, HBM] + [VMEM] * group,
        out_specs=HBM,
        scratch_shapes=[pltpu.VMEM((rows_n, whole), F32), pltpu.SemaphoreType.DMA((parts,))],
        input_output_aliases={len(scalars) + 1: 0},
        cost_estimate=pl.CostEstimate(flops=10**6, bytes_accessed=10**6, transcendentals=0),
        compiler_params=pltpu.CompilerParams(vmem_limit_bytes=8 << 20),
    )(*scalars, base, held, *arrived)


def on_device(distribution, relax_rate, block_level, block_link, remap_values):
    blocks, group = lax.axis_size("gx"), lax.axis_size("gy")
    cells_y = distribution.shape[1]
    local = remap_values.shape[1]
    cells = distribution[0]

    def exchange(value, parity):
        pairs = []
        for low in range(parity, blocks - 1, 2):
            for y in range(group):
                here, there = low * group + y, (low + 1) * group + y
                pairs += [(here, there), (there, here)]
        return lax.ppermute(value, BOTH, pairs)

    everyone = range(group)

    def around(steps, outgoing, sources=everyone, targets=everyone, rows=False):
        arrived = []
        for s, value in zip(steps, outgoing):
            pairs = [
                (i, peer(i, s, group))
                for i in everyone
                if (i in sources and peer(i, s, group) in targets)
                or (rows and abs(i - peer(i, s, group)) == 1)
            ]
            arrived.append(lax.ppermute(value, "gy", pairs) if s and pairs else value)
        return arrived

    level_row = block_level[None]
    even, odd = prepare(block_level, block_link, cells)
    odd = exchange(odd, 1)
    even = exchange(even, 0)
    role, head = load(block_level, block_link, remap_values, 0, local // 2)
    edges = edge_rows(block_level, cells)

    def settle(level, rows):
        return relax(level, block_level, relax_rate, cells, even, odd, rows)

    def alone():
        left = lax.ppermute(edges[0], "gy", [(i, i + 1) for i in range(group - 1)])
        right = lax.ppermute(edges[1], "gy", [(i + 1, i) for i in range(group - 1)])
        return settle(None, [left, right])[0]

    def remapped(level, kernel, tables, slots, scratch, arrived):
        tail = load(block_level, block_link, remap_values, local // 2, local)[1]
        values = [head, tail]
        made = multiply(kernel, tables, values, arrived, slots, scratch)
        made = dict(zip(entry(group), made))
        return [made[s] for s in order(group)], settle(level, [p for s, p in zip(entry(group), arrived) if s in near(group)])

    def to_coarse(slots):
        outgoing = pieces(level_row, block_link, even, odd, edges, group, slots)
        sums = [pltpu.VMEM((HALF_C, group * cells_y, BLK), F32)]
        made, (out, base) = remapped(0, functools.partial(to_coarse_kernel, group), [level_row, block_link], HALF_C, sums, around(entry(group), outgoing))
        return finish(1, None, level_row, base, out, around(order(group), made))

    def to_fine(active):
        outgoing = coarse_pieces(active[0] > 0, even, odd, edges, group)
        arrived = around(entry(group), outgoing, targets=active, rows=True)
        made, (out, base) = remapped(1, functools.partial(to_fine_kernel, group, active[0] > 0), [block_link], local, [], arrived)
        return finish(2, active[0] > 0, block_level, base, out, around(order(group), made, sources=active))

    branches = [alone]
    for slots in sizes(local):
        branches.append(functools.partial(to_coarse, slots))
    for active in (range(group // 2, group), range(group // 2)):
        branches.append(functools.partial(to_fine, active))
    updated = lax.switch(role[0], branches)
    return updated[None]


def solution(mesh):
    in_specs = (P("gx", "gy", None), P("gx", "gy"), P(), P(), P(None, "gy", None, None))
    out_specs = P("gx", "gy", None)
    return jax.shard_map(
        on_device, mesh=mesh, in_specs=in_specs, out_specs=out_specs, check_vma=False
    )
```

```python
import functools
import math

import jax
import jax.numpy as jnp
from jax import lax
from jax.experimental import pallas as pl
from jax.experimental.pallas import tpu as pltpu
from jax.sharding import PartitionSpec as P

SC = 16
SF = 32
BLK = 512
NVC = 4096
NVF = 32768
VBC = NVC // BLK
VBF = NVF // BLK
HALF_F = VBF // 2
HALF_C = VBC // 2
CHUNKS = 8
PART = NVF // CHUNKS

cfl_ratio = 0.03
spacing_coarse = 0.5
spacing_fine = 0.4

BOTH = ("gx", "gy")
SMEM = pl.BlockSpec(memory_space=pltpu.SMEM)
VMEM = pl.BlockSpec(memory_space=pltpu.VMEM)
HBM = pl.BlockSpec(memory_space=pltpu.HBM)
F32 = jnp.float32
BF16 = jnp.bfloat16


def place(level_ref):
    block = lax.axis_index("gx")
    own = level_ref[block]
    lower = level_ref[jnp.maximum(block - 1, 0)]
    upper = level_ref[jnp.minimum(block + 1, level_ref.shape[0] - 1)]
    return block, own, lower != own, upper != own


def pick(values, row, column):
    rows = lax.broadcasted_iota(jnp.int32, values.shape, 0)
    columns = lax.broadcasted_iota(jnp.int32, values.shape, 1)
    return jnp.sum(jnp.where((rows == row) & (columns == column), values, 0.0))


def faces_lower(level_ref):
    levels = level_ref[...].astype(F32)
    block = lax.axis_index("gx")
    return pick(levels, 0, block) != pick(levels, 0, jnp.maximum(block - 1, 0))


def peer(me, step, group):
    if group & (group - 1):
        raise ValueError(group)
    return me ^ step


def order(group):
    return sorted(range(group), key=lambda s: (s == 1, s))


def entry(group):
    return order(group)


def near(group):
    return [s for s in entry(group) if s and not s & (s + 1)]


def sizes(local):
    return [max(1, (5 * local) // 8), max(1, (3 * local) // 4), local]


def block_at(ref, index):
    return ref[:, pl.ds(pl.multiple_of(index * BLK, BLK), BLK)]


def prepare_kernel(level_ref, link_ref, cells_ref, even_ref, odd_ref, index_ref):
    block, own, lower_differs, upper_differs = place(level_ref)
    fine = own == 1

    def fill(target_ref, going_up):
        differs = jnp.where(going_up, upper_differs, lower_differs)
        gathers = differs & fine

        @pl.when(gathers)
        def _():
            def look(f, count):
                index_ref[count] = f
                hit = (link_ref[1, f] >= HALF_C) == going_up
                return count + hit.astype(jnp.int32)

            lax.fori_loop(0, VBF, look, jnp.int32(0), unroll=8)

            def copy(j, carry):
                target_ref[j] = block_at(cells_ref, index_ref[j]).astype(BF16)
                return carry

            lax.fori_loop(0, HALF_F, copy, 0, unroll=8)

        @pl.when(fine & jnp.logical_not(differs))
        def _():
            start = jnp.where(going_up, HALF_F, 0)
            for j in range(HALF_F):
                target_ref[j] = block_at(cells_ref, start + j).astype(BF16)

        @pl.when(jnp.logical_not(fine))
        def _():
            start = jnp.where(going_up & jnp.logical_not(differs), HALF_C, 0)
            for j in range(VBC):
                target_ref[j] = block_at(cells_ref, start + j).astype(BF16)

    on_even = block % 2 == 0
    fill(odd_ref, jnp.logical_not(on_even))
    fill(even_ref, on_even)


def prepare(levels, links, cells):
    half = jax.ShapeDtypeStruct((HALF_F, cells.shape[0], BLK), BF16)
    return pl.pallas_call(
        prepare_kernel,
        name="prepare",
        out_shape=(half, half),
        in_specs=[SMEM, SMEM, VMEM],
        out_specs=(VMEM,) * 2,
        scratch_shapes=[pltpu.SMEM((VBF + 1,), jnp.int32)],
        cost_estimate=pl.CostEstimate(flops=10**6, bytes_accessed=2 * 10**6, transcendentals=0),
        compiler_params=pltpu.CompilerParams(vmem_limit_bytes=8 << 20),
    )(levels, links, cells)


def rows_kernel(level_ref, cells_ref, ahead_ref, back_ref, row_ref):
    _, own, _, _ = place(level_ref)
    cells_y = cells_ref.shape[0]

    def rows(target_ref, row, parity):
        @pl.when(own == 1)
        def _():
            for i in range(HALF_F):
                row_ref[i : i + 1, :] = cells_ref[
                    row : row + 1, (2 * i + parity) * BLK : (2 * i + parity + 1) * BLK
                ]

        @pl.when(own != 1)
        def _():
            for i in range(VBC):
                row_ref[i : i + 1, :] = cells_ref[row : row + 1, i * BLK : (i + 1) * BLK]

        target_ref[...] = row_ref[...].astype(BF16)

    rows(ahead_ref, cells_y - 1, 1)
    rows(back_ref, 0, 0)


def edge_rows(levels, cells):
    row = jax.ShapeDtypeStruct((HALF_F, BLK), BF16)
    return pl.pallas_call(
        rows_kernel,
        name="edge_rows",
        out_shape=(row, row),
        in_specs=[SMEM, VMEM],
        out_specs=(VMEM, VMEM),
        scratch_shapes=[pltpu.VMEM((HALF_F, BLK), F32)],
        cost_estimate=pl.CostEstimate(flops=10**6, bytes_accessed=2 * 10**6, transcendentals=0),
        compiler_params=pltpu.CompilerParams(vmem_limit_bytes=8 << 20),
    )(levels, cells)


def ghost_at(ref, index):
    return ref[index].astype(F32)


def relax_kernel(
    level,
    level_ref,
    rate_ref,
    cells_ref,
    even_ref,
    odd_ref,
    *refs,
):
    side_ref, done_ref, sems = refs[-3:]
    results = 1 if level is None else 2
    row_refs, out_ref = refs[: -3 - results], refs[-3 - results]
    block, own, lower_differs, upper_differs = place(level_ref)
    on_even = block % 2 == 0
    rows_n = cells_ref.shape[0]

    def flush(chunk):
        at = pl.ds(chunk * PART, PART)
        return pltpu.make_async_copy(done_ref.at[:, at], out_ref.at[:, at], sems.at[chunk])

    def run(side, spacing):
        width = side * side
        mid = width // 2
        middle = side // 2
        centre = (side - 1) * 0.5
        lane = lax.broadcasted_iota(jnp.int32, (rows_n, width), 1)
        along_y = spacing * ((lane // side).astype(F32) - centre)
        along_z = spacing * ((lane % side).astype(F32) - centre)

        def span(i):
            start = i * width
            return pl.ds(start if isinstance(i, int) else pl.multiple_of(start, width), width)

        def speed_at(i):
            return spacing * (lax.convert_element_type(i, F32) - centre)

        def gather(i, sums):
            total, first, second = sums
            plane = cells_ref[:, span(i)]
            speed = speed_at(i)
            return total + plane, first + plane * speed, second + plane * (speed * speed)

        zero = jnp.zeros((rows_n, width), F32)
        total, first, second = lax.fori_loop(0, side, gather, (zero, zero, zero), unroll=4)

        def over(value):
            return jnp.broadcast_to(jnp.sum(value, axis=1, keepdims=True), (rows_n, 128))

        weight = spacing * spacing * spacing
        density = weight * over(total)
        scale = weight / density
        mean_x = scale * over(first)
        mean_y = scale * over(total * along_y)
        mean_z = scale * over(total * along_z)
        square = scale * over(second + total * (along_y * along_y + along_z * along_z))
        heat = (square - mean_x * mean_x - mean_y * mean_y - mean_z * mean_z) / 3.0
        row = lax.broadcasted_iota(jnp.int32, (rows_n, 128), 0)
        rate = jnp.zeros((rows_n, 128), F32)
        for r in range(rows_n):
            rate = jnp.where(row == r, rate_ref[0, r], rate)
        spread = 2.0 * math.pi * heat
        peak = rate * density / (spread * jnp.sqrt(spread))
        inverse = -0.5 / heat

        def wide(value):
            return jnp.concatenate([value] * (width // 128), axis=1)

        off_y = along_y - wide(mean_y)
        off_z = along_z - wide(mean_z)
        across = wide(peak) * jnp.exp((off_y * off_y + off_z * off_z) * wide(inverse))
        drift = cfl_ratio * jnp.abs(along_y)
        keep = (1.0 - wide(rate)) - drift
        wide_row = lax.broadcasted_iota(jnp.int32, (rows_n, mid), 0)

        def update(i, upward):
            plane = cells_ref[:, span(i)]
            speed = speed_at(i)
            off_x = speed - mean_x
            along = wide(jnp.exp(off_x * off_x * inverse))
            take_even = on_even == upward
            if side == SF:
                right = side_ref[1, pl.ds(i, 1), :]
                left = side_ref[0, pl.ds(i, 1), :]
                slot = 2 * (i if upward else i - middle)
                ghosts = []
                for half in range(2):
                    a, b = ghost_at(even_ref, slot + half), ghost_at(odd_ref, slot + half)
                    ghosts.append(jnp.where(take_even, a, b))
                ghost = jnp.concatenate(ghosts, axis=1)
            else:
                slot, offset = i // 2, (i % 2) * width
                right = side_ref[1, slot : slot + 1, offset : offset + mid]
                left = side_ref[0, slot : slot + 1, offset + mid : offset + width]
                slot = slot if upward else slot - HALF_C
                a, b = ghost_at(even_ref, slot), ghost_at(odd_ref, slot)
                ghost = jnp.where(take_even, a, b)[:, offset : offset + width]
            if level is not None:
                ghost = jnp.where(upper_differs if upward else lower_differs, 0.0, ghost)
            low, high = plane[:, :mid], plane[:, mid:]
            beyond = jnp.where(wide_row == rows_n - 1, right, pltpu.roll(low, rows_n - 1, 0))
            before = jnp.where(wide_row == 0, left, pltpu.roll(high, 1, 0))
            beside = jnp.concatenate([beyond, before], axis=1)
            push = cfl_ratio * jnp.abs(speed)
            done_ref[:, span(i)] = (
                plane * (keep - push) + push * ghost + drift * beside + along * across
            )

        if side == SF:
            each = side // CHUNKS
            for chunk in range(CHUNKS):
                upward = chunk < CHUNKS // 2

                def step(k, carry, chunk=chunk, upward=upward):
                    update(chunk * each + k, upward)
                    return carry

                lax.fori_loop(0, each, step, 0, unroll=4)
                flush(chunk).start()
        else:
            for i in range(side):
                update(i, i < middle)
            flush(0).start()
            done_ref[:, NVC:] = jnp.zeros((rows_n, NVF - NVC), F32)
            for chunk in range(1, CHUNKS):
                flush(chunk).start()

    if level is None:
        for k, row_ref in enumerate(row_refs):
            side_ref[k] = row_ref[...].astype(F32)
    else:
        side_ref[...] = jnp.zeros_like(side_ref)
        me, group = lax.axis_index("gy"), lax.axis_size("gy")
        steps = order(group)[1:] if len(row_refs) == group - 1 else near(group)
        for s, ref in zip(steps, row_refs):
            if s not in near(group):
                continue
            first = ref.shape[0] - ROWS
            for k, by in ((0, -1), (1, 1)):

                @pl.when(peer(me, s, group) == me + by)
                def _(ref=ref, k=k, first=first):
                    for j in range(ROWS):
                        side_ref[k, 8 * j : 8 * j + 8, :] = ref[first + j].astype(F32)

    if level is None:

        @pl.when(own == 1)
        def _():
            run(SF, spacing_fine)

        @pl.when(own != 1)
        def _():
            run(SC, spacing_coarse)

    elif level == 1:
        run(SF, spacing_fine)
    else:
        run(SC, spacing_coarse)

    if level is not None:
        base_ref = refs[-4]
        split = (NVF if level == 1 else NVC) // 2

        @pl.when(upper_differs)
        def _():
            base_ref[...] = done_ref[:, :split]

        @pl.when(jnp.logical_not(upper_differs))
        def _():
            base_ref[...] = done_ref[:, split : 2 * split]

    for chunk in range(CHUNKS):
        flush(chunk).wait()


def relax(level, levels, rate, cells, even, odd, rows):
    out = jax.ShapeDtypeStruct(cells.shape, F32)
    half = jax.ShapeDtypeStruct((cells.shape[0], (NVF if level == 1 else NVC) // 2), F32)
    return pl.pallas_call(
        functools.partial(relax_kernel, level),
        name="relax",
        out_shape=(out,) if level is None else (out, half),
        in_specs=[SMEM, SMEM, VMEM, VMEM, VMEM] + [VMEM] * len(rows),
        out_specs=(HBM,) if level is None else (HBM, VMEM),
        scratch_shapes=[
            pltpu.VMEM((2, HALF_F, BLK), F32),
            pltpu.VMEM(cells.shape, F32),
            pltpu.SemaphoreType.DMA((CHUNKS,)),
        ],
        cost_estimate=pl.CostEstimate(flops=10**7, bytes_accessed=4 * 10**6, transcendentals=10**5),
        compiler_params=pltpu.CompilerParams(vmem_limit_bytes=16 << 20),
    )(levels, rate, cells, even, odd, *rows)


ROWS = HALF_F // 8


def attach(steps, group, ahead_ref, back_ref, out_refs):
    me = lax.axis_index("gy")
    for s, out_ref in zip(steps, out_refs):
        if s not in near(group):
            continue
        first = out_ref.shape[0] - ROWS
        for source_ref, by in ((ahead_ref, 1), (back_ref, -1)):

            @pl.when(peer(me, s, group) == me + by)
            def _(out_ref=out_ref, source_ref=source_ref, first=first):
                for j in range(ROWS):
                    out_ref[first + j] = source_ref[8 * j : 8 * j + 8, :]


def coarse_kernel(group, from_lower, even_ref, odd_ref, ahead_ref, back_ref, *out_refs):
    use_even = (lax.axis_index("gx") % 2 == 0) != from_lower
    for j in range(VBC):
        a, b = even_ref[j].astype(F32), odd_ref[j].astype(F32)
        piece = jnp.where(use_even, a, b).astype(BF16)
        for out_ref in out_refs:
            out_ref[j] = piece
    attach(order(group), group, ahead_ref, back_ref, out_refs)


def pieces_kernel(group, level_ref, link_ref, even_ref, odd_ref, ahead_ref, back_ref, *out_refs):
    me = lax.axis_index("gy")
    local = VBF // group
    slots = out_refs[0].shape[0]
    from_lower = faces_lower(level_ref)
    use_even = (lax.axis_index("gx") % 2 == 0) != from_lower
    links = link_ref[...].astype(F32)
    rows = lax.broadcasted_iota(jnp.int32, links.shape, 0)
    columns = lax.broadcasted_iota(jnp.int32, links.shape, 1)
    high = jnp.where(links >= HALF_C, 1.0, 0.0)
    hits = jnp.where(rows == 1, jnp.where(from_lower, high, 1.0 - high), 0.0)

    def start_of(holder):
        return jnp.sum(jnp.where(columns < holder * local, hits, 0.0)).astype(jnp.int32)

    starts = {s: start_of(peer(me, s, group)) for s in order(group)}

    def fill(source_ref):
        for s, out_ref in zip(entry(group), out_refs):
            start = starts[s]
            for j in range(slots):
                out_ref[j] = source_ref[jnp.minimum(start + j, HALF_F - 1)]

    @pl.when(use_even)
    def _():
        fill(even_ref)

    @pl.when(jnp.logical_not(use_even))
    def _():
        fill(odd_ref)

    attach(entry(group), group, ahead_ref, back_ref, out_refs)


def outgoing_shapes(steps, pad, slots, group, rows_n):
    return tuple(
        jax.ShapeDtypeStruct((slots + (ROWS if s in near(group) or (s and pad) else 0), rows_n, BLK), BF16)
        for s in steps
    )


def coarse_pieces(pad, from_lower, even, odd, edges, group):
    return pl.pallas_call(
        functools.partial(coarse_kernel, group, from_lower),
        name="coarse_pieces",
        out_shape=outgoing_shapes(order(group), pad, VBC, group, even.shape[1]),
        in_specs=[VMEM] * 4,
        out_specs=(VMEM,) * group,
        cost_estimate=pl.CostEstimate(flops=10**5, bytes_accessed=10**6, transcendentals=0),
        compiler_params=pltpu.CompilerParams(vmem_limit_bytes=8 << 20),
    )(even, odd, *edges)


def pieces(levels, links, even, odd, edges, group, slots):
    return pl.pallas_call(
        functools.partial(pieces_kernel, group),
        name="pieces",
        out_shape=outgoing_shapes(entry(group), False, slots, group, even.shape[1]),
        in_specs=[VMEM] * 6,
        out_specs=(VMEM,) * group,
        cost_estimate=pl.CostEstimate(flops=10**5, bytes_accessed=10**6, transcendentals=0),
        compiler_params=pltpu.CompilerParams(vmem_limit_bytes=8 << 20),
    )(levels, links, even, odd, *edges)


def stacked(refs, index):
    return jnp.concatenate([ref[index].astype(F32) for ref in refs], axis=0).astype(BF16)


def to_coarse_kernel(group, level_ref, link_ref, head_ref, tail_ref, *refs):
    in_refs, out_refs, sum_ref = refs[:group], refs[group : 2 * group], refs[-1]
    lower_differs = faces_lower(level_ref)
    links = link_ref[...].astype(F32)
    half = head_ref.shape[0]
    local = half + tail_ref.shape[0]
    cells_y = in_refs[0].shape[1]
    first = lax.axis_index("gy") * local
    offset = jnp.where(lower_differs, HALF_C, 0)

    targets = [pick(links, 1, first + j).astype(jnp.int32) - offset for j in range(local)]
    needed = [(t >= 0) & (t < HALF_C) for t in targets]
    sum_ref[...] = jnp.zeros_like(sum_ref)
    slot = jnp.int32(0)
    for j in range(local):

        @pl.when(needed[j])
        def _(j=j, slot=slot):
            sum_ref[targets[j]] += jnp.dot(
                stacked(in_refs, slot), (head_ref[j] if j < half else tail_ref[j - half]), preferred_element_type=F32
            )

        slot = slot + needed[j].astype(jnp.int32)
    for s, out_ref in enumerate(out_refs):
        out_ref[...] = sum_ref[:, s * cells_y : (s + 1) * cells_y, :].astype(BF16)


def to_fine_kernel(group, from_lower, link_ref, head_ref, tail_ref, *refs):
    in_refs, out_refs = refs[:group], refs[group : 2 * group]
    half = head_ref.shape[0]
    local = half + tail_ref.shape[0]
    cells_y = in_refs[0].shape[1]
    first = lax.axis_index("gy") * local
    active = (first >= HALF_F) == from_lower

    @pl.when(active)
    def _():
        links = link_ref[...].astype(F32)
        picks = [pick(links, 0, first + j).astype(jnp.int32) for j in range(local)]
        for j in range(local):
            product = jnp.dot(
                stacked(in_refs, picks[j]),
                (head_ref[j] if j < half else tail_ref[j - half]),
                preferred_element_type=F32,
            ).astype(BF16)
            for s, out_ref in enumerate(out_refs):
                out_ref[j] = product[s * cells_y : (s + 1) * cells_y, :]


def load_kernel(start, stop, level_ref, link_ref, values_ref, role_ref, held_ref, sems):
    _, own, lower_differs, upper_differs = place(level_ref)
    local = values_ref.shape[1]
    first = lax.axis_index("gy") * local
    fine = own == 1
    source = jnp.where(fine, 0, 1)
    differs = lower_differs | upper_differs

    def needed(j):
        coarse = (link_ref[1, first + j] >= HALF_C) == lower_differs
        here = jnp.where(fine, (first >= HALF_F) == lower_differs, coarse)
        return here & differs

    def copy(j):
        at = j - start
        return pltpu.make_async_copy(values_ref.at[source, j], held_ref.at[at], sems.at[at])

    for j in range(start, stop):
        pl.when(needed(j))(lambda j=j: copy(j).start())

    counts = sizes(local)
    inside = lax.axis_index("gx") % 2 == 0
    fine_role = len(counts) + jnp.where(lower_differs, 1, jnp.where(inside, 3, 2))
    role_ref[0] = jnp.where(differs & fine, fine_role, 0)

    @pl.when(differs & jnp.logical_not(fine) & (start == 0))
    def _():
        def most(h, worst):
            count = jnp.int32(0)
            for j in range(local):
                hit = (link_ref[1, h * local + j] >= HALF_C) == lower_differs
                count = count + hit.astype(jnp.int32)
            return jnp.maximum(worst, count)

        worst = lax.fori_loop(0, VBF // local, most, jnp.int32(0))
        role = jnp.int32(1)
        for size in counts[:-1]:
            role = role + (worst > size).astype(jnp.int32)
        role_ref[0] = role

    for j in range(start, stop):
        pl.when(needed(j))(lambda j=j: copy(j).wait())


def load(levels, links, values, start, stop):
    return pl.pallas_call(
        functools.partial(load_kernel, start, stop),
        name="load",
        out_shape=(
            jax.ShapeDtypeStruct((1,), jnp.int32),
            jax.ShapeDtypeStruct((stop - start,) + values.shape[2:], BF16),
        ),
        in_specs=[SMEM, SMEM, HBM],
        out_specs=(SMEM, VMEM),
        scratch_shapes=[pltpu.SemaphoreType.DMA((stop - start,))],
        cost_estimate=pl.CostEstimate(
            flops=0, bytes_accessed=(stop - start) * BLK * BLK * 2, transcendentals=0
        ),
        compiler_params=pltpu.CompilerParams(vmem_limit_bytes=44 << 20),
    )(levels, links, values)


def multiply(kernel, tables, values, arrived, slots, scratch):
    group = len(arrived)
    local = sum(part.shape[0] for part in values)
    out = jax.ShapeDtypeStruct((slots,) + arrived[0].shape[1:], BF16)
    return pl.pallas_call(
        kernel,
        name=kernel.func.__name__,
        out_shape=(out,) * group,
        in_specs=[VMEM] * (len(tables) + 2 + group),
        out_specs=(VMEM,) * group,
        scratch_shapes=scratch,
        cost_estimate=pl.CostEstimate(
            flops=2 * local * 32 * BLK * BLK, bytes_accessed=2 * local * BLK * BLK, transcendentals=0
        ),
        compiler_params=pltpu.CompilerParams(vmem_limit_bytes=24 << 20),
    )(*tables, *values, *arrived)


def finish_kernel(role, group, from_lower, *refs):
    if from_lower is None:
        upper_differs, refs = jnp.logical_not(faces_lower(refs[0])), refs[1:]
    else:
        upper_differs = not from_lower
    base_ref, in_refs = refs[0], refs[2:-3]
    out_ref, done_ref, sems = refs[-3:]
    me = lax.axis_index("gy")
    parts = sems.shape[0]
    side, spacing, count = (
        (SC, spacing_coarse, HALF_C) if role == 1 else (SF, spacing_fine, HALF_F)
    )
    whole = count * BLK
    part = whole // parts
    centre = (side - 1) * 0.5

    def flush(index):
        start = index * part + jnp.where(upper_differs, 0, whole)
        at = pl.ds(pl.multiple_of(start, part), part)
        return pltpu.make_async_copy(
            done_ref.at[:, pl.ds(pl.multiple_of(index * part, part), part)],
            out_ref.at[:, at],
            sems.at[index],
        )

    first_plane = jnp.where(upper_differs, 0, side // 2)
    if role == 1:
        width = side * side
        for o in range(HALF_C):
            ghost = in_refs[0][o].astype(F32)
            for ref in in_refs[1:]:
                ghost = ghost + ref[o].astype(F32)
            for k in range(BLK // width):
                plane = lax.convert_element_type(first_plane + o * (BLK // width) + k, F32)
                push = cfl_ratio * spacing * jnp.abs(plane - centre)
                at = slice(o * BLK + k * width, o * BLK + (k + 1) * width)
                done_ref[:, at] = base_ref[:, at] + push * ghost[:, k * width : (k + 1) * width]
        flush(0).start()
        flush(0).wait()
        return

    offset = jnp.where(upper_differs, 0, HALF_F)
    per = HALF_F // parts
    for s, ref in zip(order(group), in_refs):
        local = ref.shape[0]
        first = peer(me, s, group) * local - offset

        @pl.when((first >= 0) & (first < HALF_F))
        def _(ref=ref, first=first, local=local):
            for j in range(local):
                slot = first + j
                if j and j % per == 0:
                    flush(lax.div(slot, per) - 1).start()
                plane = lax.convert_element_type(first_plane + slot // 2, F32)
                push = cfl_ratio * spacing * jnp.abs(plane - centre)
                at = pl.ds(pl.multiple_of(slot * BLK, BLK), BLK)
                done_ref[:, at] = base_ref[:, at] + push * ref[j].astype(F32)
            flush(lax.div(first + local, per) - 1).start()

    for index in range(parts):
        flush(index).wait()


def finish(role, from_lower, levels, base, held, arrived):
    group = len(arrived)
    rows_n = base.shape[0]
    parts = 1 if role == 1 else HALF_F // min(4, VBF // group)
    whole = NVC // 2 if role == 1 else NVF // 2
    scalars = [levels] if from_lower is None else []
    return pl.pallas_call(
        functools.partial(finish_kernel, role, group, from_lower),
        name="finish",
        out_shape=jax.ShapeDtypeStruct(held.shape, F32),
        in_specs=[VMEM] * len(scalars) + [VMEM, HBM] + [VMEM] * group,
        out_specs=HBM,
        scratch_shapes=[pltpu.VMEM((rows_n, whole), F32), pltpu.SemaphoreType.DMA((parts,))],
        input_output_aliases={len(scalars) + 1: 0},
        cost_estimate=pl.CostEstimate(flops=10**6, bytes_accessed=10**6, transcendentals=0),
        compiler_params=pltpu.CompilerParams(vmem_limit_bytes=8 << 20),
    )(*scalars, base, held, *arrived)


def on_device(distribution, relax_rate, block_level, block_link, remap_values):
    blocks, group = lax.axis_size("gx"), lax.axis_size("gy")
    cells_y = distribution.shape[1]
    local = remap_values.shape[1]
    cells = distribution[0]

    def exchange(value, parity):
        pairs = []
        for low in range(parity, blocks - 1, 2):
            for y in range(group):
                here, there = low * group + y, (low + 1) * group + y
                pairs += [(here, there), (there, here)]
        return lax.ppermute(value, BOTH, pairs)

    everyone = range(group)

    def around(steps, outgoing, sources=everyone, targets=everyone, rows=False):
        arrived = []
        for s, value in zip(steps, outgoing):
            pairs = [
                (i, peer(i, s, group))
                for i in everyone
                if (i in sources and peer(i, s, group) in targets)
                or (rows and abs(i - peer(i, s, group)) == 1)
            ]
            arrived.append(lax.ppermute(value, "gy", pairs) if s and pairs else value)
        return arrived

    level_row = block_level[None]
    even, odd = prepare(block_level, block_link, cells)
    odd = exchange(odd, 1)
    even = exchange(even, 0)
    role, head = load(block_level, block_link, remap_values, 0, local // 2)
    edges = edge_rows(block_level, cells)

    def settle(level, rows):
        return relax(level, block_level, relax_rate, cells, even, odd, rows)

    def alone():
        left = lax.ppermute(edges[0], "gy", [(i, i + 1) for i in range(group - 1)])
        right = lax.ppermute(edges[1], "gy", [(i + 1, i) for i in range(group - 1)])
        return settle(None, [left, right])[0]

    def remapped(pad, steps, level, kernel, tables, slots, scratch, arrived):
        tail = load(block_level, block_link, remap_values, local // 2, local)[1]
        values = [head, tail]
        made = multiply(kernel, tables, values, arrived, slots, scratch)
        made = dict(zip(steps, made))
        return [made[s] for s in order(group)], settle(level, arrived[1:] if pad else [p for s, p in zip(steps, arrived) if s in near(group)])

    def to_coarse(slots):
        outgoing = pieces(level_row, block_link, even, odd, edges, group, slots)
        sums = [pltpu.VMEM((HALF_C, group * cells_y, BLK), F32)]
        made, (out, base) = remapped(False, entry(group), 0, functools.partial(to_coarse_kernel, group), [level_row, block_link], HALF_C, sums, around(entry(group), outgoing))
        return finish(1, None, level_row, base, out, around(order(group), made))

    def to_fine(pad, active):
        outgoing = coarse_pieces(pad, active[0] > 0, even, odd, edges, group)
        arrived = around(order(group), outgoing, targets=active, rows=True)
        made, (out, base) = remapped(pad, order(group), 1, functools.partial(to_fine_kernel, group, active[0] > 0), [block_link], local, [], arrived)
        return finish(2, active[0] > 0, block_level, base, out, around(order(group), made, sources=active))

    branches = [alone]
    for slots in sizes(local):
        branches.append(functools.partial(to_coarse, slots))
    low, high = range(group // 2), range(group // 2, group)
    for pad, active in ((False, high), (False, low), (True, low)):
        branches.append(functools.partial(to_fine, pad, active))
    updated = lax.switch(role[0], branches)
    return updated[None]


def solution(mesh):
    in_specs = (P("gx", "gy", None), P("gx", "gy"), P(), P(), P(None, "gy", None, None))
    out_specs = P("gx", "gy", None)
    return jax.shard_map(
        on_device, mesh=mesh, in_specs=in_specs, out_specs=out_specs, check_vma=False
    )
```
